32 devices in a mesh: ep: 8 (over z, x), ctx: 4 (over y, core).
Axes of the slice: x: 2, y: 2, z: 4, core: 2. Of those that a mesh axis runs over, the one named last changes fastest.
Arguments:
- tokens: bfloat16 [8, 1536, 1024], P('ep', 'ctx'), may hold values from -6 to 6
- lengths: int32 [8], P('ep'), may hold values from 192 to 1536, as said below
- routes: int32 [8, 1536, 8], P('ep', 'ctx'), may hold values from 0 to 15, all different within a row; in each aligned block of 384 rows (0 to 383, 384 to 767, ..., all dimensions but the last counted through in order) at most 288 rows name the same one
- cotangent: bfloat16 [8, 1536, 1024], P('ep', 'ctx'), may hold values from -6 to 6
- attn_norm: float32 [1024], replicated, may hold values from 0.5 to 1.5
- w_query: bfloat16 [1024, 1024], replicated, may hold values from -0.21875 to 0.21875
- w_key: bfloat16 [1024, 512], replicated, may hold values from -0.21875 to 0.21875
- w_value: bfloat16 [1024, 512], replicated, may hold values from -0.1875 to 0.1875
- w_out: bfloat16 [1024, 1024], replicated, may hold values from -1.25 to 1.25
- ffn_norm: float32 [1024], replicated, may hold values from 0.5 to 1.5
- w_router: bfloat16 [1024, 16], replicated, may hold values from -0.09375 to 0.09375
- expert_gate_weight: bfloat16 [16, 1024, 512], P('ep'), may hold values from -0.1875 to 0.1875
- expert_up_weight: bfloat16 [16, 1024, 512], P('ep'), may hold values from -0.1875 to 0.1875
- expert_down_weight: bfloat16 [16, 512, 1024], P('ep'), may hold values from -1.5 to 1.5
Outputs:
- out: bfloat16 [8, 1536, 1024], P('ep', 'ctx')
- grad_tokens: bfloat16 [8, 1536, 1024], P('ep', 'ctx')
- grad_attn_norm: float32 [1024], replicated
- grad_w_query: float32 [1024, 1024], replicated
- grad_w_key: float32 [1024, 512], replicated
- grad_w_value: float32 [1024, 512], replicated
- grad_w_out: float32 [1024, 1024], replicated
- grad_ffn_norm: float32 [1024], replicated
- grad_w_router: float32 [1024, 16], replicated
- grad_w_gate: float32 [16, 1024, 512], P('ep')
- grad_w_up: float32 [16, 1024, 512], P('ep')
- grad_w_down: float32 [16, 512, 1024], P('ep')
The draws below stay inside these ranges and needn't reach their ends.
Inputs may be any that keep to these rules, and one draw needn't show every extreme that they name: `routes`: within the 384 rows of one device (aligned blocks of the flattened positions), no expert is named by more than 288 rows, a bound that some block reaches; each row names 8 different experts. A sequence's valid positions are its first lengths ones; some sequence has all 1536.
All inputs are finite; a program needn't handle non-finite values.
Results may differ from the reference program's by a relative error of at most 0.024.
Values may be sent and summed in bfloat16 or wider, within the bound.
No kernel may reach another device: no remote copies, remote signals or barrier semaphores. Data moves between devices by JAX's collectives and lax.ppermute only.
A program may use at most 256 MiB of HBM per device.

```python
import math
import jax
import jax.numpy as jnp
import numpy as np
from jax import lax

D = 1024
HEADS = 16
KV_HEADS = 8
HEAD_DIM = 64
EXPERT_FF = 512
TOPK = 8
CH = 384
EXPERTS = 16
SEQLEN = 1536
NSEQ = 8
CAP = 288


def draw_lengths(key, part):
    first_key, second_key = jax.random.split(key)
    sampled = jax.random.randint(first_key, (NSEQ,), SEQLEN // 8, SEQLEN + 1, dtype=jnp.int32)
    full_at = jax.random.randint(second_key, (), 0, NSEQ, dtype=jnp.int32)
    return jnp.where(jnp.arange(NSEQ, dtype=jnp.int32) == full_at, jnp.int32(SEQLEN), sampled)


def levels(own_key, extent, cuts, low, high):
    def one(position, parts):
        steps = jax.random.uniform(jax.random.fold_in(jax.random.fold_in(own_key, 6), position), (parts,), jnp.float32, low / len(cuts), high / len(cuts))
        return jnp.repeat(jnp.exp(steps), extent[position] // parts).reshape((-1,) + (1,) * (len(extent) - position - 1))

    loudness = one(*cuts[0])
    for cut in cuts[1:]:
        loudness = loudness * one(*cut)
    return loudness


def routed_block(rng, own, number, rows, number_of, top, limit, lean):
    order = jax.random.permutation(rng, number_of)
    crowded, usual = portions_of(number_of, rows * top, limit, lean, True), portions_of(number_of, rows * top, limit, lean, False)
    places = jnp.arange(number_of)

    def named(tallies, turn):
        used = int((tallies > 0).sum())
        fixed = max(1, used // 4)
        shifted = fixed + (places - fixed + turn * (used - fixed)) % max(1, number_of - fixed)
        return jnp.zeros((number_of,), jnp.int32).at[order[jnp.where(places < fixed, places, shifted)]].set(jnp.asarray(tallies, jnp.int32))

    tallies = jnp.where(number % 4 == 0, named(crowded, number // 4), named(usual, number - number // 4 - 1))
    mixed = jax.random.permutation(jax.random.fold_in(own, 3), number_of)
    source_of, taker = mixed[0:number_of // 2 * 2:2], mixed[1:number_of // 2 * 2:2]
    room = jnp.minimum(tallies[source_of] - 1, limit - tallies[taker]) // 2
    room = jnp.where((source_of == order[0]) | (taker == order[0]) | (tallies[taker] == 0), 0, jnp.maximum(room, 0))
    shifted = jax.random.randint(jax.random.fold_in(own, 4), (number_of // 2,), 0, 1 << 20) % (room + 1)
    tallies = tallies.at[source_of].add(-shifted).at[taker].add(shifted)
    members = jnp.searchsorted(jnp.cumsum(tallies), jnp.arange(rows * top), side="right").astype(jnp.int32)
    grid = members.reshape(top, rows).T
    grid = grid[jax.random.permutation(jax.random.fold_in(own, 1), rows)]
    turn = jax.random.randint(jax.random.fold_in(own, 2), (rows, 1), 0, top)
    return jnp.take_along_axis(grid, (jnp.arange(top)[None, :] + turn) % top, axis=1)


def portions_of(amount, total, bound, skew, full):
    loads = [(1 << 20) // math.isqrt(grade ** skew) + 1 for grade in range(1, amount + 1)]
    largest = bound if full else min(bound, max(-(-total // amount), total * loads[0] // sum(loads)))
    least = 1 if total - largest >= amount - 1 else 0
    counts, surplus = [largest] + [least] * (amount - 1), total - largest - least * (amount - 1)
    while surplus > 0:
        candidates = [i for i in range(1, amount) if counts[i] < largest] or [i for i in range(1, amount) if counts[i] < bound]
        pool, remaining = sum([loads[i] for i in candidates]), surplus
        for i in candidates:
            more = min(bound - counts[i], max(1, remaining * loads[i] // pool), surplus)
            counts[i] = counts[i] + more
            surplus = surplus - more
    return np.array(counts)


def centred(stream_key, shape, scale, limit, pieces=(), held_as=jnp.bfloat16):
    values = jax.random.normal(stream_key, shape, jnp.float32) * scale
    if len(pieces) > 0:
        values = levels(stream_key, shape, pieces, -0.22, 0.18) * values
    return jnp.clip(values, min=-limit, max=limit).astype(held_as)


def setup_inputs(seed: int = 0) -> dict:
    key_list = jax.random.split(jax.random.key(seed), 15)
    tokens = centred(key_list[0], (NSEQ, SEQLEN, D), 1.0, 6.0, ((0, 8), (1, 4)))
    lengths = draw_lengths(jax.random.fold_in(key_list[14], 71), 0)
    routes_keys = jax.random.split(jax.random.fold_in(key_list[2], 1), NSEQ * SEQLEN // CH)
    routes_turns = jax.random.permutation(jax.random.fold_in(key_list[2], 3), NSEQ * SEQLEN // CH)
    routes = jax.vmap(lambda own, number: routed_block(jax.random.fold_in(key_list[2], 2), own, number, CH, EXPERTS, TOPK, CAP, 1))(routes_keys, routes_turns).reshape((NSEQ, SEQLEN, TOPK))
    cotangent = centred(key_list[3], (NSEQ, SEQLEN, D), 1.0, 6.0, ((0, 8), (1, 4)))
    attn_norm = jnp.clip(1.0 + 0.1 * jax.random.normal(key_list[4], (D,), jnp.float32), 0.5, 1.5)
    w_query = centred(key_list[5], (D, HEADS * HEAD_DIM), (2 * D // 3) ** -0.5, 0.21875)
    w_key = centred(key_list[6], (D, KV_HEADS * HEAD_DIM), (2 * D // 3) ** -0.5, 0.21875)
    w_value = centred(key_list[7], (D, KV_HEADS * HEAD_DIM), D ** -0.5, 0.1875)
    w_out = centred(key_list[8], (HEADS * HEAD_DIM, D), (HEADS * HEAD_DIM // 48) ** -0.5, 1.25)
    ffn_norm = jnp.clip(1.0 + 0.1 * jax.random.normal(key_list[9], (D,), jnp.float32), 0.5, 1.5)
    w_router = centred(key_list[10], (D, EXPERTS), (4 * D) ** -0.5, 0.09375)
    expert_gate_weight = centred(key_list[11], (EXPERTS, D, EXPERT_FF), D ** -0.5, 0.1875, ((0, 8),))
    expert_up_weight = centred(key_list[12], (EXPERTS, D, EXPERT_FF), D ** -0.5, 0.1875, ((0, 8),))
    expert_down_weight = centred(key_list[13], (EXPERTS, EXPERT_FF, D), (EXPERT_FF // 32) ** -0.5, 1.5, ((0, 8),))
    return {"tokens": tokens, "lengths": lengths, "routes": routes, "cotangent": cotangent, "attn_norm": attn_norm, "w_query": w_query, "w_key": w_key, "w_value": w_value, "w_out": w_out, "ffn_norm": ffn_norm, "w_router": w_router, "expert_gate_weight": expert_gate_weight, "expert_up_weight": expert_up_weight, "expert_down_weight": expert_down_weight}


EPS = 1e-06
THETA = 10000.0
NEG = -1e+30
HIGH = lax.Precision.HIGHEST

@jax.custom_vjp
def low(v):
    return lax.optimization_barrier(v.astype(jnp.bfloat16)).astype(jnp.float32)

@jax.custom_vjp
def low_back(v):
    return v

def low_keep(v):
    return (low(v), None)

def low_pass(kept, grad):
    return (grad,)

def back_keep(v):
    return (v, None)

def back_low(kept, grad):
    return (low(grad),)
low.defvjp(low_keep, low_pass)
low_back.defvjp(back_keep, back_low)

def matmul(left, right):
    return jnp.dot(left, right, preferred_element_type=jnp.float32, precision=HIGH)

def rope_tables(positions, head_dim):
    half_dim = head_dim // 2
    inv_freq = THETA ** (-jnp.arange(half_dim, dtype=jnp.float32) / half_dim)
    angles = positions.astype(jnp.float32)[:, None] * inv_freq[None, :]
    return (jnp.cos(angles)[:, None, :], jnp.sin(angles)[:, None, :])

def rotate(values, cos_tab, sin_tab):
    half_dim = values.shape[-1] // 2
    front_half = values[..., :half_dim]
    back_half = values[..., half_dim:]
    return jnp.concatenate([front_half * cos_tab - back_half * sin_tab, back_half * cos_tab + front_half * sin_tab], -1)

def forward(inputs, attn_norm, w_query, w_key, w_value, w_out, ffn_norm, w_router, expert_gate_weight, expert_up_weight, expert_down_weight, lengths, routes):
    group_size = HEADS // KV_HEADS
    positions = jnp.arange(SEQLEN, dtype=jnp.int32)
    cos_tab, sin_tab = rope_tables(positions, HEAD_DIM)
    score_scale = HEAD_DIM ** (-0.5)

    def attend_one(seq_pair):
        sequence, seq_len = seq_pair
        normed = low(sequence * lax.rsqrt(lax.optimization_barrier(jnp.mean(sequence * sequence, -1, keepdims=True)) + EPS) * attn_norm)
        query_lin = low_back(matmul(normed, w_query)).reshape(SEQLEN, HEADS, HEAD_DIM)
        key_lin = low_back(matmul(normed, w_key)).reshape(SEQLEN, KV_HEADS, HEAD_DIM)
        queries = low(rotate(query_lin, cos_tab, sin_tab)).reshape(SEQLEN, KV_HEADS, group_size, HEAD_DIM)
        keys_rot = low(rotate(key_lin, cos_tab, sin_tab))
        values_rot = low(low_back(matmul(normed, w_value))).reshape(SEQLEN, KV_HEADS, HEAD_DIM)
        raw_scores = jnp.einsum('qhgd,khd->hgqk', queries, keys_rot, precision=HIGH)
        allowed = (positions[None, :] <= positions[:, None]) & (positions[None, :] < seq_len)
        scores = jnp.where(allowed, low_back(raw_scores) * score_scale, NEG)
        softmax_w = jax.nn.softmax(scores, -1)
        attended = jnp.einsum('hgqk,khd->qhgd', low(softmax_w), values_rot, precision=HIGH).reshape(SEQLEN, HEADS * HEAD_DIM)
        branch = low_back(matmul(low(low_back(attended)), w_out))
        return sequence + branch
    hidden = lax.map(jax.checkpoint(attend_one), (inputs, lengths))

    def mix_one(triple):
        sequence, seq_len, route_rows = triple
        normed = low(sequence * lax.rsqrt(lax.optimization_barrier(jnp.mean(sequence * sequence, -1, keepdims=True)) + EPS) * ffn_norm)
        logits = low_back(matmul(normed, w_router))
        route_hot = (route_rows[:, :, None] == jnp.arange(EXPERTS, dtype=jnp.int32)[None, None, :]).astype(jnp.float32)
        picked = lax.optimization_barrier(jnp.sum(route_hot * logits[:, None, :], -1))
        gate_vals = jax.nn.softmax(picked, -1)
        weights = lax.optimization_barrier(jnp.sum(route_hot * gate_vals[:, :, None], 1))

        def expert_step(expert_sum, expert_item):
            gate_w, up_w, down_w, column = expert_item
            expert_in = low_back(normed)
            gate_before_activation = low_back(matmul(expert_in, gate_w))
            up_before_activation = low_back(matmul(expert_in, up_w))
            inner_activation = low(jax.nn.silu(gate_before_activation) * up_before_activation)
            output = low(low_back(matmul(inner_activation, down_w)))
            return (expert_sum + column[:, None] * output, None)
        start_sum = jnp.zeros((SEQLEN, D), jnp.float32)
        expert_sum, unused = lax.scan(jax.checkpoint(expert_step), start_sum, (expert_gate_weight, expert_up_weight, expert_down_weight, weights.T))
        valid_rows = (positions < seq_len).astype(jnp.float32)[:, None]
        return valid_rows * (sequence + expert_sum)
    return lax.map(jax.checkpoint(mix_one), (hidden, lengths, routes))

def reference(tokens, lengths, routes, cotangent, attn_norm, w_query, w_key, w_value, w_out, ffn_norm, w_router, expert_gate_weight, expert_up_weight, expert_down_weight):
    params = tuple((array.astype(jnp.float32) for array in (tokens, attn_norm, w_query, w_key, w_value, w_out, ffn_norm, w_router, expert_gate_weight, expert_up_weight, expert_down_weight)))

    def wrapped(inputs, gain_one, query_w, key_w, value_w, out_w, gain_two, router_w, gate_w, up_w, down_w):
        return forward(inputs, gain_one, query_w, key_w, value_w, out_w, gain_two, router_w, gate_w, up_w, down_w, lengths, routes)
    result, pullback = jax.vjp(wrapped, *params)
    grads = pullback(cotangent.astype(jnp.float32))
    return (result.astype(jnp.bfloat16), grads[0].astype(jnp.bfloat16), grads[1], grads[2], grads[3], grads[4], grads[5], grads[6], grads[7], grads[8], grads[9], grads[10])
```

```python
import functools

import jax
import jax.numpy as jnp
import numpy as np
from jax import lax
from jax.experimental import pallas as pl
from jax.experimental.pallas import tpu as pltpu
from jax.sharding import PartitionSpec as P

HEAD_DIM = 64
EPS = 1e-06
THETA = 10000.0
NEG = -1e30
LOG2E = 1.4426950408889634
NZ = 4
CORES = 2
F32 = jnp.float32
BF16 = jnp.bfloat16


def dot(a, b, ca, cb):
    return lax.dot_general(a, b, (((ca,), (cb,)), ((), ())), preferred_element_type=F32)


def params(semantics, mib):
    return pltpu.CompilerParams(
        dimension_semantics=semantics, vmem_limit_bytes=mib * 1024 * 1024
    )


def cost(flops, nbytes, trans=0):
    return pl.CostEstimate(flops=flops, bytes_accessed=nbytes, transcendentals=trans)


def rope_tables(ctx_index, ctx_size, rows):
    half = HEAD_DIM // 2
    inv = THETA ** (-np.arange(half, dtype=np.float64) / half)
    fine = np.arange(rows, dtype=np.float64)[:, None] * inv[None, :]
    coarse = (rows * np.arange(ctx_size, dtype=np.float64))[:, None] * inv[None, :]
    tile = lambda t: np.tile(t, (1, 128 // half)).astype(np.float32)
    pick = lambda t: lax.dynamic_slice_in_dim(jnp.asarray(tile(t)), ctx_index, 1, 0)
    cos_f, sin_f = jnp.asarray(tile(np.cos(fine))), jnp.asarray(tile(np.sin(fine)))
    cos_c, sin_c = pick(np.cos(coarse)), pick(np.sin(coarse))
    cos = cos_f * cos_c - sin_f * sin_c
    sin = sin_f * cos_c + cos_f * sin_c
    sign = np.where(np.arange(128) % HEAD_DIM < half, -1.0, 1.0).astype(np.float32)
    return cos, sin * jnp.asarray(sign)[None, :]


def swap_halves(x, roll):
    half = HEAD_DIM // 2
    width = x.shape[1]
    lane = lax.broadcasted_iota(jnp.int32, x.shape, 1)
    return jnp.where(lane % HEAD_DIM < half, roll(x, width - half), roll(x, half))


def project_body(x_ref, gain_ref, wq_ref, wk_ref, wv_ref, cos_ref, sin_ref, n_ref, q_ref, kv_ref):
    step = pl.program_id(0)
    nq = pl.num_programs(0) - 4

    @pl.when(step == 0)
    def _():
        x = x_ref[...].astype(F32)
        scale = lax.rsqrt(jnp.mean(x * x, -1, keepdims=True) + EPS)
        n_ref[...] = (x * scale * gain_ref[...]).astype(BF16)

    def rope(lin):
        cos = jnp.concatenate([cos_ref[...]] * 2, 1)
        sin = jnp.concatenate([sin_ref[...]] * 2, 1)
        return lin * cos + swap_halves(lin, lambda v, s: pltpu.roll(v, s, 1)) * sin

    @pl.when(step < nq)
    def _():
        lin = dot(n_ref[...], wq_ref[...], 1, 0)
        q_ref[...] = rope(lin).astype(BF16) * jnp.asarray(HEAD_DIM**-0.5, BF16)

    @pl.when((step >= nq) & (step < nq + 2))
    def _():
        kv_ref[...] = rope(dot(n_ref[...], wk_ref[...], 1, 0)).astype(BF16)[None]

    @pl.when(step >= nq + 2)
    def _():
        kv_ref[...] = dot(n_ref[...], wv_ref[...], 1, 0).astype(BF16)[None]


def project(x, gain, wq, wk, wv, cos, sin):
    rows, width = x.shape
    nq = wq.shape[1] // 256
    kvw = wk.shape[1]
    nk = kvw // 256
    clip = lambda v, hi: jnp.minimum(jnp.maximum(v, 0), hi)
    full = lambda shape: pl.BlockSpec(shape, lambda i: (0, 0))
    return pl.pallas_call(
        project_body,
        grid=(nq + 2 * nk,),
        in_specs=[
            full((rows, width)),
            full((1, width)),
            pl.BlockSpec((width, 256), lambda i: (0, clip(i, nq - 1))),
            pl.BlockSpec((width, 256), lambda i: (0, clip(i - nq, nk - 1))),
            pl.BlockSpec((width, 256), lambda i: (0, clip(i - nq - nk, nk - 1))),
            full((rows, 128)),
            full((rows, 128)),
        ],
        out_specs=[
            full((rows, width)),
            pl.BlockSpec((rows, 256), lambda i: (0, clip(i, nq - 1))),
            pl.BlockSpec(
                (1, rows, 256),
                lambda i: (clip(i - nq, 2 * nk - 1) // nk, 0, clip(i - nq, 2 * nk - 1) % nk),
            ),
        ],
        out_shape=[
            jax.ShapeDtypeStruct((rows, width), BF16),
            jax.ShapeDtypeStruct((rows, wq.shape[1]), BF16),
            jax.ShapeDtypeStruct((2, rows, kvw), BF16),
        ],
        compiler_params=params(("arbitrary",), 32),
        cost_estimate=cost(2 * rows * width * 2 * width, 6 * 1024 * 1024),
        name="project",
    )(x, gain, wq, wk, wv, cos, sin)


def split_heads(block):
    lane = lax.broadcasted_iota(jnp.int32, block.shape, 1)
    low = lane < HEAD_DIM
    zero = jnp.zeros_like(block)
    turned = jnp.concatenate([block[:, HEAD_DIM:], block[:, :HEAD_DIM]], 1)
    first = jnp.concatenate([jnp.where(low, block, zero), jnp.where(low, zero, turned)], 0)
    second = jnp.concatenate([jnp.where(low, turned, zero), jnp.where(low, zero, block)], 0)
    return first, second


def attend_body(roles, info_ref, q_ref, *refs):
    kv_refs = refs[:roles]
    wo_ref, x_ref, gain_ref, att_ref, lse_ref, hid_ref, mix_ref, acc, top, proj = refs[roles:]
    step = pl.program_id(0)
    rows = q_ref.shape[0]
    seq_len = info_ref[0]
    acc[...] = jnp.zeros_like(acc)
    top[...] = jnp.full_like(top, NEG)
    row = lax.broadcasted_iota(jnp.int32, (rows, rows), 0)
    col = lax.broadcasted_iota(jnp.int32, (rows, rows), 1)
    lane = lax.broadcasted_iota(jnp.int32, (rows, 128), 1)
    stack_row = lax.broadcasted_iota(jnp.int32, (2 * rows, 128), 0)
    stack_lane = lax.broadcasted_iota(jnp.int32, (2 * rows, 128), 1)
    ones = jnp.where((stack_lane == 0) == (stack_row < rows), 1.0, 0.0)
    ones = jnp.where(stack_lane < 2, ones, 0.0).astype(BF16)

    for role in range(roles):
        start, active, causal = (info_ref[1 + 3 * role + i] for i in range(3))

        @pl.when(active > 0)
        def _(role=role, start=start, causal=causal):
            keys = split_heads(kv_refs[role][0])
            values = split_heads(kv_refs[role][1])
            bad = col + start >= seq_len
            if role == 0:
                bad = bad | (col > row)
            bias = jnp.where(bad, NEG, 0.0)
            for pair in range(2):
                q = q_ref[:, pair * 128 : pair * 128 + 128]
                scores = dot(q, keys[pair], 1, 1)
                weights, shrinks, news = [], [], []
                for head in range(2):
                    part = scores[:, head * rows : (head + 1) * rows] + bias
                    old = top[:, 2 * pair + head : 2 * pair + head + 1]
                    new = jnp.maximum(old, jnp.max(part, 1, keepdims=True))
                    weights.append(jnp.exp2((part - new) * LOG2E).astype(BF16))
                    shrinks.append(jnp.exp2((old - new) * LOG2E))
                    top[:, 2 * pair + head : 2 * pair + head + 1] = new
                both = jnp.concatenate(weights, 1)
                full = jnp.concatenate([values[pair], ones], 1)
                fresh = dot(both, full, 1, 0)
                shrink = jnp.concatenate(
                    [
                        jnp.where(lane < HEAD_DIM, shrinks[0], shrinks[1]),
                        jnp.where(lane == 0, shrinks[0], shrinks[1]),
                    ],
                    1,
                )
                acc[pair] = acc[pair] * shrink + fresh

    for pair in range(2):
        sums = [acc[pair, :, 128 + head : 129 + head] for head in range(2)]
        total = jnp.where(lane < HEAD_DIM, sums[0], sums[1])
        att = (acc[pair, :, :128] / total).astype(BF16)
        att_ref[:, pair * 128 : pair * 128 + 128] = att
        for head in range(2):
            at = 2 * pair + head
            lse_ref[0, :, at : at + 1] = top[:, at : at + 1] * LOG2E + jnp.log2(sums[head])

    @pl.when(step == 0)
    def _():
        proj[...] = x_ref[...].astype(F32)

    proj[...] += dot(att_ref[...], wo_ref[...], 1, 0)

    @pl.when(step == pl.num_programs(0) - 1)
    def _():
        hidden = proj[...]
        scale = lax.rsqrt(jnp.mean(hidden * hidden, -1, keepdims=True) + EPS)
        hid_ref[...] = hidden
        mix_ref[...] = (hidden * scale * gain_ref[...]).astype(BF16)


def attend(info, q, blocks, wo, x, gain):
    rows, width = q.shape
    steps = width // 256
    roles = len(blocks)
    full = lambda shape: pl.BlockSpec(shape, lambda i, s: (0, 0))
    return pl.pallas_call(
        functools.partial(attend_body, roles),
        grid_spec=pltpu.PrefetchScalarGridSpec(
            num_scalar_prefetch=1,
            grid=(steps,),
            in_specs=[pl.BlockSpec((rows, 256), lambda i, s: (0, i))]
            + [pl.BlockSpec((2, rows, 128), lambda i, s: (0, 0, i))] * roles
            + [
                pl.BlockSpec((256, x.shape[1]), lambda i, s: (i, 0)),
                full(x.shape),
                full((1, x.shape[1])),
            ],
            out_specs=[
                pl.BlockSpec((rows, 256), lambda i, s: (0, i)),
                pl.BlockSpec((1, rows, 128), lambda i, s: (i, 0, 0)),
                full(x.shape),
                full(x.shape),
            ],
            scratch_shapes=[
                pltpu.VMEM((2, rows, 256), F32),
                pltpu.VMEM((rows, 128), F32),
                pltpu.VMEM(x.shape, F32),
            ],
        ),
        out_shape=[
            jax.ShapeDtypeStruct((rows, width), BF16),
            jax.ShapeDtypeStruct((steps, rows, 128), F32),
            jax.ShapeDtypeStruct(x.shape, F32),
            jax.ShapeDtypeStruct(x.shape, BF16),
        ],
        compiler_params=params(("arbitrary",), 40),
        cost_estimate=cost(16 * rows * rows * roles * width, 8 * 1024 * 1024),
        name="attend",
    )(info, q, *blocks, wo, x, gain)


def attend_back_body(roles, info_ref, q_ref, do_ref, lse_ref, delta_ref, *refs):
    kv_refs, dq_ref, dkv_refs = refs[:roles], refs[roles], refs[roles + 1 :]
    rows = q_ref.shape[0]
    seq_len = info_ref[0]
    dq_ref[...] = jnp.zeros_like(dq_ref)
    key = lax.broadcasted_iota(jnp.int32, (rows, rows), 0)
    query = lax.broadcasted_iota(jnp.int32, (rows, rows), 1)
    lane = lax.broadcasted_iota(jnp.int32, (rows, 128), 1)
    low = lane < HEAD_DIM

    for role in range(roles):
        start, active, causal = (info_ref[1 + 3 * role + i] for i in range(3))

        @pl.when(active == 0)
        def _(role=role):
            dkv_refs[role][...] = jnp.zeros_like(dkv_refs[role])

        @pl.when(active > 0)
        def _(role=role, start=start):
            keys = split_heads(kv_refs[role][0])
            values = split_heads(kv_refs[role][1])
            bad = key + start >= seq_len
            if role == 0:
                bad = bad | (key > query)
            bias = jnp.where(bad, NEG, 0.0)
            dks, dvs = [], []
            for pair in range(2):
                q = q_ref[:, pair * 128 : pair * 128 + 128]
                do = do_ref[:, pair * 128 : pair * 128 + 128]
                scores = dot(keys[pair], q, 1, 1)
                grads = dot(values[pair], do, 1, 1)
                probs, raws = [], []
                for head in range(2):
                    at = 2 * pair + head
                    part = scores[head * rows : (head + 1) * rows] * LOG2E + bias
                    prob = jnp.exp2(part - lse_ref[0, at : at + 1, :])
                    grad = grads[head * rows : (head + 1) * rows]
                    raws.append((prob * (grad - delta_ref[0, at : at + 1, :])).astype(BF16))
                    probs.append(prob.astype(BF16))
                raw = jnp.concatenate(raws, 0)
                dq_ref[:, pair * 128 : pair * 128 + 128] += dot(raw, keys[pair], 0, 0)
                dks.append(dot(raw, q, 1, 0))
                dvs.append(dot(jnp.concatenate(probs, 0), do, 1, 0))
            for which, parts in enumerate((dks, dvs)):
                top_a, bottom_a = parts[0][:rows], parts[0][rows:]
                top_b, bottom_b = parts[1][:rows], parts[1][rows:]
                turn = pltpu.roll(jnp.where(low, top_b, bottom_a), HEAD_DIM, 1)
                whole = jnp.where(low, top_a, bottom_b) + turn
                dkv_refs[role][which] = whole.astype(dkv_refs[role].dtype)


def attend_back(info, q, do, lse, delta, blocks):
    rows, width = q.shape
    steps = width // 256
    roles = len(blocks)
    kvw = blocks[0].shape[2]
    wide = pl.BlockSpec((rows, 256), lambda i, s: (0, i))
    heads = pl.BlockSpec((1, 8, rows), lambda i, s: (i, 0, 0))
    kv = pl.BlockSpec((2, rows, 128), lambda i, s: (0, 0, i))
    return pl.pallas_call(
        functools.partial(attend_back_body, roles),
        grid_spec=pltpu.PrefetchScalarGridSpec(
            num_scalar_prefetch=1,
            grid=(steps,),
            in_specs=[wide, wide, heads, heads] + [kv] * roles,
            out_specs=[wide] + [kv] * roles,
        ),
        out_shape=[jax.ShapeDtypeStruct((rows, width), F32)]
        + [jax.ShapeDtypeStruct((2, rows, kvw), F32)]
        + [jax.ShapeDtypeStruct((2, rows, kvw), BF16)] * (roles - 1),
        compiler_params=params(("arbitrary",), 40),
        cost_estimate=cost(40 * rows * rows * roles * width, 16 * 1024 * 1024),
        name="attend_back",
    )(info, q, do, lse, delta, *blocks)


def expert_body(own, remotes, experts, info_ref, x_ref, cot_ref, wr_ref, *refs):
    wg_hbm, wu_hbm, wd_hbm = refs[:3]
    far = refs[3 : 3 + remotes]
    outs = refs[3 + remotes :]
    if len(outs) == 18:
        outs = outs[5:]
    (gm_ref, gate_ref, out_ref, xs_ref, inner_ref, dg_ref, du_ref) = outs[:7]
    wbuf, sem, gm_acc, out_acc, gates, back = outs[7:]
    step = pl.program_id(0)
    total = own + remotes
    rows, width = x_ref.shape
    ff = width // 2
    slot = lax.rem(step, 2)

    def fetch(target, at):
        @pl.when(target < own)
        def _():
            src = (
                wg_hbm.at[target],
                wu_hbm.at[target],
                wd_hbm.at[target, :, pl.ds(0, ff)],
                wd_hbm.at[target, :, pl.ds(ff, ff)],
            )
            offsets = (0, width, 2 * width, 2 * width + ff)
            sizes = (width, width, ff, ff)
            for piece, (ref, off, size) in enumerate(zip(src, offsets, sizes)):
                pltpu.make_async_copy(
                    ref, wbuf.at[at, pl.ds(off, size)], sem.at[at, piece]
                ).start()

        for i in range(remotes):

            @pl.when(target == own + i)
            def _(i=i):
                offsets = (0, width, 2 * width, 2 * width + ff)
                sizes = (width, width, ff, ff)
                for piece, (off, size) in enumerate(zip(offsets, sizes)):
                    pltpu.make_async_copy(
                        far[i].at[pl.ds(off, size)],
                        wbuf.at[at, pl.ds(off, size)],
                        sem.at[at, piece],
                    ).start()

    @pl.when(step == 0)
    def _():
        fetch(jnp.int32(0), 0)

    @pl.when(step + 1 < total)
    def _():
        fetch(step + 1, lax.rem(step + 1, 2))

    lane = lax.broadcasted_iota(jnp.int32, (rows, 128), 1)

    @pl.when(step == 0)
    def _():
        logits = dot(x_ref[...], wr_ref[...], 1, 0)
        mask_t = cot_ref[pl.ds(rows, experts), :rows].astype(F32)
        mask_t = jnp.concatenate([mask_t, jnp.zeros((128 - experts, rows), F32)], 0)
        mask = jnp.transpose(mask_t) > 0.5
        high = jnp.max(jnp.where(mask, logits, NEG), 1, keepdims=True)
        raised = jnp.where(mask, jnp.exp(logits - high), 0.0)
        gates[...] = raised / jnp.sum(raised, 1, keepdims=True)
        gate_ref[...] = gates[...]
        back[...] = jnp.zeros_like(back)
        gm_acc[...] = jnp.zeros_like(gm_acc)
        out_acc[...] = jnp.zeros_like(out_acc)
        xs_ref[0] = x_ref[...]

    offsets = (0, width, 2 * width, 2 * width + ff)
    sizes = (width, width, ff, ff)
    for piece, (off, size) in enumerate(zip(offsets, sizes)):
        pltpu.make_async_copy(
            far[0].at[pl.ds(off, size)] if remotes else wg_hbm.at[0, pl.ds(0, size)],
            wbuf.at[slot, pl.ds(off, size)],
            sem.at[slot, piece],
        ).wait()

    wg = wbuf[slot, :width, :]
    wu = wbuf[slot, width : 2 * width, :]
    wd0 = wbuf[slot, 2 * width : 2 * width + ff, :]
    wd1 = wbuf[slot, 2 * width + ff :, :]
    which = info_ref[2] + info_ref[3 + step]
    x = x_ref[...]
    cot = cot_ref[pl.ds(0, rows), :]
    g = dot(x, wg, 1, 0)
    u = dot(x, wu, 1, 0)
    raw = dot(cot[:, :ff], wd0, 1, 1) + dot(cot[:, ff:], wd1, 1, 1)
    gate = jnp.sum(jnp.where(lane == which, gates[...], 0.0), 1, keepdims=True)
    sig = 1.0 / (1.0 + jnp.exp(-g))
    silu = g * sig
    inner = silu * u
    gg = jnp.sum(raw * inner, 1, keepdims=True)
    back[...] += jnp.where(lane == which, gg, 0.0)
    scaled = (gate * inner).astype(BF16)
    gi = gate * raw
    dg = (gi * u * (sig * (1.0 + g * (1.0 - sig)))).astype(BF16)
    du = (gi * silu).astype(BF16)
    inner_ref[0] = scaled
    dg_ref[0] = dg
    du_ref[0] = du
    out_acc[:, :ff] += dot(scaled, wd0, 1, 0)
    out_acc[:, ff:] += dot(scaled, wd1, 1, 0)
    gm_acc[...] += dot(dg, wg, 1, 1) + dot(du, wu, 1, 1)

    @pl.when(step == total - 1)
    def _():
        gm_ref[pl.ds(0, rows), :] = gm_acc[...].astype(BF16)
        back_t = jnp.transpose(back[...])[:experts, :].astype(BF16)
        pad = jnp.zeros((experts, width - rows), BF16)
        gm_ref[pl.ds(rows, experts), :] = jnp.concatenate([back_t, pad], 1)
        out_ref[0] = out_acc[...].astype(BF16)


def expert_call(info, x, cot_all, wr, own_weights, far, experts, kept):
    rows, width = x.shape
    own = own_weights[0].shape[0]
    remotes = len(far)
    total = own + remotes
    ff = width // 2
    ext = rows + experts
    full = lambda shape: pl.BlockSpec(shape, lambda i, s: (0, 0))
    anywhere = pl.BlockSpec(memory_space=pl.ANY)
    big = pl.BlockSpec((1, rows, width), lambda i, s: (s[0], 0, 0))
    part = pl.BlockSpec((1, rows, ff), lambda i, s: (s[0], 0, s[3 + i]))
    wide = jax.ShapeDtypeStruct((NZ, rows, width), BF16)
    hidden = jax.ShapeDtypeStruct((NZ, rows, total * ff), BF16)
    alias = {} if kept is None else {7 + remotes + i: 2 + i for i in range(5)}
    outs = pl.pallas_call(
        functools.partial(expert_body, own, remotes, experts),
        grid_spec=pltpu.PrefetchScalarGridSpec(
            num_scalar_prefetch=1,
            grid=(total,),
            in_specs=[
                full((rows, width)),
                pl.BlockSpec((ext, width), lambda i, s: (s[0], 0)),
                full(wr.shape),
            ]
            + [anywhere] * (3 + remotes + (0 if kept is None else 5)),
            out_specs=[full((ext, width)), full((rows, 128)), big, big, part, part, part],
            scratch_shapes=[
                pltpu.VMEM((2, 3 * width, ff), BF16),
                pltpu.SemaphoreType.DMA((2, 4)),
                pltpu.VMEM((rows, width), F32),
                pltpu.VMEM((rows, width), F32),
                pltpu.VMEM((rows, 128), F32),
                pltpu.VMEM((rows, 128), F32),
            ],
        ),
        out_shape=[
            jax.ShapeDtypeStruct((ext, width), BF16),
            jax.ShapeDtypeStruct((rows, 128), F32),
            wide,
            wide,
            hidden,
            hidden,
            hidden,
        ],
        input_output_aliases=alias,
        compiler_params=params(("arbitrary",), 40),
        cost_estimate=cost(12 * rows * width * ff * total, total * 6 * width * ff),
        name="experts",
    )(info, x, cot_all, wr, *own_weights, *far, *(kept or ()))
    return outs[0], outs[1], tuple(outs[2:])


def local(
    tokens,
    lengths,
    routes,
    cotangent,
    attn_norm,
    w_query,
    w_key,
    w_value,
    w_out,
    ffn_norm,
    w_router,
    expert_gate_weight,
    expert_up_weight,
    expert_down_weight,
):
    rows, width = tokens.shape[1:]
    experts = w_router.shape[1]
    own = expert_gate_weight.shape[0]
    ff = expert_gate_weight.shape[2]
    ctx_size, ep_size = lax.axis_size("ctx"), lax.axis_size("ep")
    ny, nx = ctx_size // CORES, ep_size // NZ
    ctx_index, ep_index = lax.axis_index("ctx"), lax.axis_index("ep")
    y, core = ctx_index // CORES, ctx_index % CORES
    z, xpos = ep_index // nx, ep_index % nx
    seq_len = lengths[0]
    low = tokens[0]
    positions = ctx_index * rows + jnp.arange(rows, dtype=jnp.int32)
    valid_flag = positions < seq_len
    valid = valid_flag.astype(F32)[:, None]

    core_swap = [(c, c ^ 1) for c in range(ctx_size)]
    core_up = [(c, c + 1) for c in range(0, ctx_size, CORES)]
    core_down = [(c + 1, c) for c in range(0, ctx_size, CORES)]
    y_up = lambda k: [(c, c + CORES * k) for c in range(ctx_size - CORES * k)]
    y_down = lambda k: [(b, a) for a, b in y_up(k)]
    zx = lambda pairs: [(a * nx + i, b * nx + i) for a, b in pairs for i in range(nx)]
    z_groups = [[i + nx * k for k in range(NZ)] for i in range(nx)]
    x_groups = [[nx * k + i for i in range(nx)] for k in range(NZ)]
    x_shift = lambda s: [(k * nx + i, k * nx + (i + s) % nx) for k in range(NZ) for i in range(nx)]

    sent = jnp.concatenate(
        [
            expert_gate_weight[core],
            expert_up_weight[core],
            expert_down_weight[core][:, :ff],
            expert_down_weight[core][:, ff:],
        ],
        0,
    )
    far, places = [], [xpos * own, xpos * own + 1]
    for shift in range(1, nx):
        arrived = lax.ppermute(sent, "ep", x_shift(shift))
        far += [arrived, lax.ppermute(arrived, "ctx", core_swap)]
        origin = (xpos - shift) % nx * own
        places += [origin + core, origin + 1 - core]

    cot_low = jnp.where(valid_flag[:, None], cotangent[0], jnp.zeros((), BF16))
    ids = jnp.arange(experts, dtype=jnp.int32)
    mask_t = jnp.any(routes[0][None] == ids[:, None, None], -1).astype(BF16)
    mask_t = jnp.pad(mask_t, ((0, 0), (0, width - rows)))
    cot_all = lax.all_gather(
        jnp.concatenate([cot_low, mask_t], 0), "ep", axis_index_groups=z_groups, tiled=True
    )

    cos, sin = rope_tables(ctx_index, ctx_size, rows)
    normed, q, kv = project(low, attn_norm[None], w_query, w_key, w_value, cos, sin)

    blocks = [kv, lax.ppermute(kv, "ctx", core_up)]
    facts = [(ctx_index * rows, True), ((ctx_index - 1) * rows, core == 1)]
    travelling = kv
    for back in range(1, ny):
        travelling = lax.ppermute(travelling, "ctx", y_up(1))
        blocks += [travelling, lax.ppermute(travelling, "ctx", core_swap)]
        base = (y - back) * CORES
        facts += [((base + core) * rows, y >= back), ((base + 1 - core) * rows, y >= back)]
    info = [seq_len]
    for start, reach in facts:
        info += [start, (jnp.asarray(reach) & (start < seq_len)).astype(jnp.int32), jnp.int32(0)]
    info = jnp.stack([jnp.asarray(v, jnp.int32) for v in info])

    attended, lse, hidden, mixed = attend(info, q, blocks, w_out, low, ffn_norm[None])

    near = lax.ppermute(mixed, "ep", zx([(0, 1), (1, 0), (2, 3), (3, 2)]))
    middle = lax.ppermute(mixed, "ep", zx([(1, 2), (2, 1)]))
    across = lax.ppermute(near, "ep", zx([(1, 2), (2, 1)]))
    outward = lax.ppermute(middle, "ep", zx([(1, 0), (2, 3)]))
    last = lax.ppermute(across, "ep", zx([(1, 0), (2, 3)]))
    inside = (z == 1) | (z == 2)
    shards = [
        (mixed, z),
        (near, z ^ 1),
        (jnp.where(inside, middle, outward), jnp.where(z < 2, 2, 1)),
        (jnp.where(inside, across, last), jnp.where(z < 2, 3, 0)),
    ]
    wr = jnp.pad(w_router, ((0, 0), (0, 128 - experts)))
    weights = (expert_gate_weight, expert_up_weight, expert_down_weight)
    kept, gms, gates = None, [], None
    for data, shard in shards:
        facts = [shard, jnp.int32(0), z * nx * own] + places
        facts = jnp.stack([jnp.asarray(v, jnp.int32) for v in facts])
        gm, gate, kept = expert_call(facts, data, cot_all, wr, weights, far, experts, kept)
        gms.append(gm)
        gates = gate if gates is None else gates

    add = lambda a, b: (a.astype(F32) + b.astype(F32)).astype(BF16)
    first = lax.ppermute(gms[3], "ep", zx([(0, 1), (3, 2)]))
    second = lax.ppermute(gms[2], "ep", zx([(0, 1), (3, 2)]))
    carried = lax.ppermute(add(gms[3], first), "ep", zx([(1, 2), (2, 1)]))
    third = lax.ppermute(gms[1], "ep", zx([(0, 1), (3, 2)]))
    turned = lax.ppermute(add(gms[2], second), "ep", zx([(1, 2), (2, 1)]))
    final = lax.ppermute(add(gms[1], carried), "ep", zx([(2, 3), (1, 0)]))
    summed = gms[0].astype(F32) + third.astype(F32) + turned.astype(F32) + final.astype(F32)

    out_all, x_all, inner_all, dg_all, du_all = kept
    cot_rows = cot_all.reshape(NZ, rows + experts, width)[:, :rows].reshape(NZ * rows, width)
    x_rows = x_all.reshape(NZ * rows, width)
    group = nx * own
    flat = lambda a: a.reshape(NZ * rows, group * ff)
    grad_gate_w = dot(x_rows, flat(dg_all), 0, 0).astype(BF16)
    grad_up_w = dot(x_rows, flat(du_all), 0, 0).astype(BF16)
    grad_down = dot(flat(inner_all), cot_rows, 0, 0).astype(BF16)
    stack = lambda w: w.reshape(width, nx, own, ff).transpose(1, 2, 0, 3).reshape(nx * own, width, ff)
    expert_grads = (stack(grad_gate_w), stack(grad_up_w), grad_down.reshape(nx * own, ff, width))
    expert_grads = tuple(
        lax.psum(
            lax.psum_scatter(
                g, "ep", scatter_dimension=0, axis_index_groups=x_groups, tiled=True
            ),
            "ctx",
        ).astype(F32)
        for g in expert_grads
    )
    expert_sum = lax.psum_scatter(
        out_all.reshape(NZ * rows, width),
        "ep",
        scatter_dimension=0,
        axis_index_groups=z_groups,
        tiled=True,
    ).astype(F32)
    result_out = (valid * (hidden + expert_sum)).astype(BF16)

    grad_mixed = summed[:rows]
    grad_gates = summed[rows:, :rows].T
    gates = gates[:, :experts]
    grad_logits = gates * (grad_gates - jnp.sum(gates * grad_gates, -1, keepdims=True))
    grad_logits = grad_logits.astype(BF16)
    grad_router = dot(mixed, grad_logits, 0, 0)
    grad_mixed = grad_mixed + dot(grad_logits, w_router, 1, 1)
    rms_ffn = lax.rsqrt(jnp.mean(hidden * hidden, -1, keepdims=True) + EPS)
    grad_ffn_norm = jnp.sum(grad_mixed * hidden * rms_ffn, 0)
    weighted = grad_mixed * ffn_norm
    mean_term = jnp.mean(weighted * hidden, -1, keepdims=True)
    grad_hidden = cot_low.astype(F32) + rms_ffn * weighted - hidden * rms_ffn**3 * mean_term
    grad_branch = grad_hidden.astype(BF16)
    grad_w_out = dot(attended, grad_branch, 0, 0)
    grad_attended = dot(grad_branch, w_out, 1, 1).astype(BF16)
    heads = w_query.shape[1] // HEAD_DIM
    delta = grad_attended.astype(F32) * attended.astype(F32)
    delta = jnp.sum(delta.reshape(rows, heads, HEAD_DIM), -1)
    to_rows = lambda a: jnp.pad(a, ((0, 0), (0, 4), (0, 0)))
    delta = to_rows(delta.T.reshape(heads // 4, 4, rows))
    lse = to_rows(lse[:, :, :4].transpose(0, 2, 1))
    dq, *dkvs = attend_back(info, q, grad_attended, lse, delta, blocks)

    dkv = dkvs[0] + lax.ppermute(dkvs[1], "ctx", core_down).astype(F32)
    for back in range(1, ny):
        same, other = dkvs[2 * back], dkvs[2 * back + 1]
        both = add(same, lax.ppermute(other, "ctx", core_swap))
        dkv = dkv + lax.ppermute(both, "ctx", y_down(back)).astype(F32)

    def rope_back(g):
        reps = g.shape[1] // 128
        swapped = swap_halves(g, lambda v, s: jnp.roll(v, s, 1))
        return (g * jnp.tile(cos, (1, reps)) - swapped * jnp.tile(sin, (1, reps))).astype(BF16)

    grad_query_lin = rope_back(dq * HEAD_DIM**-0.5)
    grad_key_lin = rope_back(dkv[0])
    grad_value_lin = dkv[1].astype(BF16)
    grad_w_query = dot(normed, grad_query_lin, 0, 0)
    grad_w_key = dot(normed, grad_key_lin, 0, 0)
    grad_w_value = dot(normed, grad_value_lin, 0, 0)
    grad_normed = (
        dot(grad_query_lin, w_query, 1, 1)
        + dot(grad_key_lin, w_key, 1, 1)
        + dot(grad_value_lin, w_value, 1, 1)
    )
    inputs = low.astype(F32)
    rms_attn = lax.rsqrt(jnp.mean(inputs * inputs, -1, keepdims=True) + EPS)
    grad_attn_norm = jnp.sum(grad_normed * inputs * rms_attn, 0)
    weighted = grad_normed * attn_norm
    mean_term = jnp.mean(weighted * inputs, -1, keepdims=True)
    grad_inputs = grad_hidden + rms_attn * weighted - inputs * rms_attn**3 * mean_term
    total = lax.psum(
        (
            grad_w_query,
            grad_w_key,
            grad_w_value,
            grad_w_out,
            grad_router,
            grad_attn_norm,
            grad_ffn_norm,
        ),
        ("ep", "ctx"),
    )
    return (
        result_out[None],
        grad_inputs.astype(BF16)[None],
        total[5],
        total[0],
        total[1],
        total[2],
        total[3],
        total[6],
        total[4],
        *expert_grads,
    )


def solution(mesh):
    rows, whole, split = P("ep", "ctx", None), P(), P("ep", None, None)
    return jax.shard_map(
        local,
        mesh=mesh,
        in_specs=(rows, P("ep"), rows, rows) + (whole,) * 7 + (split,) * 3,
        out_specs=(rows, rows) + (whole,) * 7 + (split,) * 3,
        check_vma=False,
    )
```

```python
import functools

import jax
import jax.numpy as jnp
import numpy as np
from jax import lax
from jax.experimental import pallas as pl
from jax.experimental.pallas import tpu as pltpu
from jax.sharding import PartitionSpec as P

HEAD_DIM = 64
EPS = 1e-06
THETA = 10000.0
NEG = -1e30
LOG2E = 1.4426950408889634
NZ = 4
VMEM = 58 * 1024 * 1024
CORES = 2
F32 = jnp.float32
BF16 = jnp.bfloat16


def dot(a, b, ca, cb):
    return lax.dot_general(a, b, (((ca,), (cb,)), ((), ())), preferred_element_type=F32)


def params(semantics):
    return pltpu.CompilerParams(dimension_semantics=semantics, vmem_limit_bytes=VMEM)


COST = pl.CostEstimate(flops=1 << 20, bytes_accessed=1 << 20, transcendentals=0)


def cost(flops, nbytes):
    return pl.CostEstimate(flops=flops, bytes_accessed=nbytes, transcendentals=0)


def rope_constants(ctx_size, rows):
    half = HEAD_DIM // 2
    inv = THETA ** (-np.arange(half, dtype=np.float64) / half)
    fine = np.arange(rows, dtype=np.float64)[:, None] * inv[None, :]
    coarse = (rows * np.arange(ctx_size, dtype=np.float64))[:, None] * inv[None, :]
    tile = lambda t: jnp.asarray(np.tile(t, (1, 128 // half)).astype(np.float32))
    pad = np.zeros(((-2 * ctx_size) % 8, half))
    return (
        tile(np.concatenate([np.cos(fine), np.sin(fine)], 0)),
        tile(np.concatenate([np.cos(coarse), np.sin(coarse), pad], 0)),
    )


def swap_halves(x, roll):
    half = HEAD_DIM // 2
    width = x.shape[1]
    lane = lax.broadcasted_iota(jnp.int32, x.shape, 1)
    return jnp.where(lane % HEAD_DIM < half, roll(x, width - half), roll(x, half))


def prepare_body(experts, info_ref, r_ref, c_ref, wg, wu, wd, ext_ref, sent_ref, buf, sem):
    rows, width = c_ref.shape
    ff = width // 2
    core, count = info_ref[0], info_ref[1]
    pieces = [wg.at[core], wu.at[core]] + [wd.at[core, :, pl.ds(k * ff, ff)] for k in range(2)]
    spans = [pl.ds(0, width), pl.ds(width, width), pl.ds(2 * width, ff), pl.ds(2 * width + ff, ff)]
    into = [
        pltpu.make_async_copy(piece, buf.at[span], sem.at[0, k])
        for k, (piece, span) in enumerate(zip(pieces, spans))
    ]
    back = [
        pltpu.make_async_copy(buf.at[span], sent_ref.at[span], sem.at[1, k])
        for k, span in enumerate(spans)
    ]
    for copy in into:
        copy.start()
    row = lax.broadcasted_iota(jnp.int32, (rows, width), 0)
    ext_ref[:rows] = jnp.where(row < count, c_ref[...], jnp.zeros((), BF16))
    lane = lax.broadcasted_iota(jnp.int32, (rows, 128), 1)
    named = jnp.zeros((rows, 128), F32)
    for k in range(r_ref.shape[1]):
        named = jnp.where(lane == r_ref[:, k : k + 1], 1.0, named)
    named = jnp.transpose(named)[:experts]
    ext_ref[rows:] = jnp.concatenate(
        [named, jnp.zeros((experts, width - rows), F32)], 1
    ).astype(BF16)
    for k in range(4):
        into[k].wait()
        back[k].start()
    for copy in back:
        copy.wait()


def prepare(info, routes, cot, weights, experts):
    rows, width = cot.shape
    ff = width // 2
    anywhere = pl.BlockSpec(memory_space=pl.ANY)
    full = lambda shape: pl.BlockSpec(shape, lambda i, s: (0, 0))
    return pl.pallas_call(
        functools.partial(prepare_body, experts),
        grid_spec=pltpu.PrefetchScalarGridSpec(
            num_scalar_prefetch=1,
            grid=(1,),
            in_specs=[full(routes.shape), full(cot.shape)] + [anywhere] * 3,
            out_specs=[full((rows + experts, width)), anywhere],
            scratch_shapes=[
                pltpu.VMEM((3 * width, ff), BF16),
                pltpu.SemaphoreType.DMA((2, 4)),
            ],
        ),
        out_shape=[
            jax.ShapeDtypeStruct((rows + experts, width), BF16),
            jax.ShapeDtypeStruct((3 * width, ff), BF16),
        ],
        compiler_params=params(("arbitrary",)),
        cost_estimate=COST,
        name="prepare",
    )(info, routes, cot, *weights)


def project_body(blocks, info_ref, x_ref, gain_ref, wq_ref, wk_ref, wv_ref, fine_ref, start_ref,
                 n_ref, q_ref, kv_ref, cos_ref, sin_ref):
    step = pl.program_id(0)
    nq = pl.num_programs(0) - 4
    rows = x_ref.shape[0]

    @pl.when(step == 0)
    def _():
        x = x_ref[...].astype(F32)
        scale = lax.rsqrt(jnp.mean(x * x, -1, keepdims=True) + EPS)
        n_ref[...] = (x * scale * gain_ref[...]).astype(BF16)
        cos_f, sin_f = fine_ref[:rows], fine_ref[rows:]
        cos_c = start_ref[pl.ds(info_ref[0], 1), :]
        sin_c = start_ref[pl.ds(info_ref[0] + blocks, 1), :]
        lane = lax.broadcasted_iota(jnp.int32, (rows, 128), 1)
        sign = jnp.where(lane % HEAD_DIM < HEAD_DIM // 2, -1.0, 1.0)
        cos_ref[...] = cos_f * cos_c - sin_f * sin_c
        sin_ref[...] = (sin_f * cos_c + cos_f * sin_c) * sign

    def rope(lin):
        cos = jnp.concatenate([cos_ref[...]] * 2, 1)
        sin = jnp.concatenate([sin_ref[...]] * 2, 1)
        return lin * cos + swap_halves(lin, lambda v, s: pltpu.roll(v, s, 1)) * sin

    @pl.when(step < nq)
    def _():
        lin = dot(n_ref[...], wq_ref[...], 1, 0)
        q_ref[...] = rope(lin).astype(BF16) * jnp.asarray(HEAD_DIM**-0.5, BF16)

    @pl.when((step >= nq) & (step < nq + 2))
    def _():
        kv_ref[...] = rope(dot(n_ref[...], wk_ref[...], 1, 0)).astype(BF16)[None]

    @pl.when(step >= nq + 2)
    def _():
        kv_ref[...] = dot(n_ref[...], wv_ref[...], 1, 0).astype(BF16)[None]


def project(info, x, gain, wq, wk, wv, fine, starts, blocks):
    rows, width = x.shape
    nq = wq.shape[1] // 256
    kvw = wk.shape[1]
    nk = kvw // 256
    clip = lambda v, hi: jnp.minimum(jnp.maximum(v, 0), hi)
    full = lambda shape: pl.BlockSpec(shape, lambda i, s: (0, 0))
    return pl.pallas_call(
        functools.partial(project_body, blocks),
        grid_spec=pltpu.PrefetchScalarGridSpec(
            num_scalar_prefetch=1,
            grid=(nq + 2 * nk,),
            in_specs=[
                full((rows, width)),
                full((1, width)),
                pl.BlockSpec((width, 256), lambda i, s: (0, clip(i, nq - 1))),
                pl.BlockSpec((width, 256), lambda i, s: (0, clip(i - nq, nk - 1))),
                pl.BlockSpec((width, 256), lambda i, s: (0, clip(i - nq - nk, nk - 1))),
                full(fine.shape),
                full(starts.shape),
            ],
            out_specs=[
                full((rows, width)),
                pl.BlockSpec((rows, 256), lambda i, s: (0, clip(i, nq - 1))),
                pl.BlockSpec(
                    (1, rows, 256),
                    lambda i, s: (
                        clip(i - nq, 2 * nk - 1) // nk,
                        0,
                        clip(i - nq, 2 * nk - 1) % nk,
                    ),
                ),
                full((rows, 128)),
                full((rows, 128)),
            ],
        ),
        out_shape=[
            jax.ShapeDtypeStruct((rows, width), BF16),
            jax.ShapeDtypeStruct((rows, wq.shape[1]), BF16),
            jax.ShapeDtypeStruct((2, rows, kvw), BF16),
            jax.ShapeDtypeStruct((rows, 128), F32),
            jax.ShapeDtypeStruct((rows, 128), F32),
        ],
        compiler_params=params(("arbitrary",)),
        cost_estimate=COST,
        name="project",
    )(info, x, gain, wq, wk, wv, fine, starts)


def split_heads(block):
    lane = lax.broadcasted_iota(jnp.int32, block.shape, 1)
    low = lane < HEAD_DIM
    zero = jnp.zeros_like(block)
    turned = jnp.concatenate([block[:, HEAD_DIM:], block[:, :HEAD_DIM]], 1)
    first = jnp.concatenate([jnp.where(low, block, zero), jnp.where(low, zero, turned)], 0)
    second = jnp.concatenate([jnp.where(low, turned, zero), jnp.where(low, zero, block)], 0)
    return first, second


def attend_blocks(info_ref, q_ref, kv_refs, acc, top, low, diagonal):
    rows = q_ref.shape[0]
    seq_len = info_ref[0]
    key = lax.broadcasted_iota(jnp.int32, (rows, rows), 0)
    query = lax.broadcasted_iota(jnp.int32, (rows, rows), 1)

    for role in range(len(kv_refs)):
        start, active = (info_ref[1 + 2 * role + i] for i in range(2))

        @pl.when(active > 0)
        def _(role=role, start=start):
            keys = split_heads(kv_refs[role][0])
            values = split_heads(kv_refs[role][1])
            bad = key + start >= seq_len
            if diagonal and role == 0:
                bad = bad | (key > query)
            bias = jnp.where(bad, NEG, 0.0)
            for pair in range(2):
                q = q_ref[:, pair * 128 : pair * 128 + 128]
                scores = dot(keys[pair], q, 1, 1)
                weights, shrinks = [], []
                for head in range(2):
                    at = 2 * pair + head
                    part = scores[head * rows : (head + 1) * rows] * LOG2E + bias
                    old = top[0, at : at + 1, :]
                    new = jnp.maximum(old, jnp.max(part, 0, keepdims=True))
                    prob = jnp.exp2(part - new)
                    shrink = jnp.exp2(old - new)
                    top[0, at : at + 1, :] = new
                    fresh = jnp.sum(prob, 0, keepdims=True)
                    low[0, at : at + 1, :] = low[0, at : at + 1, :] * shrink + fresh
                    weights.append(prob.astype(BF16))
                    shrinks.append(jnp.broadcast_to(shrink, (HEAD_DIM, rows)))
                fresh = dot(values[pair], jnp.concatenate(weights, 0), 0, 0)
                acc[0, pair] = acc[0, pair] * jnp.concatenate(shrinks, 0) + fresh


def attend_start_body(roles, info_ref, q_ref, *refs):
    acc, top, low = refs[roles:]
    acc[...] = jnp.zeros_like(acc)
    top[...] = jnp.full_like(top, NEG)
    low[...] = jnp.zeros_like(low)
    attend_blocks(info_ref, q_ref, refs[:roles], acc, top, low, True)


def attend_finish_body(roles, info_ref, q_ref, *refs):
    acc_in, top_in, low_in, wo_ref, x_ref, gain_ref = refs[roles : roles + 6]
    att_ref, lse_ref, hid_ref, mix_ref, acc, top, low, proj = refs[roles + 6 :]
    step = pl.program_id(0)
    rows = q_ref.shape[0]
    acc[...] = acc_in[...]
    top[...] = top_in[...]
    low[...] = low_in[...]
    attend_blocks(info_ref, q_ref, refs[:roles], acc, top, low, False)
    for pair in range(2):
        sums = [low[0, 2 * pair + head : 2 * pair + head + 1, :] for head in range(2)]
        total = [jnp.broadcast_to(1.0 / s, (HEAD_DIM, rows)) for s in sums]
        att = acc[0, pair] * jnp.concatenate(total, 0)
        att_ref[:, pair * 128 : pair * 128 + 128] = jnp.transpose(att).astype(BF16)
    lse_ref[...] = top[...] + jnp.log2(jnp.maximum(low[...], 1e-30))

    @pl.when(step == 0)
    def _():
        proj[...] = x_ref[...].astype(F32)

    proj[...] += dot(att_ref[...], wo_ref[...], 1, 0)

    @pl.when(step == pl.num_programs(0) - 1)
    def _():
        hidden = proj[...]
        scale = lax.rsqrt(jnp.mean(hidden * hidden, -1, keepdims=True) + EPS)
        hid_ref[...] = hidden
        mix_ref[...] = (hidden * scale * gain_ref[...]).astype(BF16)


def attend(info, q, blocks, state, wo=None, x=None, gain=None):
    rows, width = q.shape
    steps = width // 256
    roles = len(blocks)
    full = lambda shape: pl.BlockSpec(shape, lambda i, s: (0, 0))
    wide = pl.BlockSpec((rows, 256), lambda i, s: (0, i))
    heads = pl.BlockSpec((1, 8, rows), lambda i, s: (i, 0, 0))
    accs = pl.BlockSpec((1, 2, 128, rows), lambda i, s: (i, 0, 0, 0))
    in_specs = [wide] + [pl.BlockSpec((2, rows, 128), lambda i, s: (0, 0, i))] * roles
    state_specs = [accs, heads, heads]
    state_shapes = [jax.ShapeDtypeStruct((steps, 2, 128, rows), F32)]
    state_shapes += [jax.ShapeDtypeStruct((steps, 8, rows), F32)] * 2
    args = [info, q, *blocks]
    scratch = []
    if state is None:
        body, out_specs, out_shape = attend_start_body, state_specs, state_shapes
    else:
        body = attend_finish_body
        args += [*state, wo, x, gain]
        in_specs += state_specs
        in_specs += [
            pl.BlockSpec((256, x.shape[1]), lambda i, s: (i, 0)),
            full(x.shape),
            full((1, x.shape[1])),
        ]
        out_specs = [wide, heads, full(x.shape), full(x.shape)]
        out_shape = [
            jax.ShapeDtypeStruct((rows, width), BF16),
            jax.ShapeDtypeStruct((steps, 8, rows), F32),
            jax.ShapeDtypeStruct(x.shape, F32),
            jax.ShapeDtypeStruct(x.shape, BF16),
        ]
        scratch = [
            pltpu.VMEM((1, 2, 128, rows), F32),
            pltpu.VMEM((1, 8, rows), F32),
            pltpu.VMEM((1, 8, rows), F32),
            pltpu.VMEM(x.shape, F32),
        ]
    return pl.pallas_call(
        functools.partial(body, roles),
        grid_spec=pltpu.PrefetchScalarGridSpec(
            num_scalar_prefetch=1,
            grid=(steps,),
            in_specs=in_specs,
            out_specs=out_specs,
            scratch_shapes=scratch,
        ),
        out_shape=out_shape,
        compiler_params=params(("arbitrary",)),
        cost_estimate=COST,
        name="attend",
    )(*args)


def attend_back_body(roles, diagonal, info_ref, q_ref, do_ref, lse_ref, delta_ref, *refs):
    kv_refs, (start_ref, dq_ref), dkv_refs = refs[:roles], refs[-roles - 2 : -roles], refs[-roles:]
    rows = q_ref.shape[0]
    seq_len = info_ref[0]
    if len(refs) > 2 * roles + 1:
        dq_ref[...] = start_ref[...]
    else:
        dq_ref[...] = jnp.zeros_like(dq_ref)
    key = lax.broadcasted_iota(jnp.int32, (rows, rows), 0)
    query = lax.broadcasted_iota(jnp.int32, (rows, rows), 1)
    lane = lax.broadcasted_iota(jnp.int32, (rows, 128), 1)
    low = lane < HEAD_DIM

    for role in range(roles):
        start, active = (info_ref[1 + 2 * role + i] for i in range(2))

        @pl.when(active == 0)
        def _(role=role):
            dkv_refs[role][...] = jnp.zeros_like(dkv_refs[role])

        @pl.when(active > 0)
        def _(role=role, start=start):
            keys = split_heads(kv_refs[role][0])
            values = split_heads(kv_refs[role][1])
            bad = key + start >= seq_len
            if diagonal and role == 0:
                bad = bad | (key > query)
            bias = jnp.where(bad, NEG, 0.0)
            dks, dvs = [], []
            for pair in range(2):
                q = q_ref[:, pair * 128 : pair * 128 + 128]
                do = do_ref[:, pair * 128 : pair * 128 + 128]
                scores = dot(keys[pair], q, 1, 1)
                grads = dot(values[pair], do, 1, 1)
                probs, raws = [], []
                for head in range(2):
                    at = 2 * pair + head
                    part = scores[head * rows : (head + 1) * rows] * LOG2E + bias
                    prob = jnp.exp2(part - lse_ref[0, at : at + 1, :])
                    grad = grads[head * rows : (head + 1) * rows]
                    raws.append((prob * (grad - delta_ref[0, at : at + 1, :])).astype(BF16))
                    probs.append(prob.astype(BF16))
                raw = jnp.concatenate(raws, 0)
                dq_ref[:, pair * 128 : pair * 128 + 128] += dot(raw, keys[pair], 0, 0)
                dks.append(dot(raw, q, 1, 0))
                dvs.append(dot(jnp.concatenate(probs, 0), do, 1, 0))
            for which, parts in enumerate((dks, dvs)):
                top_a, bottom_a = parts[0][:rows], parts[0][rows:]
                top_b, bottom_b = parts[1][:rows], parts[1][rows:]
                turn = pltpu.roll(jnp.where(low, top_b, bottom_a), HEAD_DIM, 1)
                whole = jnp.where(low, top_a, bottom_b) + turn
                dkv_refs[role][which] = whole.astype(dkv_refs[role].dtype)


def attend_back(info, q, do, lse, delta, blocks, before, diagonal):
    rows, width = q.shape
    steps = width // 256
    roles = len(blocks)
    kvw = blocks[0].shape[2]
    wide = pl.BlockSpec((rows, 256), lambda i, s: (0, i))
    heads = pl.BlockSpec((1, 8, rows), lambda i, s: (i, 0, 0))
    kv = pl.BlockSpec((2, rows, 128), lambda i, s: (0, 0, i))
    more = [] if before is None else [before]
    return pl.pallas_call(
        functools.partial(attend_back_body, roles, diagonal),
        grid_spec=pltpu.PrefetchScalarGridSpec(
            num_scalar_prefetch=1,
            grid=(steps,),
            in_specs=[wide, wide, heads, heads] + [kv] * roles + [wide] * len(more),
            out_specs=[wide] + [kv] * roles,
        ),
        out_shape=[jax.ShapeDtypeStruct((rows, width), F32)]
        + [jax.ShapeDtypeStruct((2, rows, kvw), BF16)] * roles,
        compiler_params=params(("arbitrary",)),
        cost_estimate=cost(40 * rows * rows * roles * width, 16 * 1024 * 1024),
        name="attend_back",
    )(info, q, do, lse, delta, *blocks, *more)


def expert_body(own, remotes, rows, low, half, first, carry, experts, info_ref, *refs):
    xa_hbm, xb_hbm, cot_hbm, wr_ref = refs[:4]
    near = refs[4 : 4 + (3 if own else 0)]
    at = 4 + len(near)
    far = refs[at : at + remotes]
    at += remotes
    before = refs[at] if carry else None
    outs = refs[-17 if first else -15 :]
    out_before = refs[at + 1] if carry else None
    gm_ref, gate_ref, out_ref, inner_ref, dg_ref, du_ref = outs[:6]
    copies = outs[6:8] if first else ()
    wbuf, sem, gm_acc, out_acc, gates, back, x_ref, cot_ref, row_sem = outs[-9:]
    step = pl.program_id(0)
    total = own + remotes
    width = x_ref.shape[1]
    shard_rows = 2 * half
    ff = width // 2
    slot = lax.rem(step, 2)
    offsets = (0, width, 2 * width, 2 * width + ff)
    sizes = (width, width, ff, ff)

    def fetch(target, where):
        def start(sources):
            for piece, (ref, off, size) in enumerate(zip(sources, offsets, sizes)):
                pltpu.make_async_copy(
                    ref, wbuf.at[where, pl.ds(off, size)], sem.at[where, piece]
                ).start()

        if own:

            @pl.when(target < own)
            def _():
                down = [near[2].at[target, :, pl.ds(k * ff, ff)] for k in range(2)]
                start([near[0].at[target], near[1].at[target]] + down)

        for i in range(remotes):

            @pl.when(target == own + i)
            def _(i=i):
                start([far[i].at[pl.ds(off, size)] for off, size in zip(offsets, sizes)])

    @pl.when(step == 0)
    def _():
        ext = shard_rows + experts
        block = pl.ds(pl.multiple_of(info_ref[0] * ext, 16), ext)
        cot_copy = pltpu.make_async_copy(cot_hbm.at[block], cot_ref, row_sem.at[0])

        @pl.when(info_ref[3] > 0)
        def _():
            pltpu.make_async_copy(xa_hbm, x_ref, row_sem.at[1]).start()

        @pl.when(info_ref[3] == 0)
        def _():
            pltpu.make_async_copy(xb_hbm, x_ref, row_sem.at[1]).start()

        cot_copy.start()
        fetch(jnp.int32(0), 0)
        pltpu.make_async_copy(xa_hbm, x_ref, row_sem.at[1]).wait()
        cot_copy.wait()

    @pl.when(step + 1 < total)
    def _():
        fetch(step + 1, lax.rem(step + 1, 2))

    lane = lax.broadcasted_iota(jnp.int32, (rows, 128), 1)

    @pl.when(step == 0)
    def _():
        logits = dot(x_ref[...], wr_ref[...], 1, 0)
        mask_t = cot_ref[pl.ds(shard_rows, experts), :shard_rows].astype(F32)
        mask_t = jnp.concatenate([mask_t, jnp.zeros((128 - experts, shard_rows), F32)], 0)
        mask = jnp.transpose(mask_t)[low : low + rows] > 0.5
        high = jnp.max(jnp.where(mask, logits, NEG), 1, keepdims=True)
        raised = jnp.where(mask, jnp.exp(logits - high), 0.0)
        gates[...] = raised / jnp.sum(raised, 1, keepdims=True)
        gate_ref[...] = gates[...]
        back[...] = jnp.zeros_like(back)
        gm_acc[...] = jnp.zeros_like(gm_acc)
        if carry:
            out_acc[...] = out_before[0].astype(F32)
        else:
            out_acc[...] = jnp.zeros_like(out_acc)
        if first:
            copies[0][0] = x_ref[...]
            copies[1][0] = cot_ref[pl.ds(low, rows), :]

    for piece, (off, size) in enumerate(zip(offsets, sizes)):
        place = wbuf.at[slot, pl.ds(off, size)]
        pltpu.make_async_copy(place, place, sem.at[slot, piece]).wait()

    wg = wbuf[slot, :width, :]
    wu = wbuf[slot, width : 2 * width, :]
    wd0 = wbuf[slot, 2 * width : 2 * width + ff, :]
    wd1 = wbuf[slot, 2 * width + ff :, :]
    which = info_ref[2] + info_ref[4 + step]
    x = x_ref[...]
    cot = cot_ref[pl.ds(low, rows), :]
    g = dot(x, wg, 1, 0)
    u = dot(x, wu, 1, 0)
    raw = dot(cot[:, :ff], wd0, 1, 1) + dot(cot[:, ff:], wd1, 1, 1)
    gate = jnp.sum(jnp.where(lane == which, gates[...], 0.0), 1, keepdims=True)
    sig = 1.0 / (1.0 + jnp.exp(-g))
    silu = g * sig
    inner = silu * u
    gg = jnp.sum(raw * inner, 1, keepdims=True)
    back[...] += jnp.where(lane == which, gg, 0.0)
    scaled = (gate * inner).astype(BF16)
    gi = gate * raw
    dg = (gi * u * (sig * (1.0 + g * (1.0 - sig)))).astype(BF16)
    du = (gi * silu).astype(BF16)
    inner_ref[0] = scaled
    dg_ref[0] = dg
    du_ref[0] = du
    out_acc[:, :ff] += dot(scaled, wd0, 1, 0)
    out_acc[:, ff:] += dot(scaled, wd1, 1, 0)
    gm_acc[...] += dot(dg, wg, 1, 1) + dot(du, wu, 1, 1)

    @pl.when(step == total - 1)
    def _():
        back_t = jnp.transpose(back[...])[:experts, :]
        for k in range(rows // half):
            body = gm_acc[k * half : (k + 1) * half, :]
            tail = back_t[:, k * half : (k + 1) * half]
            tail = jnp.concatenate([tail, jnp.zeros((experts, width - half), F32)], 1)
            if carry:
                body = body + before[k, :half, :].astype(F32)
                tail = tail + before[k, half:, :].astype(F32)
            gm_ref[k, :half, :] = body.astype(BF16)
            gm_ref[k, half:, :] = tail.astype(BF16)
        out_ref[0] = out_acc[...].astype(BF16)


def expert_call(info, xs, cot, wr, own_weights, far, experts, low, half, kept, before=None):
    rows, width = xs[0].shape
    shard_rows = 2 * half
    own = own_weights[0].shape[0] if own_weights else 0
    remotes = len(far)
    total = own + remotes
    carry = before is not None
    first = not carry
    ff = width // 2
    at = low // rows
    full = lambda shape: pl.BlockSpec(shape, lambda i, s: (0,) * len(shape))
    anywhere = pl.BlockSpec(memory_space=pl.ANY)
    big = pl.BlockSpec((1, rows, width), lambda i, s: (s[1], at, 0))
    part = pl.BlockSpec((1, rows, ff), lambda i, s: (s[1], at, s[4 + i]))
    count = 6 if first else 4
    fresh = isinstance(kept[0], jax.ShapeDtypeStruct)
    aliased = [] if fresh else list(kept[:count])
    inputs = [*xs, cot, wr, *own_weights, *far] + ([before] if carry else [])
    specs = [anywhere] * 3 + [full(wr.shape)]
    specs += [anywhere] * (len(own_weights) + remotes)
    specs += [full(before.shape)] if carry else []
    specs += [big if carry and k == 0 else anywhere for k in range(len(aliased))]
    gm_shape = (rows // half, half + experts, width)
    outs = pl.pallas_call(
        functools.partial(expert_body, own, remotes, rows, low, half, first, carry, experts),
        grid_spec=pltpu.PrefetchScalarGridSpec(
            num_scalar_prefetch=1,
            grid=(total,),
            in_specs=specs,
            out_specs=[full(gm_shape), full((rows, 128)), big, part, part, part]
            + ([big, big] if first else []),
            scratch_shapes=[
                pltpu.VMEM((2, 3 * width, ff), BF16),
                pltpu.SemaphoreType.DMA((2, 4)),
                pltpu.VMEM((rows, width), F32),
                pltpu.VMEM((rows, width), F32),
                pltpu.VMEM((rows, 128), F32),
                pltpu.VMEM((rows, 128), F32),
                pltpu.VMEM((rows, width), BF16),
                pltpu.VMEM((shard_rows + experts, width), BF16),
                pltpu.SemaphoreType.DMA((2,)),
            ],
        ),
        out_shape=[
            jax.ShapeDtypeStruct(gm_shape, BF16),
            jax.ShapeDtypeStruct((rows, 128), F32),
        ]
        + [jax.ShapeDtypeStruct(k.shape, k.dtype) for k in kept[:count]],
        input_output_aliases={1 + len(inputs) + k: 2 + k for k in range(len(aliased))},
        compiler_params=params(("arbitrary",)),
        cost_estimate=cost(12 * rows * width * ff * total, total * 6 * width * ff),
        name="experts",
    )(info, *inputs, *aliased)
    return outs[0], outs[1], tuple(outs[2:]) + tuple(kept[count:])


def expert_grads_body(info_ref, x_hbm, c_hbm, in_hbm, dg_hbm, du_hbm, o_ref, x, c, cols, sem):
    place, kind = pl.program_id(0), pl.program_id(1)
    step = place * 3 + kind
    ff = cols.shape[2]
    hidden = (dg_hbm, du_hbm, in_hbm)

    def fetch(target, start):
        at = lax.rem(target, 2)
        off = pl.ds(pl.multiple_of(info_ref[lax.div(target, 3)] * ff, 128), ff)
        for k, ref in enumerate(hidden):

            @pl.when(lax.rem(target, 3) == k)
            def _(ref=ref):
                pltpu.make_async_copy(ref.at[:, off], cols.at[at], sem.at[at]).start()

    @pl.when(step == 0)
    def _():
        pltpu.make_async_copy(x_hbm, x, sem.at[2]).start()
        fetch(step, True)
        pltpu.make_async_copy(c_hbm, c, sem.at[3]).start()
        pltpu.make_async_copy(x_hbm, x, sem.at[2]).wait()

    @pl.when(step + 1 < 3 * pl.num_programs(0))
    def _():
        fetch(step + 1, True)

    slot = lax.rem(step, 2)
    pltpu.make_async_copy(cols.at[slot], cols.at[slot], sem.at[slot]).wait()

    @pl.when(kind < 2)
    def _():
        o_ref[0, 0] = dot(x[...], cols[slot], 0, 0).astype(BF16)

    @pl.when(step == 2)
    def _():
        pltpu.make_async_copy(c_hbm, c, sem.at[3]).wait()

    @pl.when(kind == 2)
    def _():
        o_ref[0, 0, :ff] = dot(cols[slot], c[:, :ff], 0, 0).astype(BF16)
        o_ref[0, 0, ff:] = dot(cols[slot], c[:, ff:], 0, 0).astype(BF16)


def expert_grads(places, x, c, inner, dg, du):
    rows, width = x.shape
    ff = width // 2
    count = places.shape[0]
    anywhere = pl.BlockSpec(memory_space=pl.ANY)
    return pl.pallas_call(
        expert_grads_body,
        grid_spec=pltpu.PrefetchScalarGridSpec(
            num_scalar_prefetch=1,
            grid=(count, 3),
            in_specs=[anywhere] * 5,
            out_specs=pl.BlockSpec((1, 1, width, ff), lambda i, k, s: (i, k, 0, 0)),
            scratch_shapes=[
                pltpu.VMEM((rows, width), BF16),
                pltpu.VMEM((rows, width), BF16),
                pltpu.VMEM((2, rows, ff), BF16),
                pltpu.SemaphoreType.DMA((4,)),
            ],
        ),
        out_shape=jax.ShapeDtypeStruct((count, 3, width, ff), BF16),
        compiler_params=params(("arbitrary",) * 2),
        cost_estimate=cost(6 * rows * width * ff * count, 16 * 1024 * 1024),
        name="expert_grads",
    )(places, x, c, inner, dg, du)


def middle_body(experts, half, *refs):
    sums, refs = refs[:5], refs[5:]
    gate_ref, wr_ref, hid_ref, cot_ref, att_ref, mix_ref, gain_ref, wo_hbm = refs[:8]
    gh_ref, gb_ref, do_ref, delta_ref, ffn_ref, router_ref, wo, sem, deltas = refs[8:]
    step = pl.program_id(0)
    width = hid_ref.shape[1]

    @pl.when(step == 0)
    def _():
        pltpu.make_async_copy(wo_hbm, wo, sem).start()
        ffn_ref[...] = jnp.zeros_like(ffn_ref)
        router_ref[...] = jnp.zeros_like(router_ref)

    total = sums[0][0].astype(F32)
    for ref in sums[1:3]:
        total = total + ref[0].astype(F32)
    total = total + jnp.where(step == 0, sums[3][0].astype(F32), sums[4][0].astype(F32))
    wide = (half + 127) // 128 * 128
    gg = jnp.concatenate([total[half:, :wide], jnp.zeros((128 - experts, wide), F32)], 0)
    gg = jnp.transpose(gg)[:half]
    gates = gate_ref[...]
    gl = (gates * (gg - jnp.sum(gates * gg, 1, keepdims=True))).astype(BF16)
    router_ref[...] += dot(gl, mix_ref[...], 0, 0)
    hidden = hid_ref[...]
    grad_mixed = total[:half] + dot(gl, wr_ref[...], 1, 1)
    scale = lax.rsqrt(jnp.mean(hidden * hidden, -1, keepdims=True) + EPS)
    ffn_ref[...] += jnp.sum(grad_mixed * hidden * scale, 0, keepdims=True)
    weighted = grad_mixed * gain_ref[...]
    mean = jnp.mean(weighted * hidden, -1, keepdims=True)
    grad = cot_ref[...].astype(F32) + scale * weighted - hidden * (scale * scale * scale * mean)
    gh_ref[...] = grad
    low = grad.astype(BF16)
    gb_ref[...] = low

    @pl.when(step == 0)
    def _():
        pltpu.make_async_copy(wo_hbm, wo, sem).wait()

    do = dot(low, wo[...], 1, 1).astype(BF16)
    do_ref[...] = do
    both = do.astype(F32) * att_ref[...].astype(F32)
    lane = lax.broadcasted_iota(jnp.int32, (half, 128), 1)
    found = jnp.zeros((half, 128), F32)
    for block in range(both.shape[1] // 128):
        pair = both[:, block * 128 : block * 128 + 128]
        front = jnp.sum(jnp.where(lane < HEAD_DIM, pair, 0.0), 1, keepdims=True)
        back = jnp.sum(jnp.where(lane < HEAD_DIM, 0.0, pair), 1, keepdims=True)
        found = jnp.where(lane == 2 * block, front, found)
        found = jnp.where(lane == 2 * block + 1, back, found)
    deltas[pl.ds(pl.multiple_of(step * half, half), half), :] = found

    @pl.when(step == pl.num_programs(0) - 1)
    def _():
        turned = jnp.transpose(deltas[...])
        for group in range(delta_ref.shape[0]):
            delta_ref[group, :4, :] = turned[4 * group : 4 * group + 4]
            delta_ref[group, 4:, :] = jnp.zeros((4, turned.shape[1]), F32)


def middle(sums, gates, wr, hidden, cot_ext, attended, mixed, gain, wo, experts):
    rows, width = hidden.shape
    half = rows // 2
    ext = half + experts
    heads = attended.shape[1] // HEAD_DIM
    stacked = pl.BlockSpec((1, ext, width), lambda i: (i, 0, 0))
    alone = pl.BlockSpec((1, ext, width), lambda i: (0, 0, 0))
    row = lambda w: pl.BlockSpec((half, w), lambda i: (i, 0))
    full = lambda shape: pl.BlockSpec(shape, lambda i: (0,) * len(shape))
    return pl.pallas_call(
        functools.partial(middle_body, experts, half),
        grid=(2,),
        in_specs=[stacked] * 3
        + [alone] * 2
        + [
            row(128),
            full(wr.shape),
            row(width),
            row(width),
            row(attended.shape[1]),
            row(width),
            full((1, width)),
            pl.BlockSpec(memory_space=pl.ANY),
        ],
        out_specs=[
            row(width),
            row(width),
            row(attended.shape[1]),
            full((heads // 4, 8, rows)),
            full((1, width)),
            full((128, width)),
        ],
        out_shape=[
            jax.ShapeDtypeStruct((rows, width), F32),
            jax.ShapeDtypeStruct((rows, width), BF16),
            jax.ShapeDtypeStruct(attended.shape, BF16),
            jax.ShapeDtypeStruct((heads // 4, 8, rows), F32),
            jax.ShapeDtypeStruct((1, width), F32),
            jax.ShapeDtypeStruct((128, width), F32),
        ],
        scratch_shapes=[
            pltpu.VMEM(wo.shape, BF16),
            pltpu.SemaphoreType.DMA(()),
            pltpu.VMEM((rows, 128), F32),
        ],
        compiler_params=params(("arbitrary",)),
        cost_estimate=COST,
        name="middle",
    )(*sums, gates, wr, hidden, cot_ext, attended, mixed, gain, wo)


def early_body(experts, info_ref, att_ref, gb_ref, router_ref, ffn_ref, give_ref, keep_ref):
    size = att_ref.shape[1] // 2
    core = info_ref[0]
    width = gb_ref.shape[1]
    row = lax.broadcasted_iota(jnp.int32, (16, width), 0)
    extra = jnp.concatenate([router_ref[:experts], jnp.where(row == 0, ffn_ref[...], 0.0)], 0)
    for ref, half in ((keep_ref, core), (give_ref, 1 - core)):
        part = att_ref[:, pl.ds(pl.multiple_of(half * size, 128), size)]
        ref[:size] = dot(part, gb_ref[...], 0, 0).astype(BF16)
        ref[size : size + experts + 16] = jnp.where(half == 0, extra, 0.0).astype(BF16)
        rest = ref.shape[0] - (size + experts + 16)
        ref[size + experts + 16 :] = jnp.zeros((rest, width), BF16)


def early_grads(info, attended, gb, router, ffn, experts):
    rows, width = gb.shape
    count = attended.shape[1]
    col = lambda r: pl.BlockSpec((r, 256), lambda i, s: (0, i))
    size = count // 2 + count // 8
    return pl.pallas_call(
        functools.partial(early_body, experts),
        grid_spec=pltpu.PrefetchScalarGridSpec(
            num_scalar_prefetch=1,
            grid=(width // 256,),
            in_specs=[
                pl.BlockSpec(attended.shape, lambda i, s: (0, 0)),
                col(rows),
                col(router.shape[0]),
                col(1),
            ],
            out_specs=[col(size)] * 2,
        ),
        out_shape=[jax.ShapeDtypeStruct((size, width), BF16)] * 2,
        compiler_params=params(("arbitrary",)),
        cost_estimate=COST,
        name="early_grads",
    )(info, attended, gb, router, ffn)


def rope_back(g, cos_ref, sin_ref):
    cos = jnp.concatenate([cos_ref[...]] * (g.shape[1] // 128), 1)
    sin = jnp.concatenate([sin_ref[...]] * (g.shape[1] // 128), 1)
    return g * cos - swap_halves(g, lambda v, s: pltpu.roll(v, s, 1)) * sin


def split_rows(core, n_ref, lin, give_ref, keep_ref):
    size = n_ref.shape[1] // 2
    for ref, half in ((give_ref, 1 - core), (keep_ref, core)):
        part = n_ref[:, pl.ds(pl.multiple_of(half * size, 128), size)]
        ref[...] = dot(part, lin, 0, 0).astype(BF16)


def query_back_body(info_ref, dq_ref, n_ref, cos_ref, sin_ref, lin_ref, give_ref, keep_ref):
    lin = rope_back(dq_ref[...] * HEAD_DIM**-0.5, cos_ref, sin_ref).astype(BF16)
    lin_ref[...] = lin
    split_rows(info_ref[0], n_ref, lin, give_ref, keep_ref)


def query_back(info, dq, normed, cos, sin):
    rows, width = dq.shape
    col = lambda r: pl.BlockSpec((r, 256), lambda i, s: (0, i))
    full = lambda shape: pl.BlockSpec(shape, lambda i, s: (0, 0))
    size = normed.shape[1] // 2
    return pl.pallas_call(
        query_back_body,
        grid_spec=pltpu.PrefetchScalarGridSpec(
            num_scalar_prefetch=1,
            grid=(width // 256,),
            in_specs=[col(rows), full(normed.shape), full(cos.shape), full(sin.shape)],
            out_specs=[col(rows), col(size), col(size)],
        ),
        out_shape=[
            jax.ShapeDtypeStruct((rows, width), BF16),
            jax.ShapeDtypeStruct((size, width), BF16),
            jax.ShapeDtypeStruct((size, width), BF16),
        ],
        compiler_params=params(("arbitrary",)),
        cost_estimate=cost(2 * rows * width * width, 8 * 1024 * 1024),
        name="query_back",
    )(info, dq, normed, cos, sin)


def pair_back_body(parts, half_steps, info_ref, *refs):
    n_ref, cos_ref, sin_ref, lin_ref, give_ref, keep_ref = refs[parts:]
    step = pl.program_id(0)
    total = refs[0][0].astype(F32)
    for ref in refs[1:parts]:
        total = total + ref[0].astype(F32)

    @pl.when(step < half_steps)
    def _():
        lin_ref[...] = rope_back(total, cos_ref, sin_ref).astype(BF16)

    @pl.when(step >= half_steps)
    def _():
        lin_ref[...] = total.astype(BF16)

    split_rows(info_ref[0], n_ref, lin_ref[...], give_ref, keep_ref)


def pair_back(info, parts, normed, cos, sin):
    _, rows, kvw = parts[0].shape
    half_steps = kvw // 256
    col = lambda r: pl.BlockSpec((r, 256), lambda i, s: (0, i))
    full = lambda shape: pl.BlockSpec(shape, lambda i, s: (0, 0))
    part = pl.BlockSpec((1, rows, 256), lambda i, s: (i // half_steps, 0, i % half_steps))
    size = normed.shape[1] // 2
    return pl.pallas_call(
        functools.partial(pair_back_body, len(parts), half_steps),
        grid_spec=pltpu.PrefetchScalarGridSpec(
            num_scalar_prefetch=1,
            grid=(2 * half_steps,),
            in_specs=[part] * len(parts) + [full(normed.shape), full(cos.shape), full(sin.shape)],
            out_specs=[col(rows), col(size), col(size)],
        ),
        out_shape=[
            jax.ShapeDtypeStruct((rows, 2 * kvw), BF16),
            jax.ShapeDtypeStruct((size, 2 * kvw), BF16),
            jax.ShapeDtypeStruct((size, 2 * kvw), BF16),
        ],
        compiler_params=params(("arbitrary",)),
        cost_estimate=COST,
        name="pair_back",
    )(info, *parts, normed, cos, sin)


def tokens_back_body(lq_ref, lkv_ref, wq_ref, wk_ref, wv_ref, x_ref, gh_ref, gain_ref, o_ref):
    kvw = wk_ref.shape[1]
    grad = dot(lq_ref[...], wq_ref[...], 1, 1)
    grad = grad + dot(lkv_ref[:, :kvw], wk_ref[...], 1, 1)
    grad = grad + dot(lkv_ref[:, kvw:], wv_ref[...], 1, 1)
    x = x_ref[...].astype(F32)
    scale = lax.rsqrt(jnp.mean(x * x, -1, keepdims=True) + EPS)
    weighted = grad * gain_ref[...]
    mean = jnp.mean(weighted * x, -1, keepdims=True)
    total = gh_ref[...] + scale * weighted - x * (scale * scale * scale * mean)
    o_ref[...] = total.astype(BF16)


def tokens_back(lq, lkv, wq, wk, wv, x, gh, gain):
    rows, width = x.shape
    row = lambda w: pl.BlockSpec((rows // 4, w), lambda i: (i, 0))
    full = lambda shape: pl.BlockSpec(shape, lambda i: (0, 0))
    return pl.pallas_call(
        tokens_back_body,
        grid=(4,),
        in_specs=[
            row(lq.shape[1]),
            row(lkv.shape[1]),
            full(wq.shape),
            full(wk.shape),
            full(wv.shape),
            row(width),
            row(width),
            full((1, width)),
        ],
        out_specs=row(width),
        out_shape=jax.ShapeDtypeStruct((rows, width), BF16),
        compiler_params=params(("arbitrary",)),
        cost_estimate=COST,
        name="tokens_back",
    )(lq, lkv, wq, wk, wv, x, gh, gain)


def total_of(parts):
    total = parts[0].astype(F32)
    for part in parts[1:]:
        total = total + part.astype(F32)
    return total.astype(BF16)


def scatter_sum(buf, axis):
    name, size, pos, pairs = axis
    rows = buf.shape[0] // size
    take = lambda k: lax.dynamic_slice_in_dim(buf, k * rows, rows, 0)
    parts = [take(pos)]
    for shift in range(1, size):
        parts.append(lax.ppermute(take((pos + shift) % size), name, pairs(shift)))
    return total_of(parts)


def gather_rows(buf, axis):
    name, size, pos, pairs = axis
    rows = buf.shape[0]
    came = [lax.ppermute(buf, name, pairs(shift)) for shift in range(size - 1, 0, -1)]
    if size == 2:
        pick = lambda a, b: jnp.concatenate([a, b], 0)
        return jnp.where(pos == 0, pick(buf, came[0]), pick(came[0], buf))
    order = came + [buf]
    double = jnp.concatenate(order + order[:-1], 0)
    return lax.dynamic_slice_in_dim(double, (size - 1 - pos) * rows, size * rows, 0)


def local(
    tokens,
    lengths,
    routes,
    cotangent,
    attn_norm,
    w_query,
    w_key,
    w_value,
    w_out,
    ffn_norm,
    w_router,
    expert_gate_weight,
    expert_up_weight,
    expert_down_weight,
):
    rows, width = tokens.shape[1:]
    half = rows // 2
    experts = w_router.shape[1]
    own = expert_gate_weight.shape[0]
    ff = expert_gate_weight.shape[2]
    kvw = w_key.shape[1]
    ctx_size, ep_size = lax.axis_size("ctx"), lax.axis_size("ep")
    ny, nx = ctx_size // CORES, ep_size // NZ
    ctx_index, ep_index = lax.axis_index("ctx"), lax.axis_index("ep")
    y, core = ctx_index // CORES, ctx_index % CORES
    z, xpos = ep_index // nx, ep_index % nx
    seq_len = lengths[0]
    tokens = tokens[0]
    valid_flag = ctx_index * rows + jnp.arange(rows, dtype=jnp.int32) < seq_len
    valid = valid_flag.astype(F32)[:, None]
    tie = lax.optimization_barrier
    ints = lambda values: jnp.stack([jnp.asarray(v, jnp.int32) for v in values])

    core_swap = [(c, c ^ 1) for c in range(ctx_size)]
    core_up = [(c, c + 1) for c in range(0, ctx_size, CORES)]
    core_down = [(c + 1, c) for c in range(0, ctx_size, CORES)]
    y_up = lambda k: [(c, c + CORES * k) for c in range(ctx_size - CORES * k)]
    y_down = lambda k: [(b, a) for a, b in y_up(k)]
    zx = lambda pairs: [(a * nx + i, b * nx + i) for a, b in pairs for i in range(nx)]
    z_groups = [[i + nx * k for k in range(NZ)] for i in range(nx)]
    x_shift = lambda s: [(k * nx + i, k * nx + (i + s) % nx) for k in range(NZ) for i in range(nx)]
    y_ring = lambda s: [(c, (c + CORES * s) % ctx_size) for c in range(ctx_size)]
    core_axis = ("ctx", CORES, core, lambda s: core_swap)
    y_axis = ("ctx", ny, y, y_ring)
    x_axis = ("ep", nx, xpos, x_shift)
    z_axis = ("ep", NZ, z, lambda s: zx([(k, (k + s) % NZ) for k in range(NZ)]))

    weights = (expert_gate_weight, expert_up_weight, expert_down_weight)
    count = jnp.clip(seq_len - ctx_index * rows, 0, rows)
    cot_ext, sent = prepare(ints([core, count]), routes[0], cotangent[0], weights, experts)
    cot_all = lax.all_gather(cot_ext, "ep", axis_index_groups=z_groups, tiled=True)
    arrived, far_places = [], []
    for shift in range(1, nx):
        arrived.append(lax.ppermute(sent, "ep", x_shift(shift)))
        origin = (xpos - shift) % nx * own
        far_places += [origin + core, origin + 1 - core]
    own_places = [xpos * own + i for i in range(own)]

    tokens, cot_ext, sent = tie((tokens, cot_ext, sent))
    fine, starts = rope_constants(ctx_size, rows)
    normed, q, kv, cos, sin = project(
        ints([ctx_index]), tokens, attn_norm[None], w_query, w_key, w_value, fine, starts, ctx_size
    )

    blocks = [kv, lax.ppermute(kv, "ctx", core_up)]
    facts = [(ctx_index * rows, True), ((ctx_index - 1) * rows, core == 1)]
    travelling = kv
    for back in range(1, ny):
        travelling = lax.ppermute(travelling, "ctx", y_up(1))
        blocks.append(travelling)
        base = (y - back) * CORES
        facts += [((base + core) * rows, y >= back), ((base + 1 - core) * rows, y >= back)]
    facts = [[start, (jnp.asarray(reach) & (start < seq_len))] for start, reach in facts]
    info_of = lambda part: ints([seq_len] + sum(part, []))
    state = attend(info_of(facts[:2]), q, blocks[:2], None)
    came = tie((*blocks[2:], *state))
    came, state = came[: ny - 1], came[ny - 1 :]
    blocks = blocks[:2]
    for piece in came:
        blocks += [piece, lax.ppermute(piece, "ctx", core_swap)]
    attended, lse, hidden, mixed = attend(
        info_of(facts[2:]), q, blocks[2:], state, w_out, tokens, ffn_norm[None]
    )

    wr = jnp.pad(w_router, ((0, 0), (0, 128 - experts)))
    group = nx * own
    widths = (width, group * ff, group * ff, group * ff, width, width)
    kept = tuple(jax.ShapeDtypeStruct((NZ, rows, w), BF16) for w in widths)

    def run(data, pick, cot, block, shard, near, far, low, kept, before=None):
        places = (own_places if near else []) + (far_places if far else [])
        facts = ints([block, shard, z * group, pick] + places)
        return expert_call(facts, data, cot, wr, near, far, experts, low, half, kept, before)

    shard_b, shard_c, shard_d = z ^ 1, jnp.where(z < 2, 2, 1), jnp.where(z < 2, 3, 0)
    inside = (z == 1) | (z == 2)
    swap, mid, out = [(0, 1), (1, 0), (2, 3), (3, 2)], [(1, 2), (2, 1)], [(1, 0), (2, 3)]
    halves = lambda a: [a[:half], a[half:]]
    near = lax.ppermute(mixed, "ep", zx(swap))
    middle_rows = lax.ppermute(mixed, "ep", zx(mid))
    gm_a, gates, kept = run((mixed, mixed), 1, cot_ext, 0, z, weights, [], 0, kept)
    near, middle_rows, arrived, kept = tie((near, middle_rows, arrived, kept))
    across = [lax.ppermute(part, "ep", zx(mid)) for part in halves(near)]
    outward = lax.ppermute(middle_rows, "ep", zx(out))
    far = []
    for piece in arrived:
        far += [piece, lax.ppermute(piece, "ctx", core_swap)]
    gm_a, _, kept = run((mixed, mixed), 1, cot_all, z, z, (), far, 0, kept, gm_a)
    across, outward, kept = tie((across, outward, kept))
    last = [lax.ppermute(part, "ep", zx(out)) for part in across]
    gm_b, _, kept = run((near, near), 1, cot_all, shard_b, shard_b, weights, far, 0, kept)
    ends, away = [(0, 1), (3, 2)], [(2, 3), (1, 0)]
    third = lax.ppermute(gm_b, "ep", zx(ends))
    last, kept = tie((last, kept))
    gm_c, _, kept = run(
        (middle_rows, outward), inside, cot_all, shard_c, shard_c, weights, far, 0, kept
    )
    second = lax.ppermute(gm_c, "ep", zx(ends))
    third, kept = tie((third, kept))
    gm_d0, _, kept = run(
        (across[0], last[0]), inside, cot_all, shard_d, shard_d, weights, far, 0, kept
    )
    first = [lax.ppermute(gm_d0, "ep", zx(ends))]
    second, kept = tie((second, kept))
    gm_d1, _, kept = run(
        (across[1], last[1]), inside, cot_all, shard_d, shard_d, weights, far, half, kept
    )
    first.append(lax.ppermute(gm_d1, "ep", zx(ends)))

    add = lambda a, b: (a.astype(F32) + b.astype(F32)).astype(BF16)
    first[0], kept = tie((first[0], kept))
    carried = [lax.ppermute(add(gm_d0, first[0]), "ep", zx(mid))]
    turned = lax.ppermute(add(gm_c, second), "ep", zx(mid))
    line = lambda a: a.reshape(NZ * rows, a.shape[2])
    turn = lambda i: ints([(xpos + j) % nx * own + i for j in range(nx)])
    saved = lambda kept: [line(kept[k]) for k in (4, 5, 1, 2, 3)]
    give = expert_grads(turn(1 - core), *saved(kept))
    first[1], carried[0], give, kept = tie((first[1], carried[0], give, kept))
    carried.append(lax.ppermute(add(gm_d1, first[1]), "ep", zx(mid)))
    final = [lax.ppermute(add(gm_b[:1], carried[0]), "ep", zx(away))]
    came = lax.ppermute(give, "ctx", core_swap)
    keep = expert_grads(turn(core), *saved(kept))
    carried[1], final[0], keep, came = tie((carried[1], final[0], keep, came))
    final.append(lax.ppermute(add(gm_b[1:], carried[1]), "ep", zx(away)))
    size = 3 * width // 2
    kept_p = [add(keep[j], came[j]).reshape(3 * width, ff)[:size] for j in range(nx)]
    kept_q = [add(keep[j], came[j]).reshape(3 * width, ff)[size:] for j in range(nx)]
    final, kept_p, kept_q = tie((final, kept_p, kept_q))
    sum_p = [lax.ppermute(kept_p[s], "ep", x_shift(s)) for s in range(1, nx)]
    rows_q = size // ny
    take_q = lambda s: jnp.concatenate(
        [lax.dynamic_slice_in_dim(k, (y + s) % ny * rows_q, rows_q, 0) for k in kept_q], 0
    )
    sum_q = [lax.ppermute(take_q(s), "ctx", y_ring(s)) for s in range(1, ny)]

    sums = [gm_a, third, turned, *final]
    gh, gb, do, delta, grad_ffn, grad_router = middle(
        sums, gates, wr, hidden, cot_ext, attended, mixed, ffn_norm[None], w_out, experts
    )
    which = ints([core])
    give, keep = early_grads(which, attended, gb, grad_router, grad_ffn, experts)
    give, keep, do = tie((give, keep, do))
    out_all = kept[0]
    out_all, do = tie((out_all, do))
    expert_sum = lax.psum_scatter(
        line(out_all), "ep", scatter_dimension=0, axis_index_groups=z_groups, tiled=True
    )

    came = lax.ppermute(give, "ctx", core_swap)
    dq = None
    homeward = []
    if ny > 1:
        far_info = info_of(facts[2:])
        dq, *far_dkv = attend_back(far_info, q, do, lse, delta, blocks[2:], None, False)
        for back in range(1, ny):
            same, other = far_dkv[2 * back - 2], far_dkv[2 * back - 1]
            homeward.append(add(same, lax.ppermute(other, "ctx", core_swap)))
    homeward, dq, came, sum_p, sum_q = tie((homeward, dq, came, sum_p, sum_q))
    homeward = [lax.ppermute(h, "ctx", y_down(k + 1)) for k, h in enumerate(homeward)]
    early = add(keep, came)
    part = early.shape[0] // 2
    early = [scatter_sum(early[:part], y_axis), scatter_sum(early[part:], x_axis)]
    half_q = total_of([take_q(0)] + sum_q)
    send_q = [half_q[s * rows_q : (s + 1) * rows_q] for s in range(nx)]
    sum_q = [lax.ppermute(send_q[s], "ep", x_shift(s)) for s in range(1, nx)]
    dq, *near_dkv = attend_back(info_of(facts[:2]), q, do, lse, delta, blocks[:2], dq, True)
    early, dq, homeward, sum_q, near_dkv = tie((early, dq, homeward, sum_q, near_dkv))
    parts = [near_dkv[0], lax.ppermute(near_dkv[1], "ctx", core_down), *homeward]
    early = [scatter_sum(early[0], x_axis), scatter_sum(early[1], y_axis)]
    sum_p = scatter_sum(total_of([kept_p[0]] + sum_p), y_axis)
    sum_q = total_of([send_q[0]] + sum_q)

    lin_q, give, keep = query_back(which, dq, normed, cos, sin)
    half_q = [keep, lax.ppermute(give, "ctx", core_swap)]
    parts, lin_q = tie((parts, lin_q))
    lin_kv, give, keep = pair_back(which, parts, normed, cos, sin)
    half_kv = [keep, lax.ppermute(give, "ctx", core_swap)]
    half_q, half_kv, early, sum_p, sum_q = tie((half_q, half_kv, early, sum_p, sum_q))
    one, two = scatter_sum(add(*half_q), y_axis), scatter_sum(add(*half_kv), x_axis)
    grad_tokens = tokens_back(
        lin_q, lin_kv, w_query, w_key, w_value, tokens, gh, attn_norm[None]
    )
    one, two, grad_tokens = tie((one, two, grad_tokens))
    one, two = scatter_sum(one, x_axis), scatter_sum(two, y_axis)
    one, two = tie((one, two))
    grads = jnp.concatenate([sum_p, sum_q], 0)
    grads = gather_rows(grads, y_axis)
    both = jnp.concatenate([one, early[0], two, early[1]], 0)
    both = gather_rows(scatter_sum(both, z_axis), z_axis)
    both, grads, expert_sum = tie((both, grads, expert_sum))
    result_out = (valid * (hidden + expert_sum.astype(F32))).astype(BF16)
    size = both.shape[0] // 2
    one, two = gather_rows(both[:size], x_axis), gather_rows(both[size:], y_axis)
    grads = gather_rows(grads.reshape(ny, 2 * rows_q, ff), core_axis)
    grads = grads.reshape(own, ny, 2, rows_q, ff).transpose(0, 2, 1, 3, 4).reshape(own, 3, width, ff)
    down = jnp.concatenate([grads[:, 2, :ff], grads[:, 2, ff:]], -1)
    expert_out = tuple(g.astype(F32) for g in (grads[:, 0], grads[:, 1], down))
    one, two, result_out, expert_out = tie((one, two, result_out, expert_out))
    one, two = gather_rows(one, y_axis), gather_rows(two, x_axis)

    wide = width // (CORES * ny * nx)
    late = gather_rows(jnp.concatenate([one, two], 0), core_axis)
    late = late.reshape(CORES, 2, ny * nx, size, width)
    late_q = late[:, 0, :, :wide].reshape(width, width).astype(F32)
    late_kv = late[:, 1, :, :wide].reshape(width, width).astype(F32)
    late_k, late_v = late_kv[:, :kvw], late_kv[:, kvw:]
    late_out = late[:, :, :, wide:].reshape(CORES, -1, width)
    w_out_sum = late_out[:, : width // 2].reshape(width, width).astype(F32)
    small = late_out[0, width // 2 :].astype(F32)
    paired = lambda w, g: jnp.sum(w.astype(F32) * g, 1)
    grad_attn_norm = paired(w_query, late_q) + paired(w_key, late_k) + paired(w_value, late_v)
    return (
        result_out[None],
        grad_tokens[None],
        grad_attn_norm / attn_norm,
        late_q,
        late_k,
        late_v,
        w_out_sum,
        small[experts],
        small[:experts].T,
        *expert_out,
    )


def solution(mesh):
    rows, whole, split = P("ep", "ctx", None), P(), P("ep", None, None)
    return jax.shard_map(
        local,
        mesh=mesh,
        in_specs=(rows, P("ep"), rows, rows) + (whole,) * 7 + (split,) * 3,
        out_specs=(rows, rows) + (whole,) * 7 + (split,) * 3,
        check_vma=False,
    )
```

```python
import functools

import jax
import jax.numpy as jnp
import numpy as np
from jax import lax
from jax.experimental import pallas as pl
from jax.experimental.pallas import tpu as pltpu
from jax.sharding import PartitionSpec as P

HEAD_DIM = 64
EPS = 1e-06
THETA = 10000.0
NEG = -1e30
LOG2E = 1.4426950408889634
NZ = 4
VMEM = 58 * 1024 * 1024
CORES = 2
F32 = jnp.float32
BF16 = jnp.bfloat16


def dot(a, b, ca, cb):
    return lax.dot_general(a, b, (((ca,), (cb,)), ((), ())), preferred_element_type=F32)


def params(semantics):
    return pltpu.CompilerParams(dimension_semantics=semantics, vmem_limit_bytes=VMEM)


COST = pl.CostEstimate(flops=1 << 20, bytes_accessed=1 << 20, transcendentals=0)


def cost(flops, nbytes):
    return pl.CostEstimate(flops=flops, bytes_accessed=nbytes, transcendentals=0)


def rope_constants(ctx_size, rows):
    half = HEAD_DIM // 2
    inv = THETA ** (-np.arange(half, dtype=np.float64) / half)
    fine = np.arange(rows, dtype=np.float64)[:, None] * inv[None, :]
    coarse = (rows * np.arange(ctx_size, dtype=np.float64))[:, None] * inv[None, :]
    tile = lambda t: jnp.asarray(np.tile(t, (1, 128 // half)).astype(np.float32))
    pad = np.zeros(((-2 * ctx_size) % 8, half))
    return (
        tile(np.concatenate([np.cos(fine), np.sin(fine)], 0)),
        tile(np.concatenate([np.cos(coarse), np.sin(coarse), pad], 0)),
    )


def swap_halves(x, roll):
    half = HEAD_DIM // 2
    width = x.shape[1]
    lane = lax.broadcasted_iota(jnp.int32, x.shape, 1)
    return jnp.where(lane % HEAD_DIM < half, roll(x, width - half), roll(x, half))


def prepare_body(experts, info_ref, len_ref, r_ref, c_ref, wg, wu, wd, ext_ref, sent_ref, buf, sem):
    rows, width = c_ref.shape
    ff = width // 2
    core = info_ref[0]
    count = len_ref[0] - info_ref[1] * rows
    pieces = [wg.at[core], wu.at[core]] + [wd.at[core, :, pl.ds(k * ff, ff)] for k in range(2)]
    spans = [pl.ds(0, width), pl.ds(width, width), pl.ds(2 * width, ff), pl.ds(2 * width + ff, ff)]
    into = [
        pltpu.make_async_copy(piece, buf.at[span], sem.at[0, k])
        for k, (piece, span) in enumerate(zip(pieces, spans))
    ]
    back = [
        pltpu.make_async_copy(buf.at[span], sent_ref.at[span], sem.at[1, k])
        for k, span in enumerate(spans)
    ]
    for copy in into:
        copy.start()
    row = lax.broadcasted_iota(jnp.int32, (rows, width), 0)
    ext_ref[:rows] = jnp.where(row < count, c_ref[...], jnp.zeros((), BF16))
    expert = lax.broadcasted_iota(jnp.int32, (experts, rows), 0)
    named = jnp.zeros((experts, rows), F32)
    for k in range(r_ref.shape[0]):
        named = jnp.where(expert == r_ref[k : k + 1, :], 1.0, named)
    ext_ref[rows:] = jnp.concatenate(
        [named, jnp.zeros((experts, width - rows), F32)], 1
    ).astype(BF16)
    for k in range(4):
        into[k].wait()
        back[k].start()
    for copy in back:
        copy.wait()


def prepare(facts, routes, cot, weights, experts):
    rows, width = cot.shape
    ff = width // 2
    anywhere = pl.BlockSpec(memory_space=pl.ANY)
    full = lambda shape: pl.BlockSpec(shape, lambda i, *s: (0, 0))
    return pl.pallas_call(
        functools.partial(prepare_body, experts),
        grid_spec=pltpu.PrefetchScalarGridSpec(
            num_scalar_prefetch=2,
            grid=(1,),
            in_specs=[full(routes.shape), full(cot.shape)] + [anywhere] * 3,
            out_specs=[full((rows + experts, width)), anywhere],
            scratch_shapes=[
                pltpu.VMEM((3 * width, ff), BF16),
                pltpu.SemaphoreType.DMA((2, 4)),
            ],
        ),
        out_shape=[
            jax.ShapeDtypeStruct((rows + experts, width), BF16),
            jax.ShapeDtypeStruct((3 * width, ff), BF16),
        ],
        compiler_params=params(("arbitrary",)),
        cost_estimate=COST,
        name="prepare",
    )(*facts, routes, cot, *weights)


def project_body(blocks, info_ref, len_ref, x_ref, gain_ref, wq_ref, wk_ref, wv_ref, fine_ref, start_ref,
                 n_ref, q_ref, kv_ref, cos_ref, sin_ref):
    step = pl.program_id(0)
    wide = q_ref.shape[1]
    nq = pl.num_programs(0) - 2
    rows = x_ref.shape[0]

    @pl.when(step == 0)
    def _():
        x = x_ref[...].astype(F32)
        scale = lax.rsqrt(jnp.mean(x * x, -1, keepdims=True) + EPS)
        n_ref[...] = (x * scale * gain_ref[...]).astype(BF16)
        cos_f, sin_f = fine_ref[:rows], fine_ref[rows:]
        cos_c = start_ref[pl.ds(info_ref[1], 1), :]
        sin_c = start_ref[pl.ds(info_ref[1] + blocks, 1), :]
        lane = lax.broadcasted_iota(jnp.int32, (rows, 128), 1)
        sign = jnp.where(lane % HEAD_DIM < HEAD_DIM // 2, -1.0, 1.0)
        cos_ref[...] = cos_f * cos_c - sin_f * sin_c
        sin_ref[...] = (sin_f * cos_c + cos_f * sin_c) * sign

    def rope(lin):
        cos = jnp.concatenate([cos_ref[...]] * (wide // 128), 1)
        sin = jnp.concatenate([sin_ref[...]] * (wide // 128), 1)
        return lin * cos + swap_halves(lin, lambda v, s: pltpu.roll(v, s, 1)) * sin

    @pl.when(step < nq)
    def _():
        lin = dot(n_ref[...], wq_ref[...], 1, 0)
        q_ref[...] = rope(lin).astype(BF16) * jnp.asarray(HEAD_DIM**-0.5, BF16)

    @pl.when(step == nq)
    def _():
        kv_ref[...] = rope(dot(n_ref[...], wk_ref[...], 1, 0)).astype(BF16)[None]

    @pl.when(step == nq + 1)
    def _():
        kv_ref[...] = dot(n_ref[...], wv_ref[...], 1, 0).astype(BF16)[None]


def project(facts, x, gain, wq, wk, wv, fine, starts, blocks):
    rows, width = x.shape
    kvw = wk.shape[1]
    nq = wq.shape[1] // kvw
    clip = lambda v, hi: jnp.minimum(jnp.maximum(v, 0), hi)
    full = lambda shape: pl.BlockSpec(shape, lambda i, *s: (0, 0))
    return pl.pallas_call(
        functools.partial(project_body, blocks),
        grid_spec=pltpu.PrefetchScalarGridSpec(
            num_scalar_prefetch=2,
            grid=(nq + 2,),
            in_specs=[
                full((rows, width)),
                full((1, width)),
                pl.BlockSpec((width, kvw), lambda i, *s: (0, clip(i, nq - 1))),
                full((width, kvw)),
                full((width, kvw)),
                full(fine.shape),
                full(starts.shape),
            ],
            out_specs=[
                full((rows, width)),
                pl.BlockSpec((rows, kvw), lambda i, *s: (0, clip(i, nq - 1))),
                pl.BlockSpec((1, rows, kvw), lambda i, *s: (clip(i - nq, 1), 0, 0)),
                full((rows, 128)),
                full((rows, 128)),
            ],
        ),
        out_shape=[
            jax.ShapeDtypeStruct((rows, width), BF16),
            jax.ShapeDtypeStruct((rows, wq.shape[1]), BF16),
            jax.ShapeDtypeStruct((2, rows, kvw), BF16),
            jax.ShapeDtypeStruct((rows, 128), F32),
            jax.ShapeDtypeStruct((rows, 128), F32),
        ],
        compiler_params=params(("arbitrary",)),
        cost_estimate=COST,
        name="project",
    )(*facts, x, gain, wq, wk, wv, fine, starts)


def split_heads(block):
    lane = lax.broadcasted_iota(jnp.int32, block.shape, 1)
    low = lane < HEAD_DIM
    zero = jnp.zeros_like(block)
    turned = jnp.concatenate([block[:, HEAD_DIM:], block[:, :HEAD_DIM]], 1)
    first = jnp.concatenate([jnp.where(low, block, zero), jnp.where(low, zero, turned)], 0)
    second = jnp.concatenate([jnp.where(low, turned, zero), jnp.where(low, zero, block)], 0)
    return first, second


def attend_blocks(info_ref, len_ref, base, q_ref, kv_refs, acc, top, low, diagonal):
    rows = q_ref.shape[0]
    seq_len = len_ref[0]
    key = lax.broadcasted_iota(jnp.int32, (rows, rows), 0)
    query = lax.broadcasted_iota(jnp.int32, (rows, rows), 1)

    for role in range(len(kv_refs)):
        start = info_ref[base + 2 * role]
        active = (info_ref[base + 2 * role + 1] > 0) & (start < seq_len)

        @pl.when(active)
        def _(role=role, start=start):
            keys = split_heads(kv_refs[role][0])
            values = split_heads(kv_refs[role][1])
            bad = key + start >= seq_len
            if diagonal and role == 0:
                bad = bad | (key > query)
            bias = jnp.where(bad, NEG, 0.0)
            for pair in range(2):
                q = q_ref[:, pair * 128 : pair * 128 + 128]
                scores = dot(keys[pair], q, 1, 1)
                weights, shrinks = [], []
                for head in range(2):
                    at = 2 * pair + head
                    part = scores[head * rows : (head + 1) * rows] * LOG2E + bias
                    old = top[0, at : at + 1, :]
                    new = jnp.maximum(old, jnp.max(part, 0, keepdims=True))
                    prob = jnp.exp2(part - new)
                    shrink = jnp.exp2(old - new)
                    top[0, at : at + 1, :] = new
                    fresh = jnp.sum(prob, 0, keepdims=True)
                    low[0, at : at + 1, :] = low[0, at : at + 1, :] * shrink + fresh
                    weights.append(prob.astype(BF16))
                    shrinks.append(jnp.broadcast_to(shrink, (HEAD_DIM, rows)))
                fresh = dot(values[pair], jnp.concatenate(weights, 0), 0, 0)
                acc[0, pair] = acc[0, pair] * jnp.concatenate(shrinks, 0) + fresh


def attend_start_body(base, roles, info_ref, len_ref, q_ref, *refs):
    acc, top, low = refs[roles:]
    acc[...] = jnp.zeros_like(acc)
    top[...] = jnp.full_like(top, NEG)
    low[...] = jnp.zeros_like(low)
    attend_blocks(info_ref, len_ref, base, q_ref, refs[:roles], acc, top, low, True)


def attend_finish_body(base, roles, info_ref, len_ref, q_ref, *refs):
    acc_in, top_in, low_in, wo_ref, x_ref, gain_ref = refs[roles : roles + 6]
    att_ref, lse_ref, hid_ref, mix_ref, acc, top, low, proj = refs[roles + 6 :]
    step = pl.program_id(0)
    rows = q_ref.shape[0]
    acc[...] = acc_in[...]
    top[...] = top_in[...]
    low[...] = low_in[...]
    attend_blocks(info_ref, len_ref, base, q_ref, refs[:roles], acc, top, low, False)
    for pair in range(2):
        sums = [low[0, 2 * pair + head : 2 * pair + head + 1, :] for head in range(2)]
        total = [jnp.broadcast_to(1.0 / s, (HEAD_DIM, rows)) for s in sums]
        att = acc[0, pair] * jnp.concatenate(total, 0)
        att_ref[:, pair * 128 : pair * 128 + 128] = jnp.transpose(att).astype(BF16)
    lse_ref[...] = top[...] + jnp.log2(jnp.maximum(low[...], 1e-30))

    @pl.when(step == 0)
    def _():
        proj[...] = x_ref[...].astype(F32)

    proj[...] += dot(att_ref[...], wo_ref[...], 1, 0)

    @pl.when(step == pl.num_programs(0) - 1)
    def _():
        hidden = proj[...]
        scale = lax.rsqrt(jnp.mean(hidden * hidden, -1, keepdims=True) + EPS)
        hid_ref[...] = hidden
        mix_ref[...] = (hidden * scale * gain_ref[...]).astype(BF16)


def attend(facts, base, q, blocks, state, wo=None, x=None, gain=None):
    rows, width = q.shape
    steps = width // 256
    roles = len(blocks)
    full = lambda shape: pl.BlockSpec(shape, lambda i, *s: (0, 0))
    wide = pl.BlockSpec((rows, 256), lambda i, *s: (0, i))
    heads = pl.BlockSpec((1, 8, rows), lambda i, *s: (i, 0, 0))
    accs = pl.BlockSpec((1, 2, 128, rows), lambda i, *s: (i, 0, 0, 0))
    in_specs = [wide] + [pl.BlockSpec((2, rows, 128), lambda i, *s: (0, 0, i))] * roles
    state_specs = [accs, heads, heads]
    state_shapes = [jax.ShapeDtypeStruct((steps, 2, 128, rows), F32)]
    state_shapes += [jax.ShapeDtypeStruct((steps, 8, rows), F32)] * 2
    args = [*facts, q, *blocks]
    scratch = []
    if state is None:
        body, out_specs, out_shape = attend_start_body, state_specs, state_shapes
    else:
        body = attend_finish_body
        args += [*state, wo, x, gain]
        in_specs += state_specs
        in_specs += [
            pl.BlockSpec((256, x.shape[1]), lambda i, *s: (i, 0)),
            full(x.shape),
            full((1, x.shape[1])),
        ]
        out_specs = [wide, heads, full(x.shape), full(x.shape)]
        out_shape = [
            jax.ShapeDtypeStruct((rows, width), BF16),
            jax.ShapeDtypeStruct((steps, 8, rows), F32),
            jax.ShapeDtypeStruct(x.shape, F32),
            jax.ShapeDtypeStruct(x.shape, BF16),
        ]
        scratch = [
            pltpu.VMEM((1, 2, 128, rows), F32),
            pltpu.VMEM((1, 8, rows), F32),
            pltpu.VMEM((1, 8, rows), F32),
            pltpu.VMEM(x.shape, F32),
        ]
    return pl.pallas_call(
        functools.partial(body, base, roles),
        grid_spec=pltpu.PrefetchScalarGridSpec(
            num_scalar_prefetch=2,
            grid=(steps,),
            in_specs=in_specs,
            out_specs=out_specs,
            scratch_shapes=scratch,
        ),
        out_shape=out_shape,
        compiler_params=params(("arbitrary",)),
        cost_estimate=COST,
        name="attend",
    )(*args)


def attend_back_body(base, roles, diagonal, info_ref, len_ref, q_ref, do_ref, lse_ref, delta_ref, *refs):
    kv_refs, (start_ref, dq_ref), dkv_refs = refs[:roles], refs[-roles - 2 : -roles], refs[-roles:]
    rows = q_ref.shape[0]
    seq_len = len_ref[0]
    if len(refs) > 2 * roles + 1:
        dq_ref[...] = start_ref[...]
    else:
        dq_ref[...] = jnp.zeros_like(dq_ref)
    key = lax.broadcasted_iota(jnp.int32, (rows, rows), 0)
    query = lax.broadcasted_iota(jnp.int32, (rows, rows), 1)
    lane = lax.broadcasted_iota(jnp.int32, (rows, 128), 1)
    low = lane < HEAD_DIM

    for role in range(roles):
        start = info_ref[base + 2 * role]
        active = (info_ref[base + 2 * role + 1] > 0) & (start < seq_len)

        @pl.when(jnp.logical_not(active))
        def _(role=role):
            dkv_refs[role][...] = jnp.zeros_like(dkv_refs[role])

        @pl.when(active)
        def _(role=role, start=start):
            keys = split_heads(kv_refs[role][0])
            values = split_heads(kv_refs[role][1])
            bad = key + start >= seq_len
            if diagonal and role == 0:
                bad = bad | (key > query)
            bias = jnp.where(bad, NEG, 0.0)
            dks, dvs = [], []
            for pair in range(2):
                q = q_ref[:, pair * 128 : pair * 128 + 128]
                do = do_ref[:, pair * 128 : pair * 128 + 128]
                scores = dot(keys[pair], q, 1, 1)
                grads = dot(values[pair], do, 1, 1)
                probs, raws = [], []
                for head in range(2):
                    at = 2 * pair + head
                    part = scores[head * rows : (head + 1) * rows] * LOG2E + bias
                    prob = jnp.exp2(part - lse_ref[0, at : at + 1, :])
                    grad = grads[head * rows : (head + 1) * rows]
                    raws.append((prob * (grad - delta_ref[0, at : at + 1, :])).astype(BF16))
                    probs.append(prob.astype(BF16))
                raw = jnp.concatenate(raws, 0)
                dq_ref[:, pair * 128 : pair * 128 + 128] += dot(raw, keys[pair], 0, 0)
                dks.append(dot(raw, q, 1, 0))
                dvs.append(dot(jnp.concatenate(probs, 0), do, 1, 0))
            for which, parts in enumerate((dks, dvs)):
                top_a, bottom_a = parts[0][:rows], parts[0][rows:]
                top_b, bottom_b = parts[1][:rows], parts[1][rows:]
                turn = pltpu.roll(jnp.where(low, top_b, bottom_a), HEAD_DIM, 1)
                whole = jnp.where(low, top_a, bottom_b) + turn
                dkv_refs[role][which] = whole.astype(dkv_refs[role].dtype)


def attend_back(facts, base, q, do, lse, delta, blocks, before, diagonal):
    rows, width = q.shape
    steps = width // 256
    roles = len(blocks)
    kvw = blocks[0].shape[2]
    wide = pl.BlockSpec((rows, 256), lambda i, *s: (0, i))
    heads = pl.BlockSpec((1, 8, rows), lambda i, *s: (i, 0, 0))
    kv = pl.BlockSpec((2, rows, 128), lambda i, *s: (0, 0, i))
    more = [] if before is None else [before]
    return pl.pallas_call(
        functools.partial(attend_back_body, base, roles, diagonal),
        grid_spec=pltpu.PrefetchScalarGridSpec(
            num_scalar_prefetch=2,
            grid=(steps,),
            in_specs=[wide, wide, heads, heads] + [kv] * roles + [wide] * len(more),
            out_specs=[wide] + [kv] * roles,
        ),
        out_shape=[jax.ShapeDtypeStruct((rows, width), F32)]
        + [jax.ShapeDtypeStruct((2, rows, kvw), BF16)] * roles,
        compiler_params=params(("arbitrary",)),
        cost_estimate=cost(40 * rows * rows * roles * width, 16 * 1024 * 1024),
        name="attend_back",
    )(*facts, q, do, lse, delta, *blocks, *more)


def expert_body(base, own, remotes, twins, first, carry, experts, info_ref, len_ref, *refs):
    x_refs, c_refs, wr_ref = refs[:twins], refs[twins : 2 * twins], refs[2 * twins]
    at = 2 * twins + 1
    near = refs[at : at + (3 if own else 0)]
    at += len(near)
    far = refs[at : at + remotes]
    at += remotes
    before, out_before = (refs[at], refs[at + 1]) if carry else (None, None)
    outs = refs[-15 if first else -13 :]
    gm_ref, gate_ref, out_ref, inner_ref, dg_ref, du_ref = outs[:6]
    copies = outs[6:8] if first else ()
    wbuf, sem, gm_acc, out_acc, gates, back, picked = outs[-7:]
    step = pl.program_id(0)
    total = own + remotes
    rows, width = x_refs[0].shape
    ff = width // 2
    slot = lax.rem(step, 2)
    offsets = (0, width, 2 * width, 2 * width + ff)
    sizes = (width, width, ff, ff)

    def fetch(target, where):
        def start(sources):
            for piece, (ref, off, size) in enumerate(zip(sources, offsets, sizes)):
                pltpu.make_async_copy(
                    ref, wbuf.at[where, pl.ds(off, size)], sem.at[where, piece]
                ).start()

        if own:

            @pl.when(target < own)
            def _():
                down = [near[2].at[target, :, pl.ds(k * ff, ff)] for k in range(2)]
                start([near[0].at[target], near[1].at[target]] + down)

        for i in range(remotes):

            @pl.when(target == own + i)
            def _(i=i):
                start([far[i].at[pl.ds(off, size)] for off, size in zip(offsets, sizes)])

    @pl.when(step == 0)
    def _():
        fetch(jnp.int32(0), 0)

    @pl.when(step + 1 < total)
    def _():
        fetch(step + 1, lax.rem(step + 1, 2))

    lane = lax.broadcasted_iota(jnp.int32, (rows, 128), 1)
    if twins == 2:
        x_ref, cot_ref = picked.at[0, pl.ds(0, rows)], picked.at[1]
    else:
        x_ref, cot_ref = x_refs[0], c_refs[0]

    @pl.when(step == 0)
    def _():
        if twins == 2:
            use = info_ref[base + 3] > 0
            picked[0, :rows] = jnp.where(use, x_refs[0][...], x_refs[1][...])
            picked[1] = jnp.where(use, c_refs[0][...], c_refs[1][...])
        logits = dot(x_ref[...], wr_ref[...], 1, 0)
        mask_t = cot_ref[pl.ds(rows, experts), :rows].astype(F32)
        mask_t = jnp.concatenate([mask_t, jnp.zeros((128 - experts, rows), F32)], 0)
        mask = jnp.transpose(mask_t) > 0.5
        high = jnp.max(jnp.where(mask, logits, NEG), 1, keepdims=True)
        raised = jnp.where(mask, jnp.exp(logits - high), 0.0)
        gates[...] = raised / jnp.sum(raised, 1, keepdims=True)
        gate_ref[...] = gates[...]
        back[...] = jnp.zeros_like(back)
        if carry:
            out_acc[...] = out_before[0].astype(F32)
            gm_acc[...] = before[:rows, :].astype(F32)
        else:
            out_acc[...] = jnp.zeros_like(out_acc)
            gm_acc[...] = jnp.zeros_like(gm_acc)
        if first:
            copies[0][0] = x_ref[...]
            copies[1][0] = cot_ref[pl.ds(0, rows), :]

    for piece, (off, size) in enumerate(zip(offsets, sizes)):
        place = wbuf.at[slot, pl.ds(off, size)]
        pltpu.make_async_copy(place, place, sem.at[slot, piece]).wait()

    wg = wbuf[slot, :width, :]
    wu = wbuf[slot, width : 2 * width, :]
    wd0 = wbuf[slot, 2 * width : 2 * width + ff, :]
    wd1 = wbuf[slot, 2 * width + ff :, :]
    which = info_ref[base + 2] + info_ref[base + 4 + step]
    x = x_ref[...]
    cot = cot_ref[pl.ds(0, rows), :]
    g = dot(x, wg, 1, 0)
    u = dot(x, wu, 1, 0)
    raw = dot(cot[:, :ff], wd0, 1, 1) + dot(cot[:, ff:], wd1, 1, 1)
    gate = jnp.sum(jnp.where(lane == which, gates[...], 0.0), 1, keepdims=True)
    sig = 1.0 / (1.0 + jnp.exp(-g))
    silu = g * sig
    inner = silu * u
    gg = jnp.sum(raw * inner, 1, keepdims=True)
    back[...] += jnp.where(lane == which, gg, 0.0)
    scaled = (gate * inner).astype(BF16)
    gi = gate * raw
    dg = (gi * u * (sig * (1.0 + g * (1.0 - sig)))).astype(BF16)
    du = (gi * silu).astype(BF16)
    inner_ref[0] = scaled
    dg_ref[0] = dg
    du_ref[0] = du
    out_acc[:, :ff] += dot(scaled, wd0, 1, 0)
    out_acc[:, ff:] += dot(scaled, wd1, 1, 0)
    gm_acc[...] += dot(dg, wg, 1, 1) + dot(du, wu, 1, 1)

    @pl.when(step == total - 1)
    def _():
        tail = jnp.transpose(back[...])[:experts, :]
        tail = jnp.concatenate([tail, jnp.zeros((experts, width - rows), F32)], 1)
        if carry:
            tail = tail + before[rows:, :].astype(F32)
        gm_ref[:rows, :] = gm_acc[...].astype(BF16)
        gm_ref[rows:, :] = tail.astype(BF16)
        out_ref[0] = out_acc[...].astype(BF16)


def expert_call(facts, base, xs, cots, wr, own_weights, far, experts, kept, before=None):
    rows, width = xs[0].shape
    own = own_weights[0].shape[0] if own_weights else 0
    remotes = len(far)
    total = own + remotes
    twins = len(xs)
    carry = before is not None
    first = not carry
    ff = width // 2
    full = lambda shape: pl.BlockSpec(shape, lambda i, *s: (0,) * len(shape))
    anywhere = pl.BlockSpec(memory_space=pl.ANY)
    big = pl.BlockSpec((1, rows, width), lambda i, s, n: (s[base + 1], 0, 0))
    part = pl.BlockSpec((1, rows, ff), lambda i, s, n: (s[base + 1], 0, s[base + 4 + i]))
    count = 6 if first else 4
    fresh = isinstance(kept[0], jax.ShapeDtypeStruct)
    aliased = [] if fresh else list(kept[:count])
    inputs = [*xs, *cots, wr, *own_weights, *far] + ([before] if carry else [])
    specs = [full((rows, width))] * twins + [full(cots[0].shape)] * twins + [full(wr.shape)]
    specs += [anywhere] * (len(own_weights) + remotes)
    specs += [full(before.shape)] if carry else []
    specs += [big if carry and k == 0 else anywhere for k in range(len(aliased))]
    gm_shape = (rows + experts, width)
    outs = pl.pallas_call(
        functools.partial(expert_body, base, own, remotes, twins, first, carry, experts),
        grid_spec=pltpu.PrefetchScalarGridSpec(
            num_scalar_prefetch=2,
            grid=(total,),
            in_specs=specs,
            out_specs=[full(gm_shape), full((rows, 128)), big, part, part, part]
            + ([big, big] if first else []),
            scratch_shapes=[
                pltpu.VMEM((2, 3 * width, ff), BF16),
                pltpu.SemaphoreType.DMA((2, 4)),
                pltpu.VMEM((rows, width), F32),
                pltpu.VMEM((rows, width), F32),
                pltpu.VMEM((rows, 128), F32),
                pltpu.VMEM((rows, 128), F32),
                pltpu.VMEM((2,) + gm_shape, BF16),
            ],
        ),
        out_shape=[
            jax.ShapeDtypeStruct(gm_shape, BF16),
            jax.ShapeDtypeStruct((rows, 128), F32),
        ]
        + [jax.ShapeDtypeStruct(k.shape, k.dtype) for k in kept[:count]],
        input_output_aliases={2 + len(inputs) + k: 2 + k for k in range(len(aliased))},
        compiler_params=params(("arbitrary",)),
        cost_estimate=COST
        if not far
        else cost(12 * rows * width * ff * total, total * 6 * width * ff),
        name="experts",
    )(*facts, *inputs, *aliased)
    return outs[0], outs[1], tuple(outs[2:]) + tuple(kept[count:])


def expert_grads_body(base, info_ref, len_ref, x_hbm, c_hbm, in_hbm, dg_hbm, du_hbm, o_ref, x, c, cols, sem):
    place, kind = pl.program_id(0), pl.program_id(1)
    step = place * 3 + kind
    ff = cols.shape[2]
    hidden = (dg_hbm, du_hbm, in_hbm)

    def fetch(target, start):
        at = lax.rem(target, 2)
        off = pl.ds(pl.multiple_of(info_ref[base + lax.div(target, 3)] * ff, 128), ff)
        for k, ref in enumerate(hidden):

            @pl.when(lax.rem(target, 3) == k)
            def _(ref=ref):
                pltpu.make_async_copy(ref.at[:, off], cols.at[at], sem.at[at]).start()

    @pl.when(step == 0)
    def _():
        pltpu.make_async_copy(x_hbm, x, sem.at[2]).start()
        fetch(step, True)
        pltpu.make_async_copy(c_hbm, c, sem.at[3]).start()
        pltpu.make_async_copy(x_hbm, x, sem.at[2]).wait()

    @pl.when(step + 1 < 3 * pl.num_programs(0))
    def _():
        fetch(step + 1, True)

    slot = lax.rem(step, 2)
    pltpu.make_async_copy(cols.at[slot], cols.at[slot], sem.at[slot]).wait()

    @pl.when(kind < 2)
    def _():
        o_ref[0, 0] = dot(x[...], cols[slot], 0, 0).astype(BF16)

    @pl.when(step == 2)
    def _():
        pltpu.make_async_copy(c_hbm, c, sem.at[3]).wait()

    @pl.when(kind == 2)
    def _():
        o_ref[0, 0, :ff] = dot(cols[slot], c[:, :ff], 0, 0).astype(BF16)
        o_ref[0, 0, ff:] = dot(cols[slot], c[:, ff:], 0, 0).astype(BF16)


def expert_grads(facts, base, count, x, c, inner, dg, du):
    rows, width = x.shape
    ff = width // 2
    anywhere = pl.BlockSpec(memory_space=pl.ANY)
    return pl.pallas_call(
        functools.partial(expert_grads_body, base),
        grid_spec=pltpu.PrefetchScalarGridSpec(
            num_scalar_prefetch=2,
            grid=(count, 3),
            in_specs=[anywhere] * 5,
            out_specs=pl.BlockSpec((1, 1, width, ff), lambda i, k, *s: (i, k, 0, 0)),
            scratch_shapes=[
                pltpu.VMEM((rows, width), BF16),
                pltpu.VMEM((rows, width), BF16),
                pltpu.VMEM((2, rows, ff), BF16),
                pltpu.SemaphoreType.DMA((4,)),
            ],
        ),
        out_shape=jax.ShapeDtypeStruct((count, 3, width, ff), BF16),
        compiler_params=params(("arbitrary",) * 2),
        cost_estimate=cost(6 * rows * width * ff * count, 16 * 1024 * 1024),
        name="expert_grads",
    )(*facts, x, c, inner, dg, du)


def middle_body(experts, *refs):
    sums, ends, refs = refs[:4], refs[4:8], refs[8:]
    gate_ref, wr_ref, hid_ref, cot_ref, att_ref, mix_ref, gain_ref, wo_hbm = refs[:8]
    gh_ref, gb_ref, do_ref, delta_ref, ffn_ref, router_ref, wo, sem, deltas, logit = refs[8:]
    step = pl.program_id(0)
    part, width = hid_ref.shape
    rows = gate_ref.shape[0]
    span = pl.ds(pl.multiple_of(step * part, part), part)

    @pl.when(step == 0)
    def _():
        pltpu.make_async_copy(wo_hbm, wo, sem).start()
        ffn_ref[...] = jnp.zeros_like(ffn_ref)
        router_ref[...] = jnp.zeros_like(router_ref)
        gg = ends[0][:, :rows].astype(F32)
        for ref in ends[1:]:
            gg = gg + ref[:, :rows].astype(F32)
        gg = jnp.transpose(jnp.concatenate([gg, jnp.zeros((128 - experts, rows), F32)], 0))
        gates = gate_ref[...]
        logit[...] = (gates * (gg - jnp.sum(gates * gg, 1, keepdims=True))).astype(BF16)

    total = sums[0][...].astype(F32)
    for ref in sums[1:]:
        total = total + ref[...].astype(F32)
    gl = logit[span, :]
    router_ref[...] += dot(gl, mix_ref[...], 0, 0)
    hidden = hid_ref[...]
    grad_mixed = total + dot(gl, wr_ref[...], 1, 1)
    scale = lax.rsqrt(jnp.mean(hidden * hidden, -1, keepdims=True) + EPS)
    ffn_ref[...] += jnp.sum(grad_mixed * hidden * scale, 0, keepdims=True)
    weighted = grad_mixed * gain_ref[...]
    mean = jnp.mean(weighted * hidden, -1, keepdims=True)
    grad = cot_ref[...].astype(F32) + scale * weighted - hidden * (scale * scale * scale * mean)
    gh_ref[...] = grad
    low = grad.astype(BF16)
    gb_ref[...] = low

    @pl.when(step == 0)
    def _():
        pltpu.make_async_copy(wo_hbm, wo, sem).wait()

    do = dot(low, wo[...], 1, 1).astype(BF16)
    do_ref[...] = do
    both = do.astype(F32) * att_ref[...].astype(F32)
    lane = lax.broadcasted_iota(jnp.int32, (part, 128), 1)
    found = jnp.zeros((part, 128), F32)
    for block in range(both.shape[1] // 128):
        pair = both[:, block * 128 : block * 128 + 128]
        front = jnp.sum(jnp.where(lane < HEAD_DIM, pair, 0.0), 1, keepdims=True)
        back = jnp.sum(jnp.where(lane < HEAD_DIM, 0.0, pair), 1, keepdims=True)
        found = jnp.where(lane == 2 * block, front, found)
        found = jnp.where(lane == 2 * block + 1, back, found)
    deltas[span, :] = found

    @pl.when(step == pl.num_programs(0) - 1)
    def _():
        turned = jnp.transpose(deltas[...])
        for group in range(delta_ref.shape[0]):
            delta_ref[group, :4, :] = turned[4 * group : 4 * group + 4]
            delta_ref[group, 4:, :] = jnp.zeros((4, rows), F32)


def middle(sums, gates, wr, hidden, cot_ext, attended, mixed, gain, wo, experts):
    rows, width = hidden.shape
    steps = 3
    heads = attended.shape[1] // HEAD_DIM
    row = lambda w: pl.BlockSpec((rows // steps, w), lambda i: (i, 0))
    end = pl.BlockSpec((experts, width), lambda i: (rows // experts, 0))
    full = lambda shape: pl.BlockSpec(shape, lambda i: (0,) * len(shape))
    return pl.pallas_call(
        functools.partial(middle_body, experts),
        grid=(steps,),
        in_specs=[row(width)] * 4
        + [end] * 4
        + [
            full((rows, 128)),
            full(wr.shape),
            row(width),
            row(width),
            row(attended.shape[1]),
            row(width),
            full((1, width)),
            pl.BlockSpec(memory_space=pl.ANY),
        ],
        out_specs=[
            row(width),
            row(width),
            row(attended.shape[1]),
            full((heads // 4, 8, rows)),
            full((1, width)),
            full((128, width)),
        ],
        out_shape=[
            jax.ShapeDtypeStruct((rows, width), F32),
            jax.ShapeDtypeStruct((rows, width), BF16),
            jax.ShapeDtypeStruct(attended.shape, BF16),
            jax.ShapeDtypeStruct((heads // 4, 8, rows), F32),
            jax.ShapeDtypeStruct((1, width), F32),
            jax.ShapeDtypeStruct((128, width), F32),
        ],
        scratch_shapes=[
            pltpu.VMEM(wo.shape, BF16),
            pltpu.SemaphoreType.DMA(()),
            pltpu.VMEM((rows, 128), F32),
            pltpu.VMEM((rows, 128), BF16),
        ],
        compiler_params=params(("arbitrary",)),
        cost_estimate=COST,
        name="middle",
    )(*sums, *sums, gates, wr, hidden, cot_ext, attended, mixed, gain, wo)


def early_body(experts, info_ref, len_ref, att_ref, gb_ref, router_ref, ffn_ref, give_ref, keep_ref):
    size = att_ref.shape[1] // 2
    core = info_ref[0]
    width = gb_ref.shape[1]
    row = lax.broadcasted_iota(jnp.int32, (16, width), 0)
    extra = jnp.concatenate([router_ref[:experts], jnp.where(row == 0, ffn_ref[...], 0.0)], 0)
    for ref, half in ((keep_ref, core), (give_ref, 1 - core)):
        part = att_ref[:, pl.ds(pl.multiple_of(half * size, 128), size)]
        ref[:size] = dot(part, gb_ref[...], 0, 0).astype(BF16)
        ref[size : size + experts + 16] = jnp.where(half == 0, extra, 0.0).astype(BF16)
        rest = ref.shape[0] - (size + experts + 16)
        ref[size + experts + 16 :] = jnp.zeros((rest, width), BF16)


def early_grads(facts, attended, gb, router, ffn, experts):
    rows, width = gb.shape
    count = attended.shape[1]
    col = lambda r: pl.BlockSpec((r, 256), lambda i, *s: (0, i))
    size = count // 2 + count // 8
    return pl.pallas_call(
        functools.partial(early_body, experts),
        grid_spec=pltpu.PrefetchScalarGridSpec(
            num_scalar_prefetch=2,
            grid=(width // 256,),
            in_specs=[
                pl.BlockSpec(attended.shape, lambda i, *s: (0, 0)),
                col(rows),
                col(router.shape[0]),
                col(1),
            ],
            out_specs=[col(size)] * 2,
        ),
        out_shape=[jax.ShapeDtypeStruct((size, width), BF16)] * 2,
        compiler_params=params(("arbitrary",)),
        cost_estimate=COST,
        name="early_grads",
    )(*facts, attended, gb, router, ffn)


def rope_back(g, cos_ref, sin_ref):
    cos = jnp.concatenate([cos_ref[...]] * (g.shape[1] // 128), 1)
    sin = jnp.concatenate([sin_ref[...]] * (g.shape[1] // 128), 1)
    return g * cos - swap_halves(g, lambda v, s: pltpu.roll(v, s, 1)) * sin


def split_rows(core, n_ref, lin, give_ref, keep_ref):
    size = n_ref.shape[1] // 2
    for ref, half in ((give_ref, 1 - core), (keep_ref, core)):
        part = n_ref[:, pl.ds(pl.multiple_of(half * size, 128), size)]
        ref[...] = dot(part, lin, 0, 0).astype(BF16)


def query_back_body(info_ref, len_ref, dq_ref, n_ref, cos_ref, sin_ref, lin_ref, give_ref, keep_ref):
    lin = rope_back(dq_ref[...] * HEAD_DIM**-0.5, cos_ref, sin_ref).astype(BF16)
    lin_ref[...] = lin
    split_rows(info_ref[0], n_ref, lin, give_ref, keep_ref)


def query_back(facts, dq, normed, cos, sin):
    rows, width = dq.shape
    col = lambda r: pl.BlockSpec((r, 256), lambda i, *s: (0, i))
    full = lambda shape: pl.BlockSpec(shape, lambda i, *s: (0, 0))
    size = normed.shape[1] // 2
    return pl.pallas_call(
        query_back_body,
        grid_spec=pltpu.PrefetchScalarGridSpec(
            num_scalar_prefetch=2,
            grid=(width // 256,),
            in_specs=[col(rows), full(normed.shape), full(cos.shape), full(sin.shape)],
            out_specs=[col(rows), col(size), col(size)],
        ),
        out_shape=[
            jax.ShapeDtypeStruct((rows, width), BF16),
            jax.ShapeDtypeStruct((size, width), BF16),
            jax.ShapeDtypeStruct((size, width), BF16),
        ],
        compiler_params=params(("arbitrary",)),
        cost_estimate=cost(2 * rows * width * width, 8 * 1024 * 1024),
        name="query_back",
    )(*facts, dq, normed, cos, sin)


def pair_back_body(parts, half_steps, info_ref, len_ref, *refs):
    n_ref, cos_ref, sin_ref, lin_ref, give_ref, keep_ref = refs[parts:]
    step = pl.program_id(0)
    total = refs[0][0].astype(F32)
    for ref in refs[1:parts]:
        total = total + ref[0].astype(F32)

    @pl.when(step < half_steps)
    def _():
        lin_ref[...] = rope_back(total, cos_ref, sin_ref).astype(BF16)

    @pl.when(step >= half_steps)
    def _():
        lin_ref[...] = total.astype(BF16)

    split_rows(info_ref[0], n_ref, lin_ref[...], give_ref, keep_ref)


def pair_back(facts, parts, normed, cos, sin):
    _, rows, kvw = parts[0].shape
    half_steps = kvw // 256
    col = lambda r: pl.BlockSpec((r, 256), lambda i, *s: (0, i))
    full = lambda shape: pl.BlockSpec(shape, lambda i, *s: (0, 0))
    part = pl.BlockSpec((1, rows, 256), lambda i, *s: (i // half_steps, 0, i % half_steps))
    size = normed.shape[1] // 2
    return pl.pallas_call(
        functools.partial(pair_back_body, len(parts), half_steps),
        grid_spec=pltpu.PrefetchScalarGridSpec(
            num_scalar_prefetch=2,
            grid=(2 * half_steps,),
            in_specs=[part] * len(parts) + [full(normed.shape), full(cos.shape), full(sin.shape)],
            out_specs=[col(rows), col(size), col(size)],
        ),
        out_shape=[
            jax.ShapeDtypeStruct((rows, 2 * kvw), BF16),
            jax.ShapeDtypeStruct((size, 2 * kvw), BF16),
            jax.ShapeDtypeStruct((size, 2 * kvw), BF16),
        ],
        compiler_params=params(("arbitrary",)),
        cost_estimate=COST,
        name="pair_back",
    )(*facts, *parts, normed, cos, sin)


def tokens_back_body(lq_ref, lkv_ref, wq_ref, wk_ref, wv_ref, x_ref, gh_ref, gain_ref, o_ref):
    kvw = wk_ref.shape[1]
    grad = dot(lq_ref[...], wq_ref[...], 1, 1)
    grad = grad + dot(lkv_ref[:, :kvw], wk_ref[...], 1, 1)
    grad = grad + dot(lkv_ref[:, kvw:], wv_ref[...], 1, 1)
    x = x_ref[...].astype(F32)
    scale = lax.rsqrt(jnp.mean(x * x, -1, keepdims=True) + EPS)
    weighted = grad * gain_ref[...]
    mean = jnp.mean(weighted * x, -1, keepdims=True)
    total = gh_ref[...] + scale * weighted - x * (scale * scale * scale * mean)
    o_ref[...] = total.astype(BF16)


def tokens_back(lq, lkv, wq, wk, wv, x, gh, gain):
    rows, width = x.shape
    row = lambda w: pl.BlockSpec((rows // 4, w), lambda i: (i, 0))
    full = lambda shape: pl.BlockSpec(shape, lambda i: (0, 0))
    return pl.pallas_call(
        tokens_back_body,
        grid=(4,),
        in_specs=[
            row(lq.shape[1]),
            row(lkv.shape[1]),
            full(wq.shape),
            full(wk.shape),
            full(wv.shape),
            row(width),
            row(width),
            full((1, width)),
        ],
        out_specs=row(width),
        out_shape=jax.ShapeDtypeStruct((rows, width), BF16),
        compiler_params=params(("arbitrary",)),
        cost_estimate=COST,
        name="tokens_back",
    )(lq, lkv, wq, wk, wv, x, gh, gain)


def finish_body(info_ref, len_ref, qa, qb, pa, pb, wq_ref, wk_ref, wv_ref, gain_ref, q_ref, k_ref, v_ref, n_ref):
    mine = pl.program_id(0) // (pl.num_programs(0) // 2) == info_ref[0]
    q = jnp.where(mine, qa[...].astype(F32), qb[...].astype(F32))
    pair = jnp.where(mine, pa[...].astype(F32), pb[...].astype(F32))
    kvw = k_ref.shape[1]
    q_ref[...] = q
    k_ref[...] = pair[:, :kvw]
    v_ref[...] = pair[:, kvw:]
    gain = jnp.sum(q * wq_ref[...].astype(F32), 1, keepdims=True)
    gain = gain + jnp.sum(pair[:, :kvw] * wk_ref[...].astype(F32), 1, keepdims=True)
    gain = gain + jnp.sum(pair[:, kvw:] * wv_ref[...].astype(F32), 1, keepdims=True)
    turned = jnp.transpose(jnp.broadcast_to(gain, (gain.shape[0], 128)))
    n_ref[...] = turned[:1] / gain_ref[...]


def finish(facts, qa, qb, pa, pb, wq, wk, wv, gain):
    width = wq.shape[0]
    part = width // 4
    half = lambda w: pl.BlockSpec((part, w), lambda i, *s: (i % 2, 0))
    row = lambda w: pl.BlockSpec((part, w), lambda i, *s: (i, 0))
    line = pl.BlockSpec((1, part), lambda i, *s: (0, i))
    return pl.pallas_call(
        finish_body,
        grid_spec=pltpu.PrefetchScalarGridSpec(
            num_scalar_prefetch=2,
            grid=(4,),
            in_specs=[half(width)] * 4
            + [row(wq.shape[1]), row(wk.shape[1]), row(wv.shape[1]), line],
            out_specs=[row(wq.shape[1]), row(wk.shape[1]), row(wv.shape[1]), line],
        ),
        out_shape=[
            jax.ShapeDtypeStruct(wq.shape, F32),
            jax.ShapeDtypeStruct(wk.shape, F32),
            jax.ShapeDtypeStruct(wv.shape, F32),
            jax.ShapeDtypeStruct((1, width), F32),
        ],
        compiler_params=params(("arbitrary",)),
        cost_estimate=COST,
        name="finish",
    )(*facts, qa, qb, pa, pb, wq, wk, wv, gain)


def total_of(parts):
    total = parts[0].astype(F32)
    for part in parts[1:]:
        total = total + part.astype(F32)
    return total.astype(BF16)


def scatter_start(buf, axis):
    name, size, pos, pairs = axis
    rows = buf.shape[0] // size
    take = lambda k: lax.dynamic_slice_in_dim(buf, k * rows, rows, 0)
    parts = [take(pos)]
    for shift in range(1, size):
        parts.append(lax.ppermute(take((pos + shift) % size), name, pairs(shift)))
    return parts


def gather_start(buf, axis):
    name, size, pos, pairs = axis
    return [lax.ppermute(buf, name, pairs(shift)) for shift in range(size - 1, 0, -1)] + [buf]


def gather_end(order, axis):
    name, size, pos, pairs = axis
    rows = order[0].shape[0]
    if size == 2:
        pick = lambda a, b: jnp.concatenate([a, b], 0)
        return jnp.where(pos == 0, pick(order[1], order[0]), pick(order[0], order[1]))
    double = jnp.concatenate(order + order[:-1], 0)
    return lax.dynamic_slice_in_dim(double, (size - 1 - pos) * rows, size * rows, 0)


def device_facts(nx, ny, own, rows, ep_index, ctx_index):
    group = nx * own
    table = np.zeros((NZ * nx, ny * CORES, 160), np.int32)
    for ep in range(NZ * nx):
        for ctx in range(ny * CORES):
            z, x, y, core = ep // nx, ep % nx, ctx // CORES, ctx % CORES
            out = table[ep, ctx]
            out[0], out[1] = core, ctx
            out[16:20] = ctx * rows, 1, (ctx - 1) * rows, core
            for back in range(1, ny):
                at, block = 16 + 4 * back, (y - back) * CORES
                out[at : at + 4] = (block + core) * rows, y >= back, (block + 1 - core) * rows, y >= back
            near = [x * own + i for i in range(own)]
            far = [(x - s) % nx * own + i for s in range(1, nx) for i in (core, 1 - core)]
            shard_c, shard_d, inside = (2, 2, 1, 1)[z], (3, 3, 0, 0)[z], int(z in (1, 2))
            calls = [(z, 1, near), (z, 1, far), (z ^ 1, 1, near + far)]
            calls += [(shard_c, inside, near + far), (shard_d, inside, near + far)]
            for k, (shard, pick, places) in enumerate(calls):
                out[48 + 16 * k : 52 + 16 * k] = 0, shard, z * group, pick
                out[52 + 16 * k : 52 + 16 * k + len(places)] = places
            for j in range(nx):
                out[128 + j] = (x + j) % nx * own + 1 - core
                out[144 + j] = (x + j) % nx * own + core
    line = lax.dynamic_slice(
        jnp.asarray(table), (ep_index, ctx_index, jnp.int32(0)), (1, 1, table.shape[2])
    )
    return line.reshape(-1)


def local(
    tokens,
    lengths,
    routes,
    cotangent,
    attn_norm,
    w_query,
    w_key,
    w_value,
    w_out,
    ffn_norm,
    w_router,
    expert_gate_weight,
    expert_up_weight,
    expert_down_weight,
):
    rows, width = tokens.shape[1:]
    half = rows // 2
    experts = w_router.shape[1]
    own = expert_gate_weight.shape[0]
    ff = expert_gate_weight.shape[2]
    kvw = w_key.shape[1]
    ctx_size, ep_size = lax.axis_size("ctx"), lax.axis_size("ep")
    ny, nx = ctx_size // CORES, ep_size // NZ
    ctx_index, ep_index = lax.axis_index("ctx"), lax.axis_index("ep")
    y, core = ctx_index // CORES, ctx_index % CORES
    z, xpos = ep_index // nx, ep_index % nx
    seq_len = lengths[0]
    tokens = tokens[0]
    valid_flag = ctx_index * rows + jnp.arange(rows, dtype=jnp.int32) < seq_len
    valid = valid_flag.astype(F32)[:, None]
    tie = lax.optimization_barrier

    core_swap = [(c, c ^ 1) for c in range(ctx_size)]
    core_up = [(c, c + 1) for c in range(0, ctx_size, CORES)]
    core_down = [(c + 1, c) for c in range(0, ctx_size, CORES)]
    y_up = lambda k: [(c, c + CORES * k) for c in range(ctx_size - CORES * k)]
    y_down = lambda k: [(b, a) for a, b in y_up(k)]
    zx = lambda pairs: [(a * nx + i, b * nx + i) for a, b in pairs for i in range(nx)]
    z_groups = [[i + nx * k for k in range(NZ)] for i in range(nx)]
    x_shift = lambda s: [(k * nx + i, k * nx + (i + s) % nx) for k in range(NZ) for i in range(nx)]
    y_ring = lambda s: [(c, (c + CORES * s) % ctx_size) for c in range(ctx_size)]
    core_axis = ("ctx", CORES, core, lambda s: core_swap)
    y_axis = ("ctx", ny, y, y_ring)
    x_axis = ("ep", nx, xpos, x_shift)
    z_axis = ("ep", NZ, z, lambda s: zx([(k, (k + s) % NZ) for k in range(NZ)]))

    weights = (expert_gate_weight, expert_up_weight, expert_down_weight)
    facts = (device_facts(nx, ny, own, rows, ep_index, ctx_index), lengths)
    cot_ext, sent = prepare(facts, routes[0].T, cotangent[0], weights, experts)
    arrived = [lax.ppermute(sent, "ep", x_shift(shift)) for shift in range(1, nx)]

    swap, mid, out = [(0, 1), (1, 0), (2, 3), (3, 2)], [(1, 2), (2, 1)], [(1, 0), (2, 3)]
    cot_near = lax.ppermute(cot_ext, "ep", zx(swap))
    cot_middle = lax.ppermute(cot_ext, "ep", zx(mid))
    tokens, cot_ext, sent = tie((tokens, cot_ext, sent))
    fine, starts = rope_constants(ctx_size, rows)
    normed, q, kv, cos, sin = project(
        facts, tokens, attn_norm[None], w_query, w_key, w_value, fine, starts, ctx_size
    )

    blocks = [kv, lax.ppermute(kv, "ctx", core_up)]
    travelling = kv
    for back in range(1, ny):
        travelling = lax.ppermute(travelling, "ctx", y_up(1))
        blocks.append(travelling)
    near_row, far_row = 16, 20
    state = attend(facts, near_row, q, blocks[:2], None)
    came, state, cot_near, cot_middle = tie((blocks[2:], state, cot_near, cot_middle))
    cot_across = lax.ppermute(cot_near, "ep", zx(mid))
    cot_outward = lax.ppermute(cot_middle, "ep", zx(out))
    blocks = blocks[:2]
    for piece in came:
        blocks += [piece, lax.ppermute(piece, "ctx", core_swap)]
    attended, lse, hidden, mixed = attend(
        facts, far_row, q, blocks[2:], state, w_out, tokens, ffn_norm[None]
    )

    wr = jnp.pad(w_router, ((0, 0), (0, 128 - experts)))
    group = nx * own
    widths = (width, group * ff, group * ff, group * ff, width, width)
    kept = tuple(jax.ShapeDtypeStruct((NZ, rows, w), BF16) for w in widths)

    def run(call, data, cots, near, far, kept, before=None):
        return expert_call(
            facts, 48 + 16 * call, data, cots, wr, near, far, experts, kept, before
        )

    ends, away = [(0, 1), (3, 2)], [(2, 3), (1, 0)]
    near = lax.ppermute(mixed, "ep", zx(swap))
    middle_rows = lax.ppermute(mixed, "ep", zx(mid))
    mixed, cot_across, cot_outward = tie((mixed, cot_across, cot_outward))
    gm_a, gates, kept = run(0, (mixed,), (cot_ext,), weights, [], kept)
    near, middle_rows, arrived, kept = tie((near, middle_rows, arrived, kept))
    across = lax.ppermute(near, "ep", zx(mid))
    outward = lax.ppermute(middle_rows, "ep", zx(out))
    far = []
    for piece in arrived:
        far += [piece, lax.ppermute(piece, "ctx", core_swap)]
    gm_a, _, kept = run(1, (mixed,), (cot_ext,), (), far, kept, gm_a)
    across, outward, kept = tie((across, outward, kept))
    last = lax.ppermute(across, "ep", zx(out))
    gm_b, _, kept = run(2, (near,), (cot_near,), weights, far, kept)
    third = lax.ppermute(gm_b, "ep", zx(ends))
    last, kept, cot_across = tie((last, kept, cot_across))
    cot_last = lax.ppermute(cot_across, "ep", zx(out))
    cots = (cot_middle, cot_outward)
    gm_c, _, kept = run(3, (middle_rows, outward), cots, weights, far, kept)
    second = lax.ppermute(gm_c, "ep", zx(ends))
    third, cot_last, kept = tie((third, cot_last, kept))
    cots = (cot_across, cot_last)
    gm_d, _, kept = run(4, (across, last), cots, weights, far, kept)
    first = lax.ppermute(gm_d, "ep", zx(ends))

    add = lambda a, b: (a.astype(F32) + b.astype(F32)).astype(BF16)
    line = lambda a: a.reshape(NZ * rows, a.shape[2])
    saved = lambda kept: [line(kept[k]) for k in (4, 5, 1, 2, 3)]
    second, kept = tie((second, kept))
    turned = lax.ppermute(add(gm_c, second), "ep", zx(mid))
    give = expert_grads(facts, 128, nx, *saved(kept))
    first, turned, give, kept = tie((first, turned, give, kept))
    carried = lax.ppermute(add(gm_d, first), "ep", zx(mid))
    came = lax.ppermute(give, "ctx", core_swap)
    keep = expert_grads(facts, 144, nx, *saved(kept))
    carried, keep, came = tie((carried, keep, came))
    send, keep, came = tie((add(gm_b, carried), keep, came))
    final = lax.ppermute(send, "ep", zx(away))
    total = [[add(keep[j, 0], came[j, 0]) for j in range(nx)]]
    total, keep, came = tie((total, keep, came))
    total += [[add(keep[j, k], came[j, k]) for j in range(nx)] for k in (1, 2)]
    over_x = lambda k: [lax.ppermute(total[k][s], "ep", x_shift(s)) for s in range(1, nx)]
    x_came = [over_x(0)]

    sums = [gm_a, third, turned, final]
    gh, gb, do, delta, grad_ffn, grad_router = middle(
        sums, gates, wr, hidden, cot_ext, attended, mixed, ffn_norm[None], w_out, experts
    )
    give, early = early_grads(facts, attended, gb, grad_router, grad_ffn, experts)
    give, early, do, x_came, out_all = tie((give, early, do, x_came, kept[0]))
    expert_sum = lax.psum_scatter(
        line(out_all), "ep", scatter_dimension=0, axis_index_groups=z_groups, tiled=True
    )

    y_parts = [scatter_start(total_of([total[0][0]] + x_came[0]), y_axis)]
    x_came.append(over_x(1))
    early = [early, lax.ppermute(give, "ctx", core_swap)]
    dq = None
    far_dkv = []
    if ny > 1:
        dq, *far_dkv = attend_back(facts, far_row, q, do, lse, delta, blocks[2:], None, False)
    dq, far_dkv, y_parts, x_came, early = tie((dq, far_dkv, y_parts, x_came, early))

    homeward = [
        lax.ppermute(add(far_dkv[2 * k], lax.ppermute(far_dkv[2 * k + 1], "ctx", core_swap)), "ctx", y_down(k + 1))
        for k in range(ny - 1)
    ]
    x_came.append(over_x(2))
    early = total_of(early)
    dq, *near_dkv = attend_back(facts, near_row, q, do, lse, delta, blocks[:2], dq, True)
    dq, homeward, x_came, near_dkv, early = tie((dq, homeward, x_came, near_dkv, early))

    parts = [near_dkv[0], lax.ppermute(near_dkv[1], "ctx", core_down), *homeward]
    y_parts.append(scatter_start(total_of([total[1][0]] + x_came[1]), y_axis))
    early = scatter_start(early, x_axis)
    lin_q, give, keep = query_back(facts, dq, normed, cos, sin)
    parts, lin_q, give, keep = tie((parts, lin_q, give, keep))

    half_q = [keep, lax.ppermute(give, "ctx", core_swap)]
    lin_kv, give, keep = pair_back(facts, parts, normed, cos, sin)
    half_q, lin_kv, give, keep, y_parts, early, expert_sum = tie(
        (half_q, lin_kv, give, keep, y_parts, early, expert_sum)
    )

    half_kv = [keep, lax.ppermute(give, "ctx", core_swap)]
    one = scatter_start(total_of(half_q), y_axis)
    two = scatter_start(total_of(half_kv), x_axis)
    early = scatter_start(total_of(early), z_axis)
    grad_tokens = tokens_back(
        lin_q, lin_kv, w_query, w_key, w_value, tokens, gh, attn_norm[None]
    )
    one, two, early, grad_tokens = tie((one, two, early, grad_tokens))
    one = scatter_start(total_of(one), x_axis)
    two = scatter_start(total_of(two), y_axis)
    early = scatter_start(total_of(early), y_axis)
    y_parts.append(scatter_start(total_of([total[2][0]] + x_came[2]), y_axis))
    one, two, early = tie((one, two, early))
    both = scatter_start(jnp.concatenate([total_of(one), total_of(two)], 0), z_axis)
    early = gather_start(total_of(early), y_axis)
    grads = [gather_start(total_of(y_parts[0]), y_axis)]
    both, early, y_parts = tie((both, early, y_parts))
    both = gather_start(total_of(both), z_axis)
    grads.append(gather_start(total_of(y_parts[1]), y_axis))
    both, early, grads[0] = tie((both, early, grads[0]))
    both = gather_end(both, z_axis)
    size = both.shape[0] // 2
    one, two = gather_start(both[:size], x_axis), gather_start(both[size:], y_axis)
    early = gather_start(gather_end(early, y_axis), z_axis)
    result_out = (valid * (hidden + expert_sum.astype(F32))).astype(BF16)
    one, two, result_out, grads = tie((one, two, result_out, grads))
    one = gather_start(gather_end(one, x_axis), y_axis)
    two = gather_start(gather_end(two, y_axis), x_axis)
    whole = lambda g: gather_end(gather_start(gather_end(g, y_axis)[None], core_axis), core_axis)
    ready = [whole(g).reshape(own, width, ff).astype(F32) for g in grads]
    grads = gather_start(total_of(y_parts[2]), y_axis)
    one, two, ready, early = tie((one, two, ready, early))
    one, two = gather_end(one, y_axis), gather_end(two, x_axis)
    swapped = lax.ppermute(one, "ctx", core_swap), lax.ppermute(two, "ctx", core_swap)
    early = gather_start(gather_end(early, z_axis), x_axis)
    swapped, one, two = tie((swapped, one, two))
    late_q, late_k, late_v, gain = finish(
        facts, one, swapped[0], two, swapped[1], w_query, w_key, w_value, attn_norm[None]
    )
    early, late_q, grads = tie((early, late_q, grads))
    early = gather_end(early, x_axis)
    down = gather_end(grads, y_axis)
    early = gather_end(gather_start(early[None], core_axis), core_axis)
    w_out_sum = early[:, : width // 2].reshape(width, width).astype(F32)
    small = early[0, width // 2 :].astype(F32)
    down = gather_end(gather_start(down[None], core_axis), core_axis).reshape(own, width, ff)
    down = jnp.concatenate([down[:, :ff], down[:, ff:]], -1).astype(F32)
    return (
        result_out[None],
        grad_tokens[None],
        gain[0],
        late_q,
        late_k,
        late_v,
        w_out_sum,
        small[experts],
        small[:experts].T,
        *ready,
        down,
    )


def solution(mesh):
    rows, whole, split = P("ep", "ctx", None), P(), P("ep", None, None)
    return jax.shard_map(
        local,
        mesh=mesh,
        in_specs=(rows, P("ep"), rows, rows) + (whole,) * 7 + (split,) * 3,
        out_specs=(rows, rows) + (whole,) * 7 + (split,) * 3,
        check_vma=False,
    )
```

```python
import functools

import jax
import jax.numpy as jnp
import numpy as np
from jax import lax
from jax.experimental import pallas as pl
from jax.experimental.pallas import tpu as pltpu
from jax.sharding import PartitionSpec as P

HEAD_DIM = 64
EPS = 1e-06
THETA = 10000.0
NEG = -1e30
LOG2E = 1.4426950408889634
PER_STEP = 2
NZ = 4
VMEM = 58 * 1024 * 1024
CORES = 2
F32 = jnp.float32
BF16 = jnp.bfloat16


def dot(a, b, ca, cb):
    return lax.dot_general(a, b, (((ca,), (cb,)), ((), ())), preferred_element_type=F32)


def params(semantics):
    return pltpu.CompilerParams(dimension_semantics=semantics, vmem_limit_bytes=VMEM)


COST = pl.CostEstimate(flops=1 << 20, bytes_accessed=1 << 20, transcendentals=0)


def cost(flops, nbytes):
    return pl.CostEstimate(flops=flops, bytes_accessed=nbytes, transcendentals=0)


def rope_constants(ctx_size, rows):
    half = HEAD_DIM // 2
    inv = THETA ** (-np.arange(half, dtype=np.float64) / half)
    fine = np.arange(rows, dtype=np.float64)[:, None] * inv[None, :]
    coarse = (rows * np.arange(ctx_size, dtype=np.float64))[:, None] * inv[None, :]
    tile = lambda t: jnp.asarray(np.tile(t, (1, 128 // half)).astype(np.float32))
    pad = np.zeros(((-2 * ctx_size) % 8, half))
    return (
        tile(np.concatenate([np.cos(fine), np.sin(fine)], 0)),
        tile(np.concatenate([np.cos(coarse), np.sin(coarse), pad], 0)),
    )


def swap_halves(x, roll):
    half = HEAD_DIM // 2
    width = x.shape[1]
    lane = lax.broadcasted_iota(jnp.int32, x.shape, 1)
    return jnp.where(lane % HEAD_DIM < half, roll(x, width - half), roll(x, half))


def prepare_body(experts, info_ref, len_ref, r_ref, c_ref, wg, wu, wd, ext_ref, sent_ref, buf, sem):
    rows, width = c_ref.shape
    ff = width // 2
    core = info_ref[0]
    count = len_ref[0] - info_ref[1] * rows
    pieces = [wg.at[core], wu.at[core]] + [wd.at[core, :, pl.ds(k * ff, ff)] for k in range(2)]
    spans = [pl.ds(0, width), pl.ds(width, width), pl.ds(2 * width, ff), pl.ds(2 * width + ff, ff)]
    into = [
        pltpu.make_async_copy(piece, buf.at[span], sem.at[0, k])
        for k, (piece, span) in enumerate(zip(pieces, spans))
    ]
    back = [
        pltpu.make_async_copy(buf.at[span], sent_ref.at[span], sem.at[1, k])
        for k, span in enumerate(spans)
    ]
    for copy in into:
        copy.start()
    row = lax.broadcasted_iota(jnp.int32, (rows, width), 0)
    ext_ref[:rows] = jnp.where(row < count, c_ref[...], jnp.zeros((), BF16))
    expert = lax.broadcasted_iota(jnp.int32, (experts, rows), 0)
    named = jnp.zeros((experts, rows), F32)
    for k in range(r_ref.shape[0]):
        named = jnp.where(expert == r_ref[k : k + 1, :], 1.0, named)
    ext_ref[rows:] = jnp.concatenate(
        [named, jnp.zeros((experts, width - rows), F32)], 1
    ).astype(BF16)
    for k in range(4):
        into[k].wait()
        back[k].start()
    for copy in back:
        copy.wait()


def prepare(facts, routes, cot, weights, experts):
    rows, width = cot.shape
    ff = width // 2
    anywhere = pl.BlockSpec(memory_space=pl.ANY)
    full = lambda shape: pl.BlockSpec(shape, lambda i, *s: (0, 0))
    return pl.pallas_call(
        functools.partial(prepare_body, experts),
        grid_spec=pltpu.PrefetchScalarGridSpec(
            num_scalar_prefetch=2,
            grid=(1,),
            in_specs=[full(routes.shape), full(cot.shape)] + [anywhere] * 3,
            out_specs=[full((rows + experts, width)), anywhere],
            scratch_shapes=[
                pltpu.VMEM((3 * width, ff), BF16),
                pltpu.SemaphoreType.DMA((2, 4)),
            ],
        ),
        out_shape=[
            jax.ShapeDtypeStruct((rows + experts, width), BF16),
            jax.ShapeDtypeStruct((3 * width, ff), BF16),
        ],
        compiler_params=params(("arbitrary",)),
        cost_estimate=COST,
        name="prepare",
    )(*facts, routes, cot, *weights)


def project_body(blocks, info_ref, len_ref, x_ref, gain_ref, wq_ref, wk_ref, wv_ref, fine_ref, start_ref,
                 n_ref, q_ref, kv_ref, cos_ref, sin_ref):
    step = pl.program_id(0)
    wide = q_ref.shape[1]
    nq = pl.num_programs(0) - 2
    rows = x_ref.shape[0]

    @pl.when(step == 0)
    def _():
        x = x_ref[...].astype(F32)
        scale = lax.rsqrt(jnp.mean(x * x, -1, keepdims=True) + EPS)
        n_ref[...] = (x * scale * gain_ref[...]).astype(BF16)
        cos_f, sin_f = fine_ref[:rows], fine_ref[rows:]
        cos_c = start_ref[pl.ds(info_ref[1], 1), :]
        sin_c = start_ref[pl.ds(info_ref[1] + blocks, 1), :]
        lane = lax.broadcasted_iota(jnp.int32, (rows, 128), 1)
        sign = jnp.where(lane % HEAD_DIM < HEAD_DIM // 2, -1.0, 1.0)
        cos_ref[...] = cos_f * cos_c - sin_f * sin_c
        sin_ref[...] = (sin_f * cos_c + cos_f * sin_c) * sign

    def rope(lin):
        cos = jnp.concatenate([cos_ref[...]] * (wide // 128), 1)
        sin = jnp.concatenate([sin_ref[...]] * (wide // 128), 1)
        return lin * cos + swap_halves(lin, lambda v, s: pltpu.roll(v, s, 1)) * sin

    @pl.when(step < nq)
    def _():
        lin = dot(n_ref[...], wq_ref[...], 1, 0)
        q_ref[...] = (rope(lin) * (LOG2E * HEAD_DIM**-0.5)).astype(BF16)

    @pl.when(step == nq)
    def _():
        kv_ref[...] = rope(dot(n_ref[...], wk_ref[...], 1, 0)).astype(BF16)[None]

    @pl.when(step == nq + 1)
    def _():
        kv_ref[...] = dot(n_ref[...], wv_ref[...], 1, 0).astype(BF16)[None]


def project(facts, x, gain, wq, wk, wv, fine, starts, blocks):
    rows, width = x.shape
    kvw = wk.shape[1]
    nq = wq.shape[1] // kvw
    clip = lambda v, hi: jnp.minimum(jnp.maximum(v, 0), hi)
    full = lambda shape: pl.BlockSpec(shape, lambda i, *s: (0, 0))
    return pl.pallas_call(
        functools.partial(project_body, blocks),
        grid_spec=pltpu.PrefetchScalarGridSpec(
            num_scalar_prefetch=2,
            grid=(nq + 2,),
            in_specs=[
                full((rows, width)),
                full((1, width)),
                pl.BlockSpec((width, kvw), lambda i, *s: (0, clip(i, nq - 1))),
                full((width, kvw)),
                full((width, kvw)),
                full(fine.shape),
                full(starts.shape),
            ],
            out_specs=[
                full((rows, width)),
                pl.BlockSpec((rows, kvw), lambda i, *s: (0, clip(i, nq - 1))),
                pl.BlockSpec((1, rows, kvw), lambda i, *s: (clip(i - nq, 1), 0, 0)),
                full((rows, 128)),
                full((rows, 128)),
            ],
        ),
        out_shape=[
            jax.ShapeDtypeStruct((rows, width), BF16),
            jax.ShapeDtypeStruct((rows, wq.shape[1]), BF16),
            jax.ShapeDtypeStruct((2, rows, kvw), BF16),
            jax.ShapeDtypeStruct((rows, 128), F32),
            jax.ShapeDtypeStruct((rows, 128), F32),
        ],
        compiler_params=params(("arbitrary",)),
        cost_estimate=COST,
        name="project",
    )(*facts, x, gain, wq, wk, wv, fine, starts)


def split_heads(block):
    lane = lax.broadcasted_iota(jnp.int32, block.shape, 1)
    low = lane < HEAD_DIM
    zero = jnp.zeros_like(block)
    turned = jnp.concatenate([block[:, HEAD_DIM:], block[:, :HEAD_DIM]], 1)
    first = jnp.concatenate([jnp.where(low, block, zero), jnp.where(low, zero, turned)], 0)
    second = jnp.concatenate([jnp.where(low, turned, zero), jnp.where(low, zero, block)], 0)
    return first, second


def with_mask(active, start, rows, seq_len, diagonal, work):
    if diagonal:
        pl.when(active)(lambda: work(True))
        return
    whole = start + rows <= seq_len
    pl.when(active & whole)(lambda: work(False))
    pl.when(active & jnp.logical_not(whole))(lambda: work(True))


def mask_of(start, rows, seq_len, diagonal):
    key = lax.broadcasted_iota(jnp.int32, (rows, rows), 0)
    bad = key + start >= seq_len
    if diagonal:
        bad = bad | (key > lax.broadcasted_iota(jnp.int32, (rows, rows), 1))
    return jnp.where(bad, NEG, 0.0)


def attend_blocks(info_ref, len_ref, base, q_ref, kv_refs, acc, top, low, diagonal):
    rows = q_ref.shape[0]
    seq_len = len_ref[0]

    def work(role, start, masked):
        if masked:
            bias = mask_of(start, rows, seq_len, diagonal and role == 0)
        for group in range(q_ref.shape[1] // 256):
            lanes = slice(group * 128, group * 128 + 128)
            keys = split_heads(kv_refs[role][0, :, lanes])
            values = split_heads(kv_refs[role][1, :, lanes])
            for pair in range(2):
                at = 256 * group + 128 * pair
                scores = dot(keys[pair], q_ref[:, at : at + 128], 1, 1)
                weights, shrinks = [], []
                for head in range(2):
                    at = 2 * pair + head
                    part = scores[head * rows : (head + 1) * rows]
                    if masked:
                        part = part + bias
                    old = top[group, at : at + 1, :]
                    new = jnp.maximum(old, jnp.max(part, 0, keepdims=True))
                    prob = jnp.exp2(part - new)
                    shrink = jnp.exp2(old - new)
                    top[group, at : at + 1, :] = new
                    fresh = jnp.sum(prob, 0, keepdims=True)
                    low[group, at : at + 1, :] = low[group, at : at + 1, :] * shrink + fresh
                    weights.append(prob.astype(BF16))
                    shrinks.append(jnp.broadcast_to(shrink, (HEAD_DIM, rows)))
                fresh = dot(values[pair], jnp.concatenate(weights, 0), 0, 0)
                acc[group, pair] = acc[group, pair] * jnp.concatenate(shrinks, 0) + fresh

    for role in range(len(kv_refs)):
        start = info_ref[base + 2 * role]
        active = (info_ref[base + 2 * role + 1] > 0) & (start < seq_len)
        with_mask(
            active, start, rows, seq_len, diagonal and role == 0, functools.partial(work, role, start)
        )


def attend_start_body(base, roles, info_ref, len_ref, q_ref, *refs):
    acc, top, low = refs[roles:]
    acc[...] = jnp.zeros_like(acc)
    top[...] = jnp.full_like(top, NEG)
    low[...] = jnp.zeros_like(low)
    attend_blocks(info_ref, len_ref, base, q_ref, refs[:roles], acc, top, low, True)


def attend_finish_body(base, roles, info_ref, len_ref, q_ref, *refs):
    acc_in, top_in, low_in, wo_ref, x_ref, gain_ref = refs[roles : roles + 6]
    att_ref, lse_ref, hid_ref, mix_ref, acc, top, low, proj = refs[roles + 6 :]
    step = pl.program_id(0)
    rows = q_ref.shape[0]
    acc[...] = acc_in[...]
    top[...] = top_in[...]
    low[...] = low_in[...]
    attend_blocks(info_ref, len_ref, base, q_ref, refs[:roles], acc, top, low, False)
    for group in range(q_ref.shape[1] // 256):
        for pair in range(2):
            sums = [low[group, 2 * pair + head : 2 * pair + head + 1, :] for head in range(2)]
            total = [jnp.broadcast_to(1.0 / s, (HEAD_DIM, rows)) for s in sums]
            att = acc[group, pair] * jnp.concatenate(total, 0)
            at = 256 * group + 128 * pair
            att_ref[:, at : at + 128] = jnp.transpose(att).astype(BF16)
    lse_ref[...] = top[...] + jnp.log2(jnp.maximum(low[...], 1e-30))

    @pl.when(step == 0)
    def _():
        proj[...] = x_ref[...].astype(F32)

    proj[...] += dot(att_ref[...], wo_ref[...], 1, 0)

    @pl.when(step == pl.num_programs(0) - 1)
    def _():
        hidden = proj[...]
        scale = lax.rsqrt(jnp.mean(hidden * hidden, -1, keepdims=True) + EPS)
        hid_ref[...] = hidden
        mix_ref[...] = (hidden * scale * gain_ref[...]).astype(BF16)


def attend(facts, base, q, blocks, state, wo=None, x=None, gain=None):
    rows, width = q.shape
    groups = width // 256
    per = PER_STEP
    steps = groups // per
    roles = len(blocks)
    full = lambda shape: pl.BlockSpec(shape, lambda i, *s: (0, 0))
    wide = pl.BlockSpec((rows, 256 * per), lambda i, *s: (0, i))
    heads = pl.BlockSpec((per, 8, rows), lambda i, *s: (i, 0, 0))
    accs = pl.BlockSpec((per, 2, 128, rows), lambda i, *s: (i, 0, 0, 0))
    in_specs = [wide] + [pl.BlockSpec((2, rows, 128 * per), lambda i, *s: (0, 0, i))] * roles
    state_specs = [accs, heads, heads]
    state_shapes = [jax.ShapeDtypeStruct((groups, 2, 128, rows), F32)]
    state_shapes += [jax.ShapeDtypeStruct((groups, 8, rows), F32)] * 2
    args = [*facts, q, *blocks]
    scratch = []
    if state is None:
        body, out_specs, out_shape = attend_start_body, state_specs, state_shapes
    else:
        body = attend_finish_body
        args += [*state, wo, x, gain]
        in_specs += state_specs
        in_specs += [
            pl.BlockSpec((256 * per, x.shape[1]), lambda i, *s: (i, 0)),
            full(x.shape),
            full((1, x.shape[1])),
        ]
        out_specs = [wide, heads, full(x.shape), full(x.shape)]
        out_shape = [
            jax.ShapeDtypeStruct((rows, width), BF16),
            jax.ShapeDtypeStruct((groups, 8, rows), F32),
            jax.ShapeDtypeStruct(x.shape, F32),
            jax.ShapeDtypeStruct(x.shape, BF16),
        ]
        scratch = [
            pltpu.VMEM((per, 2, 128, rows), F32),
            pltpu.VMEM((per, 8, rows), F32),
            pltpu.VMEM((per, 8, rows), F32),
            pltpu.VMEM(x.shape, F32),
        ]
    return pl.pallas_call(
        functools.partial(body, base, roles),
        grid_spec=pltpu.PrefetchScalarGridSpec(
            num_scalar_prefetch=2,
            grid=(steps,),
            in_specs=in_specs,
            out_specs=out_specs,
            scratch_shapes=scratch,
        ),
        out_shape=out_shape,
        compiler_params=params(("arbitrary",)),
        cost_estimate=COST,
        name="attend",
    )(*args)


def attend_back_body(base, roles, diagonal, info_ref, len_ref, q_ref, do_ref, lse_ref, delta_ref, *refs):
    kv_refs, (start_ref, dq_ref), dkv_refs = refs[:roles], refs[-roles - 2 : -roles], refs[-roles:]
    rows = q_ref.shape[0]
    seq_len = len_ref[0]
    if len(refs) > 2 * roles + 1:
        dq_ref[...] = start_ref[...]
    else:
        dq_ref[...] = jnp.zeros_like(dq_ref)
    lane = lax.broadcasted_iota(jnp.int32, (rows, 128), 1)
    low = lane < HEAD_DIM

    def work(role, start, masked):
        if masked:
            bias = mask_of(start, rows, seq_len, diagonal and role == 0)
        for group in range(q_ref.shape[1] // 256):
            lanes = slice(group * 128, group * 128 + 128)
            keys = split_heads(kv_refs[role][0, :, lanes])
            values = split_heads(kv_refs[role][1, :, lanes])
            dks, dvs = [], []
            for pair in range(2):
                cols = slice(256 * group + 128 * pair, 256 * group + 128 * pair + 128)
                q = q_ref[:, cols]
                do = do_ref[:, cols]
                scores = dot(keys[pair], q, 1, 1)
                grads = dot(values[pair], do, 1, 1)
                probs, raws = [], []
                for head in range(2):
                    at = 2 * pair + head
                    part = scores[head * rows : (head + 1) * rows]
                    if masked:
                        part = part + bias
                    prob = jnp.exp2(part - lse_ref[group, at : at + 1, :])
                    grad = grads[head * rows : (head + 1) * rows]
                    raws.append((prob * (grad - delta_ref[group, at : at + 1, :])).astype(BF16))
                    probs.append(prob.astype(BF16))
                raw = jnp.concatenate(raws, 0)
                dq_ref[:, cols] += dot(raw, keys[pair], 0, 0)
                dks.append(dot(raw, q, 1, 0) * (1.0 / LOG2E))
                dvs.append(dot(jnp.concatenate(probs, 0), do, 1, 0))
            for which, parts in enumerate((dks, dvs)):
                top_a, bottom_a = parts[0][:rows], parts[0][rows:]
                top_b, bottom_b = parts[1][:rows], parts[1][rows:]
                turn = pltpu.roll(jnp.where(low, top_b, bottom_a), HEAD_DIM, 1)
                whole = jnp.where(low, top_a, bottom_b) + turn
                dkv_refs[role][which, :, lanes] = whole.astype(dkv_refs[role].dtype)

    for role in range(roles):
        start = info_ref[base + 2 * role]
        active = (info_ref[base + 2 * role + 1] > 0) & (start < seq_len)

        @pl.when(jnp.logical_not(active))
        def _(role=role):
            dkv_refs[role][...] = jnp.zeros_like(dkv_refs[role])

        with_mask(
            active, start, rows, seq_len, diagonal and role == 0, functools.partial(work, role, start)
        )


def attend_back(facts, base, q, do, lse, delta, blocks, before, diagonal):
    rows, width = q.shape
    per = PER_STEP
    steps = width // (256 * per)
    roles = len(blocks)
    kvw = blocks[0].shape[2]
    wide = pl.BlockSpec((rows, 256 * per), lambda i, *s: (0, i))
    heads = pl.BlockSpec((per, 8, rows), lambda i, *s: (i, 0, 0))
    kv = pl.BlockSpec((2, rows, 128 * per), lambda i, *s: (0, 0, i))
    more = [] if before is None else [before]
    return pl.pallas_call(
        functools.partial(attend_back_body, base, roles, diagonal),
        grid_spec=pltpu.PrefetchScalarGridSpec(
            num_scalar_prefetch=2,
            grid=(steps,),
            in_specs=[wide, wide, heads, heads] + [kv] * roles + [wide] * len(more),
            out_specs=[wide] + [kv] * roles,
        ),
        out_shape=[jax.ShapeDtypeStruct((rows, width), F32)]
        + [jax.ShapeDtypeStruct((2, rows, kvw), BF16)] * roles,
        compiler_params=params(("arbitrary",)),
        cost_estimate=cost(40 * rows * rows * roles * width, 16 * 1024 * 1024),
        name="attend_back",
    )(*facts, q, do, lse, delta, *blocks, *more)


def expert_body(base, own, remotes, twins, first, carry, experts, info_ref, len_ref, *refs):
    x_refs, c_refs, wr_ref = refs[:twins], refs[twins : 2 * twins], refs[2 * twins]
    at = 2 * twins + 1
    near = refs[at : at + (3 if own else 0)]
    at += len(near)
    far = refs[at : at + remotes]
    at += remotes
    lead = refs[at : at + (3 if own else 1)]
    at += len(lead)
    before, out_before = (refs[at], refs[at + 1]) if carry else (None, None)
    outs = refs[-15 if first else -13 :]
    gm_ref, gate_ref, out_ref, inner_ref, dg_ref, du_ref = outs[:6]
    copies = outs[6:8] if first else ()
    wbuf, sem, gm_acc, out_acc, gates, back, picked = outs[-7:]
    step = pl.program_id(0)
    total = own + remotes
    rows, width = x_refs[0].shape
    ff = width // 2
    slot = lax.rem(step, 2)
    offsets = (0, width, 2 * width, 2 * width + ff)
    sizes = (width, width, ff, ff)

    def fetch(target, where):
        def start(sources):
            for piece, (ref, off, size) in enumerate(zip(sources, offsets, sizes)):
                pltpu.make_async_copy(
                    ref, wbuf.at[where, pl.ds(off, size)], sem.at[where, piece]
                ).start()

        if own:

            @pl.when(target < own)
            def _():
                down = [near[2].at[target, :, pl.ds(k * ff, ff)] for k in range(2)]
                start([near[0].at[target], near[1].at[target]] + down)

        for i in range(remotes):

            @pl.when(target == own + i)
            def _(i=i):
                start([far[i].at[pl.ds(off, size)] for off, size in zip(offsets, sizes)])

    @pl.when(step + 1 < total)
    def _():
        fetch(step + 1, lax.rem(step + 1, 2))

    lane = lax.broadcasted_iota(jnp.int32, (rows, 128), 1)
    if twins == 2:
        x_ref, cot_ref = picked.at[0, pl.ds(0, rows)], picked.at[1]
    else:
        x_ref, cot_ref = x_refs[0], c_refs[0]

    @pl.when(step == 0)
    def _():
        if twins == 2:
            use = info_ref[base + 3] > 0
            picked[0, :rows] = jnp.where(use, x_refs[0][...], x_refs[1][...])
            picked[1] = jnp.where(use, c_refs[0][...], c_refs[1][...])
        logits = dot(x_ref[...], wr_ref[...], 1, 0)
        mask_t = cot_ref[pl.ds(rows, experts), :rows].astype(F32)
        mask_t = jnp.concatenate([mask_t, jnp.zeros((128 - experts, rows), F32)], 0)
        mask = jnp.transpose(mask_t) > 0.5
        high = jnp.max(jnp.where(mask, logits, NEG), 1, keepdims=True)
        raised = jnp.where(mask, jnp.exp(logits - high), 0.0)
        gates[...] = raised / jnp.sum(raised, 1, keepdims=True)
        gate_ref[...] = gates[...]
        back[...] = jnp.zeros_like(back)
        if carry:
            out_acc[...] = out_before[0].astype(F32)
            gm_acc[...] = before[:rows, :].astype(F32)
        else:
            out_acc[...] = jnp.zeros_like(out_acc)
            gm_acc[...] = jnp.zeros_like(gm_acc)
        if first:
            copies[0][0] = x_ref[...]
            copies[1][0] = cot_ref[pl.ds(0, rows), :]

    def expert(wg, wu, wd0, wd1):
        which = info_ref[base + 2] + info_ref[base + 4 + step]
        x = x_ref[...]
        cot = cot_ref[pl.ds(0, rows), :]
        g = dot(x, wg, 1, 0)
        u = dot(x, wu, 1, 0)
        raw = dot(cot[:, :ff], wd0, 1, 1) + dot(cot[:, ff:], wd1, 1, 1)
        gate = jnp.sum(jnp.where(lane == which, gates[...], 0.0), 1, keepdims=True)
        sig = 1.0 / (1.0 + jnp.exp(-g))
        silu = g * sig
        inner = silu * u
        gg = jnp.sum(raw * inner, 1, keepdims=True)
        back[...] += jnp.where(lane == which, gg, 0.0)
        scaled = (gate * inner).astype(BF16)
        gi = gate * raw
        dg = (gi * u * (sig * (1.0 + g * (1.0 - sig)))).astype(BF16)
        du = (gi * silu).astype(BF16)
        inner_ref[0] = scaled
        dg_ref[0] = dg
        du_ref[0] = du
        out_acc[:, :ff] += dot(scaled, wd0, 1, 0)
        out_acc[:, ff:] += dot(scaled, wd1, 1, 0)
        gm_acc[...] += dot(dg, wg, 1, 1) + dot(du, wu, 1, 1)

    @pl.when(step == 0)
    def _():
        if own:
            down = lead[2][0]
            expert(lead[0][0], lead[1][0], down[:, :ff], down[:, ff:])
        else:
            expert(*(lead[0][off : off + size] for off, size in zip(offsets, sizes)))

    @pl.when(step > 0)
    def _():
        for piece, (off, size) in enumerate(zip(offsets, sizes)):
            place = wbuf.at[slot, pl.ds(off, size)]
            pltpu.make_async_copy(place, place, sem.at[slot, piece]).wait()
        expert(*(wbuf[slot, off : off + size, :] for off, size in zip(offsets, sizes)))

    @pl.when(step == total - 1)
    def _():
        tail = jnp.transpose(back[...])[:experts, :]
        tail = jnp.concatenate([tail, jnp.zeros((experts, width - rows), F32)], 1)
        if carry:
            tail = tail + before[rows:, :].astype(F32)
        gm_ref[:rows, :] = gm_acc[...].astype(BF16)
        gm_ref[rows:, :] = tail.astype(BF16)
        out_ref[0] = out_acc[...].astype(BF16)


def expert_call(facts, base, xs, cots, wr, own_weights, far, experts, kept, before=None):
    rows, width = xs[0].shape
    own = own_weights[0].shape[0] if own_weights else 0
    remotes = len(far)
    total = own + remotes
    twins = len(xs)
    carry = before is not None
    first = not carry
    ff = width // 2
    full = lambda shape: pl.BlockSpec(shape, lambda i, *s: (0,) * len(shape))
    anywhere = pl.BlockSpec(memory_space=pl.ANY)
    big = pl.BlockSpec((1, rows, width), lambda i, s, n: (s[base + 1], 0, 0))
    part = pl.BlockSpec((1, rows, ff), lambda i, s, n: (s[base + 1], 0, s[base + 4 + i]))
    count = 6 if first else 4
    fresh = isinstance(kept[0], jax.ShapeDtypeStruct)
    aliased = [] if fresh else list(kept[:count])
    lead = list(own_weights) if own else [far[0]]
    inputs = [*xs, *cots, wr, *own_weights, *far, *lead] + ([before] if carry else [])
    specs = [full((rows, width))] * twins + [full(cots[0].shape)] * twins + [full(wr.shape)]
    specs += [anywhere] * (len(own_weights) + remotes)
    specs += [full((1,) + w.shape[1:] if own else w.shape) for w in lead]
    specs += [full(before.shape)] if carry else []
    specs += [big if carry and k == 0 else anywhere for k in range(len(aliased))]
    gm_shape = (rows + experts, width)
    outs = pl.pallas_call(
        functools.partial(expert_body, base, own, remotes, twins, first, carry, experts),
        grid_spec=pltpu.PrefetchScalarGridSpec(
            num_scalar_prefetch=2,
            grid=(total,),
            in_specs=specs,
            out_specs=[full(gm_shape), full((rows, 128)), big, part, part, part]
            + ([big, big] if first else []),
            scratch_shapes=[
                pltpu.VMEM((2, 3 * width, ff), BF16),
                pltpu.SemaphoreType.DMA((2, 4)),
                pltpu.VMEM((rows, width), F32),
                pltpu.VMEM((rows, width), F32),
                pltpu.VMEM((rows, 128), F32),
                pltpu.VMEM((rows, 128), F32),
                pltpu.VMEM((2,) + gm_shape, BF16),
            ],
        ),
        out_shape=[
            jax.ShapeDtypeStruct(gm_shape, BF16),
            jax.ShapeDtypeStruct((rows, 128), F32),
        ]
        + [jax.ShapeDtypeStruct(k.shape, k.dtype) for k in kept[:count]],
        input_output_aliases={2 + len(inputs) + k: 2 + k for k in range(len(aliased))},
        compiler_params=params(("arbitrary",)),
        cost_estimate=COST
        if not far
        else cost(12 * rows * width * ff * total, total * 6 * width * ff),
        name="experts",
    )(*facts, *inputs, *aliased)
    return outs[0], outs[1], tuple(outs[2:]) + tuple(kept[count:])


def expert_grads_body(base, info_ref, len_ref, x_hbm, c_hbm, in_hbm, dg_hbm, du_hbm, o_ref, x, c, cols, sem):
    place, kind = pl.program_id(0), pl.program_id(1)
    step = place * 3 + kind
    ff = cols.shape[2]
    hidden = (dg_hbm, du_hbm, in_hbm)

    def fetch(target, start):
        at = lax.rem(target, 2)
        off = pl.ds(pl.multiple_of(info_ref[base + lax.div(target, 3)] * ff, 128), ff)
        for k, ref in enumerate(hidden):

            @pl.when(lax.rem(target, 3) == k)
            def _(ref=ref):
                pltpu.make_async_copy(ref.at[:, off], cols.at[at], sem.at[at]).start()

    @pl.when(step == 0)
    def _():
        pltpu.make_async_copy(x_hbm, x, sem.at[2]).start()
        fetch(step, True)
        pltpu.make_async_copy(c_hbm, c, sem.at[3]).start()
        pltpu.make_async_copy(x_hbm, x, sem.at[2]).wait()

    @pl.when(step + 1 < 3 * pl.num_programs(0))
    def _():
        fetch(step + 1, True)

    slot = lax.rem(step, 2)
    pltpu.make_async_copy(cols.at[slot], cols.at[slot], sem.at[slot]).wait()

    @pl.when(kind < 2)
    def _():
        o_ref[0, 0] = dot(x[...], cols[slot], 0, 0).astype(BF16)

    @pl.when(step == 2)
    def _():
        pltpu.make_async_copy(c_hbm, c, sem.at[3]).wait()

    @pl.when(kind == 2)
    def _():
        o_ref[0, 0, :ff] = dot(cols[slot], c[:, :ff], 0, 0).astype(BF16)
        o_ref[0, 0, ff:] = dot(cols[slot], c[:, ff:], 0, 0).astype(BF16)


def expert_grads(facts, base, count, x, c, inner, dg, du):
    rows, width = x.shape
    ff = width // 2
    anywhere = pl.BlockSpec(memory_space=pl.ANY)
    return pl.pallas_call(
        functools.partial(expert_grads_body, base),
        grid_spec=pltpu.PrefetchScalarGridSpec(
            num_scalar_prefetch=2,
            grid=(count, 3),
            in_specs=[anywhere] * 5,
            out_specs=pl.BlockSpec((1, 1, width, ff), lambda i, k, *s: (i, k, 0, 0)),
            scratch_shapes=[
                pltpu.VMEM((rows, width), BF16),
                pltpu.VMEM((rows, width), BF16),
                pltpu.VMEM((2, rows, ff), BF16),
                pltpu.SemaphoreType.DMA((4,)),
            ],
        ),
        out_shape=jax.ShapeDtypeStruct((count, 3, width, ff), BF16),
        compiler_params=params(("arbitrary",) * 2),
        cost_estimate=cost(6 * rows * width * ff * count, 16 * 1024 * 1024),
        name="expert_grads",
    )(*facts, x, c, inner, dg, du)


def middle_body(experts, *refs):
    sums, ends, refs = refs[:4], refs[4:8], refs[8:]
    gate_ref, wr_ref, hid_ref, cot_ref, att_ref, mix_ref, gain_ref, wo_hbm = refs[:8]
    gh_ref, gb_ref, do_ref, delta_ref, ffn_ref, router_ref, wo, sem, deltas, logit = refs[8:]
    step = pl.program_id(0)
    part, width = hid_ref.shape
    rows = gate_ref.shape[0]
    span = pl.ds(pl.multiple_of(step * part, part), part)

    @pl.when(step == 0)
    def _():
        pltpu.make_async_copy(wo_hbm, wo, sem).start()
        ffn_ref[...] = jnp.zeros_like(ffn_ref)
        router_ref[...] = jnp.zeros_like(router_ref)
        gg = ends[0][:, :rows].astype(F32)
        for ref in ends[1:]:
            gg = gg + ref[:, :rows].astype(F32)
        gg = jnp.transpose(jnp.concatenate([gg, jnp.zeros((128 - experts, rows), F32)], 0))
        gates = gate_ref[...]
        logit[...] = (gates * (gg - jnp.sum(gates * gg, 1, keepdims=True))).astype(BF16)

    total = sums[0][...].astype(F32)
    for ref in sums[1:]:
        total = total + ref[...].astype(F32)
    gl = logit[span, :]
    router_ref[...] += dot(gl, mix_ref[...], 0, 0)
    hidden = hid_ref[...]
    grad_mixed = total + dot(gl, wr_ref[...], 1, 1)
    scale = lax.rsqrt(jnp.mean(hidden * hidden, -1, keepdims=True) + EPS)
    ffn_ref[...] += jnp.sum(grad_mixed * hidden * scale, 0, keepdims=True)
    weighted = grad_mixed * gain_ref[...]
    mean = jnp.mean(weighted * hidden, -1, keepdims=True)
    grad = cot_ref[...].astype(F32) + scale * weighted - hidden * (scale * scale * scale * mean)
    gh_ref[...] = grad
    low = grad.astype(BF16)
    gb_ref[...] = low

    @pl.when(step == 0)
    def _():
        pltpu.make_async_copy(wo_hbm, wo, sem).wait()

    do = dot(low, wo[...], 1, 1).astype(BF16)
    do_ref[...] = do
    both = do.astype(F32) * att_ref[...].astype(F32)
    lane = lax.broadcasted_iota(jnp.int32, (part, 128), 1)
    found = jnp.zeros((part, 128), F32)
    for block in range(both.shape[1] // 128):
        pair = both[:, block * 128 : block * 128 + 128]
        front = jnp.sum(jnp.where(lane < HEAD_DIM, pair, 0.0), 1, keepdims=True)
        back = jnp.sum(jnp.where(lane < HEAD_DIM, 0.0, pair), 1, keepdims=True)
        found = jnp.where(lane == 2 * block, front, found)
        found = jnp.where(lane == 2 * block + 1, back, found)
    deltas[span, :] = found

    @pl.when(step == pl.num_programs(0) - 1)
    def _():
        turned = jnp.transpose(deltas[...])
        for group in range(delta_ref.shape[0]):
            delta_ref[group, :4, :] = turned[4 * group : 4 * group + 4]
            delta_ref[group, 4:, :] = jnp.zeros((4, rows), F32)


def middle(sums, gates, wr, hidden, cot_ext, attended, mixed, gain, wo, experts):
    rows, width = hidden.shape
    steps = 1
    heads = attended.shape[1] // HEAD_DIM
    row = lambda w: pl.BlockSpec((rows // steps, w), lambda i: (i, 0))
    end = pl.BlockSpec((experts, width), lambda i: (rows // experts, 0))
    full = lambda shape: pl.BlockSpec(shape, lambda i: (0,) * len(shape))
    return pl.pallas_call(
        functools.partial(middle_body, experts),
        grid=(steps,),
        in_specs=[row(width)] * 4
        + [end] * 4
        + [
            full((rows, 128)),
            full(wr.shape),
            row(width),
            row(width),
            row(attended.shape[1]),
            row(width),
            full((1, width)),
            pl.BlockSpec(memory_space=pl.ANY),
        ],
        out_specs=[
            row(width),
            row(width),
            row(attended.shape[1]),
            full((heads // 4, 8, rows)),
            full((1, width)),
            full((128, width)),
        ],
        out_shape=[
            jax.ShapeDtypeStruct((rows, width), F32),
            jax.ShapeDtypeStruct((rows, width), BF16),
            jax.ShapeDtypeStruct(attended.shape, BF16),
            jax.ShapeDtypeStruct((heads // 4, 8, rows), F32),
            jax.ShapeDtypeStruct((1, width), F32),
            jax.ShapeDtypeStruct((128, width), F32),
        ],
        scratch_shapes=[
            pltpu.VMEM(wo.shape, BF16),
            pltpu.SemaphoreType.DMA(()),
            pltpu.VMEM((rows, 128), F32),
            pltpu.VMEM((rows, 128), BF16),
        ],
        compiler_params=params(("arbitrary",)),
        cost_estimate=COST,
        name="middle",
    )(*sums, *sums, gates, wr, hidden, cot_ext, attended, mixed, gain, wo)


def early_body(experts, info_ref, len_ref, att_ref, gb_ref, router_ref, ffn_ref, give_ref, keep_ref):
    size = att_ref.shape[1] // 2
    core = info_ref[0]
    width = gb_ref.shape[1]
    row = lax.broadcasted_iota(jnp.int32, (16, width), 0)
    extra = jnp.concatenate([router_ref[:experts], jnp.where(row == 0, ffn_ref[...], 0.0)], 0)
    for ref, half in ((keep_ref, core), (give_ref, 1 - core)):
        part = att_ref[:, pl.ds(pl.multiple_of(half * size, 128), size)]
        ref[:size] = dot(part, gb_ref[...], 0, 0).astype(BF16)
        ref[size : size + experts + 16] = jnp.where(half == 0, extra, 0.0).astype(BF16)
        rest = ref.shape[0] - (size + experts + 16)
        ref[size + experts + 16 :] = jnp.zeros((rest, width), BF16)


def early_grads(facts, attended, gb, router, ffn, experts):
    rows, width = gb.shape
    count = attended.shape[1]
    col = lambda r: pl.BlockSpec((r, 512), lambda i, *s: (0, i))
    size = count // 2 + count // 8
    return pl.pallas_call(
        functools.partial(early_body, experts),
        grid_spec=pltpu.PrefetchScalarGridSpec(
            num_scalar_prefetch=2,
            grid=(width // 512,),
            in_specs=[
                pl.BlockSpec(attended.shape, lambda i, *s: (0, 0)),
                col(rows),
                col(router.shape[0]),
                col(1),
            ],
            out_specs=[col(size)] * 2,
        ),
        out_shape=[jax.ShapeDtypeStruct((size, width), BF16)] * 2,
        compiler_params=params(("arbitrary",)),
        cost_estimate=COST,
        name="early_grads",
    )(*facts, attended, gb, router, ffn)


def rope_back(g, cos_ref, sin_ref):
    cos = jnp.concatenate([cos_ref[...]] * (g.shape[1] // 128), 1)
    sin = jnp.concatenate([sin_ref[...]] * (g.shape[1] // 128), 1)
    return g * cos - swap_halves(g, lambda v, s: pltpu.roll(v, s, 1)) * sin


def split_rows(core, n_ref, lin, give_ref, keep_ref):
    size = n_ref.shape[1] // 2
    for ref, half in ((give_ref, 1 - core), (keep_ref, core)):
        part = n_ref[:, pl.ds(pl.multiple_of(half * size, 128), size)]
        ref[...] = dot(part, lin, 0, 0).astype(BF16)


def query_back_body(info_ref, len_ref, dq_ref, n_ref, cos_ref, sin_ref, lin_ref, give_ref, keep_ref):
    lin = rope_back(dq_ref[...] * HEAD_DIM**-0.5, cos_ref, sin_ref).astype(BF16)
    lin_ref[...] = lin
    split_rows(info_ref[0], n_ref, lin, give_ref, keep_ref)


def query_back(facts, dq, normed, cos, sin):
    rows, width = dq.shape
    col = lambda r: pl.BlockSpec((r, 512), lambda i, *s: (0, i))
    full = lambda shape: pl.BlockSpec(shape, lambda i, *s: (0, 0))
    size = normed.shape[1] // 2
    return pl.pallas_call(
        query_back_body,
        grid_spec=pltpu.PrefetchScalarGridSpec(
            num_scalar_prefetch=2,
            grid=(width // 512,),
            in_specs=[col(rows), full(normed.shape), full(cos.shape), full(sin.shape)],
            out_specs=[col(rows), col(size), col(size)],
        ),
        out_shape=[
            jax.ShapeDtypeStruct((rows, width), BF16),
            jax.ShapeDtypeStruct((size, width), BF16),
            jax.ShapeDtypeStruct((size, width), BF16),
        ],
        compiler_params=params(("arbitrary",)),
        cost_estimate=cost(2 * rows * width * width, 8 * 1024 * 1024),
        name="query_back",
    )(*facts, dq, normed, cos, sin)


def pair_back_body(parts, half_steps, info_ref, len_ref, *refs):
    n_ref, cos_ref, sin_ref, lin_ref, give_ref, keep_ref = refs[parts:]
    step = pl.program_id(0)
    total = refs[0][0].astype(F32)
    for ref in refs[1:parts]:
        total = total + ref[0].astype(F32)

    @pl.when(step < half_steps)
    def _():
        lin_ref[...] = rope_back(total, cos_ref, sin_ref).astype(BF16)

    @pl.when(step >= half_steps)
    def _():
        lin_ref[...] = total.astype(BF16)

    split_rows(info_ref[0], n_ref, lin_ref[...], give_ref, keep_ref)


def pair_back(facts, parts, normed, cos, sin):
    _, rows, kvw = parts[0].shape
    half_steps = kvw // 512
    col = lambda r: pl.BlockSpec((r, 512), lambda i, *s: (0, i))
    full = lambda shape: pl.BlockSpec(shape, lambda i, *s: (0, 0))
    part = pl.BlockSpec((1, rows, 512), lambda i, *s: (i // half_steps, 0, i % half_steps))
    size = normed.shape[1] // 2
    return pl.pallas_call(
        functools.partial(pair_back_body, len(parts), half_steps),
        grid_spec=pltpu.PrefetchScalarGridSpec(
            num_scalar_prefetch=2,
            grid=(2 * half_steps,),
            in_specs=[part] * len(parts) + [full(normed.shape), full(cos.shape), full(sin.shape)],
            out_specs=[col(rows), col(size), col(size)],
        ),
        out_shape=[
            jax.ShapeDtypeStruct((rows, 2 * kvw), BF16),
            jax.ShapeDtypeStruct((size, 2 * kvw), BF16),
            jax.ShapeDtypeStruct((size, 2 * kvw), BF16),
        ],
        compiler_params=params(("arbitrary",)),
        cost_estimate=COST,
        name="pair_back",
    )(*facts, *parts, normed, cos, sin)


def tokens_back_body(lq_ref, lkv_ref, wq_ref, wk_ref, wv_ref, x_ref, gh_ref, gain_ref, o_ref):
    kvw = wk_ref.shape[1]
    grad = dot(lq_ref[...], wq_ref[...], 1, 1)
    grad = grad + dot(lkv_ref[:, :kvw], wk_ref[...], 1, 1)
    grad = grad + dot(lkv_ref[:, kvw:], wv_ref[...], 1, 1)
    x = x_ref[...].astype(F32)
    scale = lax.rsqrt(jnp.mean(x * x, -1, keepdims=True) + EPS)
    weighted = grad * gain_ref[...]
    mean = jnp.mean(weighted * x, -1, keepdims=True)
    total = gh_ref[...] + scale * weighted - x * (scale * scale * scale * mean)
    o_ref[...] = total.astype(BF16)


def tokens_back(lq, lkv, wq, wk, wv, x, gh, gain):
    rows, width = x.shape
    row = lambda w: pl.BlockSpec((rows, w), lambda i: (i, 0))
    full = lambda shape: pl.BlockSpec(shape, lambda i: (0, 0))
    return pl.pallas_call(
        tokens_back_body,
        grid=(1,),
        in_specs=[
            row(lq.shape[1]),
            row(lkv.shape[1]),
            full(wq.shape),
            full(wk.shape),
            full(wv.shape),
            row(width),
            row(width),
            full((1, width)),
        ],
        out_specs=row(width),
        out_shape=jax.ShapeDtypeStruct((rows, width), BF16),
        compiler_params=params(("arbitrary",)),
        cost_estimate=COST,
        name="tokens_back",
    )(lq, lkv, wq, wk, wv, x, gh, gain)


def finish_body(info_ref, len_ref, qa, qb, pa, pb, wq_ref, wk_ref, wv_ref, gain_ref, q_ref, k_ref, v_ref, n_ref):
    mine = pl.program_id(0) // (pl.num_programs(0) // 2) == info_ref[0]
    q = jnp.where(mine, qa[...].astype(F32), qb[...].astype(F32))
    pair = jnp.where(mine, pa[...].astype(F32), pb[...].astype(F32))
    kvw = k_ref.shape[1]
    q_ref[...] = q
    k_ref[...] = pair[:, :kvw]
    v_ref[...] = pair[:, kvw:]
    gain = jnp.sum(q * wq_ref[...].astype(F32), 1, keepdims=True)
    gain = gain + jnp.sum(pair[:, :kvw] * wk_ref[...].astype(F32), 1, keepdims=True)
    gain = gain + jnp.sum(pair[:, kvw:] * wv_ref[...].astype(F32), 1, keepdims=True)
    turned = jnp.transpose(jnp.broadcast_to(gain, (gain.shape[0], 128)))
    n_ref[...] = turned[:1] / gain_ref[...]


def finish(facts, qa, qb, pa, pb, wq, wk, wv, gain):
    width = wq.shape[0]
    part = width // 2
    half = lambda w: pl.BlockSpec((part, w), lambda i, *s: (0, 0))
    row = lambda w: pl.BlockSpec((part, w), lambda i, *s: (i, 0))
    line = pl.BlockSpec((1, part), lambda i, *s: (0, i))
    return pl.pallas_call(
        finish_body,
        grid_spec=pltpu.PrefetchScalarGridSpec(
            num_scalar_prefetch=2,
            grid=(2,),
            in_specs=[half(width)] * 4
            + [row(wq.shape[1]), row(wk.shape[1]), row(wv.shape[1]), line],
            out_specs=[row(wq.shape[1]), row(wk.shape[1]), row(wv.shape[1]), line],
        ),
        out_shape=[
            jax.ShapeDtypeStruct(wq.shape, F32),
            jax.ShapeDtypeStruct(wk.shape, F32),
            jax.ShapeDtypeStruct(wv.shape, F32),
            jax.ShapeDtypeStruct((1, width), F32),
        ],
        compiler_params=params(("arbitrary",)),
        cost_estimate=COST,
        name="finish",
    )(*facts, qa, qb, pa, pb, wq, wk, wv, gain)


def total_of(parts):
    total = parts[0].astype(F32)
    for part in parts[1:]:
        total = total + part.astype(F32)
    return total.astype(BF16)


def scatter_start(buf, axis):
    name, size, pos, pairs = axis
    rows = buf.shape[0] // size
    take = lambda k: lax.dynamic_slice_in_dim(buf, k * rows, rows, 0)
    parts = [take(pos)]
    for shift in range(1, size):
        parts.append(lax.ppermute(take((pos + shift) % size), name, pairs(shift)))
    return parts


def gather_start(buf, axis):
    name, size, pos, pairs = axis
    return [lax.ppermute(buf, name, pairs(shift)) for shift in range(size - 1, 0, -1)] + [buf]


def gather_end(order, axis):
    name, size, pos, pairs = axis
    rows = order[0].shape[0]
    if size == 2:
        pick = lambda a, b: jnp.concatenate([a, b], 0)
        return jnp.where(pos == 0, pick(order[1], order[0]), pick(order[0], order[1]))
    double = jnp.concatenate(order + order[:-1], 0)
    return lax.dynamic_slice_in_dim(double, (size - 1 - pos) * rows, size * rows, 0)


def device_facts(nx, ny, own, rows, ep_index, ctx_index):
    group = nx * own
    table = np.zeros((NZ * nx, ny * CORES, 160), np.int32)
    for ep in range(NZ * nx):
        for ctx in range(ny * CORES):
            z, x, y, core = ep // nx, ep % nx, ctx // CORES, ctx % CORES
            out = table[ep, ctx]
            out[0], out[1] = core, ctx
            out[16:20] = ctx * rows, 1, (ctx - 1) * rows, core
            for back in range(1, ny):
                at, block = 16 + 4 * back, (y - back) * CORES
                out[at : at + 4] = (block + core) * rows, y >= back, (block + 1 - core) * rows, y >= back
            near = [x * own + i for i in range(own)]
            far = [(x - s) % nx * own + i for s in range(1, nx) for i in (core, 1 - core)]
            shard_c, shard_d, inside = (2, 2, 1, 1)[z], (3, 3, 0, 0)[z], int(z in (1, 2))
            calls = [(z, 1, near), (z, 1, far), (z ^ 1, 1, near + far)]
            calls += [(shard_c, inside, near + far), (shard_d, inside, near + far)]
            for k, (shard, pick, places) in enumerate(calls):
                out[48 + 16 * k : 52 + 16 * k] = 0, shard, z * group, pick
                out[52 + 16 * k : 52 + 16 * k + len(places)] = places
            for j in range(nx):
                out[128 + j] = (x + j) % nx * own + 1 - core
                out[144 + j] = (x + j) % nx * own + core
    line = lax.dynamic_slice(
        jnp.asarray(table), (ep_index, ctx_index, jnp.int32(0)), (1, 1, table.shape[2])
    )
    return line.reshape(-1)


def local(
    tokens,
    lengths,
    routes,
    cotangent,
    attn_norm,
    w_query,
    w_key,
    w_value,
    w_out,
    ffn_norm,
    w_router,
    expert_gate_weight,
    expert_up_weight,
    expert_down_weight,
):
    rows, width = tokens.shape[1:]
    half = rows // 2
    experts = w_router.shape[1]
    own = expert_gate_weight.shape[0]
    ff = expert_gate_weight.shape[2]
    kvw = w_key.shape[1]
    ctx_size, ep_size = lax.axis_size("ctx"), lax.axis_size("ep")
    ny, nx = ctx_size // CORES, ep_size // NZ
    ctx_index, ep_index = lax.axis_index("ctx"), lax.axis_index("ep")
    y, core = ctx_index // CORES, ctx_index % CORES
    z, xpos = ep_index // nx, ep_index % nx
    seq_len = lengths[0]
    tokens = tokens[0]
    valid_flag = ctx_index * rows + jnp.arange(rows, dtype=jnp.int32) < seq_len
    valid = valid_flag.astype(F32)[:, None]
    tie = lax.optimization_barrier

    core_swap = [(c, c ^ 1) for c in range(ctx_size)]
    core_up = [(c, c + 1) for c in range(0, ctx_size, CORES)]
    core_down = [(c + 1, c) for c in range(0, ctx_size, CORES)]
    y_up = lambda k: [(c, c + CORES * k) for c in range(ctx_size - CORES * k)]
    y_down = lambda k: [(b, a) for a, b in y_up(k)]
    zx = lambda pairs: [(a * nx + i, b * nx + i) for a, b in pairs for i in range(nx)]
    z_groups = [[i + nx * k for k in range(NZ)] for i in range(nx)]
    x_shift = lambda s: [(k * nx + i, k * nx + (i + s) % nx) for k in range(NZ) for i in range(nx)]
    y_ring = lambda s: [(c, (c + CORES * s) % ctx_size) for c in range(ctx_size)]
    core_axis = ("ctx", CORES, core, lambda s: core_swap)
    y_axis = ("ctx", ny, y, y_ring)
    x_axis = ("ep", nx, xpos, x_shift)
    z_axis = ("ep", NZ, z, lambda s: zx([(k, (k + s) % NZ) for k in range(NZ)]))

    weights = (expert_gate_weight, expert_up_weight, expert_down_weight)
    facts = (device_facts(nx, ny, own, rows, ep_index, ctx_index), lengths)
    cot_ext, sent = prepare(facts, routes[0].T, cotangent[0], weights, experts)
    arrived = [lax.ppermute(sent, "ep", x_shift(shift)) for shift in range(1, nx)]

    swap, mid, out = [(0, 1), (1, 0), (2, 3), (3, 2)], [(1, 2), (2, 1)], [(1, 0), (2, 3)]
    cot_near = lax.ppermute(cot_ext, "ep", zx(swap))
    cot_middle = lax.ppermute(cot_ext, "ep", zx(mid))
    tokens, cot_ext, sent = tie((tokens, cot_ext, sent))
    fine, starts = rope_constants(ctx_size, rows)
    normed, q, kv, cos, sin = project(
        facts, tokens, attn_norm[None], w_query, w_key, w_value, fine, starts, ctx_size
    )

    blocks = [kv, lax.ppermute(kv, "ctx", core_up)]
    travelling = kv
    for back in range(1, ny):
        travelling = lax.ppermute(travelling, "ctx", y_up(1))
        blocks.append(travelling)
    near_row, far_row = 16, 20
    state = attend(facts, near_row, q, blocks[:2], None)
    came, state, cot_near, cot_middle = tie((blocks[2:], state, cot_near, cot_middle))
    cot_across = lax.ppermute(cot_near, "ep", zx(mid))
    cot_outward = lax.ppermute(cot_middle, "ep", zx(out))
    blocks = blocks[:2]
    for piece in came:
        blocks += [piece, lax.ppermute(piece, "ctx", core_swap)]
    attended, lse, hidden, mixed = attend(
        facts, far_row, q, blocks[2:], state, w_out, tokens, ffn_norm[None]
    )

    wr = jnp.pad(w_router, ((0, 0), (0, 128 - experts)))
    group = nx * own
    widths = (width, group * ff, group * ff, group * ff, width, width)
    kept = tuple(jax.ShapeDtypeStruct((NZ, rows, w), BF16) for w in widths)

    def run(call, data, cots, near, far, kept, before=None):
        return expert_call(
            facts, 48 + 16 * call, data, cots, wr, near, far, experts, kept, before
        )

    ends, away = [(0, 1), (3, 2)], [(2, 3), (1, 0)]
    near = lax.ppermute(mixed, "ep", zx(swap))
    middle_rows = lax.ppermute(mixed, "ep", zx(mid))
    mixed, cot_across, cot_outward = tie((mixed, cot_across, cot_outward))
    gm_a, gates, kept = run(0, (mixed,), (cot_ext,), weights, [], kept)
    near, middle_rows, arrived, kept = tie((near, middle_rows, arrived, kept))
    across = lax.ppermute(near, "ep", zx(mid))
    outward = lax.ppermute(middle_rows, "ep", zx(out))
    far = []
    for piece in arrived:
        far += [piece, lax.ppermute(piece, "ctx", core_swap)]
    gm_a, _, kept = run(1, (mixed,), (cot_ext,), (), far, kept, gm_a)
    across, outward, kept = tie((across, outward, kept))
    last = lax.ppermute(across, "ep", zx(out))
    gm_b, _, kept = run(2, (near,), (cot_near,), weights, far, kept)
    third = lax.ppermute(gm_b, "ep", zx(ends))
    last, kept, cot_across = tie((last, kept, cot_across))
    cot_last = lax.ppermute(cot_across, "ep", zx(out))
    cots = (cot_middle, cot_outward)
    gm_c, _, kept = run(3, (middle_rows, outward), cots, weights, far, kept)
    second = lax.ppermute(gm_c, "ep", zx(ends))
    third, cot_last, kept = tie((third, cot_last, kept))
    cots = (cot_across, cot_last)
    gm_d, _, kept = run(4, (across, last), cots, weights, far, kept)
    first = lax.ppermute(gm_d, "ep", zx(ends))

    add = lambda a, b: (a.astype(F32) + b.astype(F32)).astype(BF16)
    line = lambda a: a.reshape(NZ * rows, a.shape[2])
    saved = lambda kept: [line(kept[k]) for k in (4, 5, 1, 2, 3)]
    second, kept = tie((second, kept))
    turned = lax.ppermute(add(gm_c, second), "ep", zx(mid))
    give = expert_grads(facts, 128, nx, *saved(kept))
    first, turned, give, kept = tie((first, turned, give, kept))
    carried = lax.ppermute(add(gm_d, first), "ep", zx(mid))
    came = lax.ppermute(give, "ctx", core_swap)
    keep = expert_grads(facts, 144, nx, *saved(kept))
    carried, keep, came = tie((carried, keep, came))
    send, keep, came = tie((add(gm_b, carried), keep, came))
    final = lax.ppermute(send, "ep", zx(away))
    total = [[add(keep[j, 0], came[j, 0]) for j in range(nx)]]
    total, keep, came = tie((total, keep, came))
    total += [[add(keep[j, k], came[j, k]) for j in range(nx)] for k in (1, 2)]
    over_x = lambda k: [lax.ppermute(total[k][s], "ep", x_shift(s)) for s in range(1, nx)]
    x_came = [over_x(0)]

    sums = [gm_a, third, turned, final]
    gh, gb, do, delta, grad_ffn, grad_router = middle(
        sums, gates, wr, hidden, cot_ext, attended, mixed, ffn_norm[None], w_out, experts
    )
    give, early = early_grads(facts, attended, gb, grad_router, grad_ffn, experts)
    give, early, do, x_came = tie((give, early, do, x_came))

    y_parts = [scatter_start(total_of([total[0][0]] + x_came[0]), y_axis)]
    x_came.append(over_x(1))
    early = [early, lax.ppermute(give, "ctx", core_swap)]
    dq = None
    far_dkv = []
    if ny > 1:
        dq, *far_dkv = attend_back(facts, far_row, q, do, lse, delta, blocks[2:], None, False)
    dq, far_dkv, y_parts, x_came, early = tie((dq, far_dkv, y_parts, x_came, early))

    homeward = [
        lax.ppermute(add(far_dkv[2 * k], lax.ppermute(far_dkv[2 * k + 1], "ctx", core_swap)), "ctx", y_down(k + 1))
        for k in range(ny - 1)
    ]
    x_came.append(over_x(2))
    early = scatter_start(total_of(early), z_axis)
    dq, *near_dkv = attend_back(facts, near_row, q, do, lse, delta, blocks[:2], dq, True)
    dq, homeward, x_came, near_dkv, early, out_all = tie(
        (dq, homeward, x_came, near_dkv, early, kept[0])
    )
    expert_sum = lax.psum_scatter(
        line(out_all), "ep", scatter_dimension=0, axis_index_groups=z_groups, tiled=True
    )

    parts = [near_dkv[0], lax.ppermute(near_dkv[1], "ctx", core_down), *homeward]
    y_parts.append(scatter_start(total_of([total[1][0]] + x_came[1]), y_axis))
    early = scatter_start(total_of(early), x_axis)
    lin_q, give, keep = query_back(facts, dq, normed, cos, sin)
    parts, lin_q, give, keep = tie((parts, lin_q, give, keep))

    half_q = [keep, lax.ppermute(give, "ctx", core_swap)]
    lin_kv, give, keep = pair_back(facts, parts, normed, cos, sin)
    half_q, lin_kv, give, keep, early = tie((half_q, lin_kv, give, keep, early))

    half_kv = [keep, lax.ppermute(give, "ctx", core_swap)]
    one = scatter_start(total_of(half_q), y_axis)
    two = scatter_start(total_of(half_kv), x_axis)
    grad_tokens = tokens_back(
        lin_q, lin_kv, w_query, w_key, w_value, tokens, gh, attn_norm[None]
    )
    one, two, early, grad_tokens, y_parts, x_came = tie(
        (one, two, early, grad_tokens, y_parts, x_came)
    )
    one = scatter_start(total_of(one), x_axis)
    two = scatter_start(total_of(two), y_axis)
    early = scatter_start(total_of(early), y_axis)
    y_parts.append(scatter_start(total_of([total[2][0]] + x_came[2]), y_axis))
    one, two, early = tie((one, two, early))
    early = gather_start(total_of(early), y_axis)
    both = scatter_start(jnp.concatenate([total_of(one), total_of(two)], 0), z_axis)
    grads = [gather_start(total_of(y_parts[0]), y_axis)]
    both, early, y_parts = tie((both, early, y_parts))
    both = gather_start(total_of(both), z_axis)
    early = gather_start(gather_end(early, y_axis), x_axis)
    grads.append(gather_start(total_of(y_parts[1]), y_axis))
    both, early, grads[0], expert_sum = tie((both, early, grads[0], expert_sum))
    early = gather_end(early, x_axis)
    hop = [lax.ppermute(early, "ep", zx(swap)), lax.ppermute(early, "ep", zx(mid))]
    both = gather_end(both, z_axis)
    size = both.shape[0] // 2
    one, two = gather_start(both[:size], x_axis), gather_start(both[size:], y_axis)
    result_out = (valid * (hidden + expert_sum.astype(F32))).astype(BF16)
    one, two, result_out, grads, hop = tie((one, two, result_out, grads, hop))
    hop2 = [lax.ppermute(hop[0], "ep", zx(mid)), lax.ppermute(hop[1], "ep", zx(out))]
    one = gather_start(gather_end(one, x_axis), y_axis)
    two = gather_start(gather_end(two, y_axis), x_axis)
    whole = lambda g: gather_end(gather_start(gather_end(g, y_axis)[None], core_axis), core_axis)
    ready = [whole(g).reshape(own, width, ff).astype(F32) for g in grads]
    grads = gather_start(total_of(y_parts[2]), y_axis)
    one, two, ready, hop2 = tie((one, two, ready, hop2))
    hop3 = lax.ppermute(hop2[0], "ep", zx(out))
    one, two = gather_end(one, y_axis), gather_end(two, x_axis)
    swapped = lax.ppermute(one, "ctx", core_swap), lax.ppermute(two, "ctx", core_swap)
    swapped, one, two, grads = tie((swapped, one, two, grads))
    down = gather_start(gather_end(grads, y_axis)[None], core_axis)
    late_q, late_k, late_v, gain = finish(
        facts, one, swapped[0], two, swapped[1], w_query, w_key, w_value, attn_norm[None]
    )
    late_q, hop3, down = tie((late_q, hop3, down))
    inner = (z == 1) | (z == 2)
    came_c, came_d = jnp.where(inner, hop[1], hop2[1]), jnp.where(inner, hop2[0], hop3)
    line_of = {0: (early, hop[0], came_c, came_d), 1: (hop[0], early, came_c, came_d)}
    line_of |= {2: (came_d, came_c, early, hop[0]), 3: (came_d, came_c, hop[0], early)}
    rows_of = [jnp.where(z == 0, line_of[0][k], line_of[1][k]) for k in range(NZ)]
    back_of = [jnp.where(z == 2, line_of[2][k], line_of[3][k]) for k in range(NZ)]
    early = jnp.concatenate([jnp.where(z < 2, a, b) for a, b in zip(rows_of, back_of)], 0)
    early = gather_end(gather_start(early[None], core_axis), core_axis)
    down = gather_end(down, core_axis).reshape(own, width, ff)
    down = jnp.concatenate([down[:, :ff], down[:, ff:]], -1).astype(F32)
    w_out_sum = early[:, : width // 2].reshape(width, width).astype(F32)
    small = early[0, width // 2 :].astype(F32)
    return (
        result_out[None],
        grad_tokens[None],
        gain[0],
        late_q,
        late_k,
        late_v,
        w_out_sum,
        small[experts],
        small[:experts].T,
        *ready,
        down,
    )


def solution(mesh):
    rows, whole, split = P("ep", "ctx", None), P(), P("ep", None, None)
    return jax.shard_map(
        local,
        mesh=mesh,
        in_specs=(rows, P("ep"), rows, rows) + (whole,) * 7 + (split,) * 3,
        out_specs=(rows, rows) + (whole,) * 7 + (split,) * 3,
        check_vma=False,
    )
```

```python
import functools

import jax
import jax.numpy as jnp
import numpy as np
from jax import lax
from jax.experimental import pallas as pl
from jax.experimental.pallas import tpu as pltpu
from jax.sharding import PartitionSpec as P

HEAD_DIM = 64
EPS = 1e-06
THETA = 10000.0
NEG = -1e30
LOG2E = 1.4426950408889634
PER_STEP = 2
NZ = 4
VMEM = 58 * 1024 * 1024
CORES = 2
F32 = jnp.float32
BF16 = jnp.bfloat16


def dot(a, b, ca, cb):
    return lax.dot_general(a, b, (((ca,), (cb,)), ((), ())), preferred_element_type=F32)


def params(semantics):
    return pltpu.CompilerParams(dimension_semantics=semantics, vmem_limit_bytes=VMEM)


COST = pl.CostEstimate(flops=1 << 20, bytes_accessed=1 << 20, transcendentals=0)


def cost(flops, nbytes):
    return pl.CostEstimate(flops=flops, bytes_accessed=nbytes, transcendentals=0)


def rope_constants(ctx_size, rows):
    half = HEAD_DIM // 2
    inv = THETA ** (-np.arange(half, dtype=np.float64) / half)
    fine = np.arange(rows, dtype=np.float64)[:, None] * inv[None, :]
    coarse = (rows * np.arange(ctx_size, dtype=np.float64))[:, None] * inv[None, :]
    tile = lambda t: jnp.asarray(np.tile(t, (1, 128 // half)).astype(np.float32))
    pad = np.zeros(((-2 * ctx_size) % 8, half))
    return (
        tile(np.concatenate([np.cos(fine), np.sin(fine)], 0)),
        tile(np.concatenate([np.cos(coarse), np.sin(coarse), pad], 0)),
    )


def swap_halves(x, roll):
    half = HEAD_DIM // 2
    width = x.shape[1]
    lane = lax.broadcasted_iota(jnp.int32, x.shape, 1)
    return jnp.where(lane % HEAD_DIM < half, roll(x, width - half), roll(x, half))


def prepare_body(experts, info_ref, len_ref, r_ref, c_ref, wg, wu, wd, ext_ref, sent_ref, buf, sem):
    rows, width = c_ref.shape
    ff = width // 2
    core = info_ref[0]
    count = len_ref[0] - info_ref[1] * rows
    pieces = [wg.at[core], wu.at[core]] + [wd.at[core, :, pl.ds(k * ff, ff)] for k in range(2)]
    spans = [pl.ds(0, width), pl.ds(width, width), pl.ds(2 * width, ff), pl.ds(2 * width + ff, ff)]
    into = [
        pltpu.make_async_copy(piece, buf.at[span], sem.at[0, k])
        for k, (piece, span) in enumerate(zip(pieces, spans))
    ]
    back = [
        pltpu.make_async_copy(buf.at[span], sent_ref.at[span], sem.at[1, k])
        for k, span in enumerate(spans)
    ]
    for copy in into:
        copy.start()
    row = lax.broadcasted_iota(jnp.int32, (rows, width), 0)
    ext_ref[:rows] = jnp.where(row < count, c_ref[...], jnp.zeros((), BF16))
    expert = lax.broadcasted_iota(jnp.int32, (experts, rows), 0)
    named = jnp.zeros((experts, rows), F32)
    for k in range(r_ref.shape[0]):
        named = jnp.where(expert == r_ref[k : k + 1, :], 1.0, named)
    ext_ref[rows:] = jnp.concatenate(
        [named, jnp.zeros((experts, width - rows), F32)], 1
    ).astype(BF16)
    for k in range(4):
        into[k].wait()
        back[k].start()
    for copy in back:
        copy.wait()


def prepare(facts, routes, cot, weights, experts):
    rows, width = cot.shape
    ff = width // 2
    anywhere = pl.BlockSpec(memory_space=pl.ANY)
    full = lambda shape: pl.BlockSpec(shape, lambda i, *s: (0, 0))
    return pl.pallas_call(
        functools.partial(prepare_body, experts),
        grid_spec=pltpu.PrefetchScalarGridSpec(
            num_scalar_prefetch=2,
            grid=(1,),
            in_specs=[full(routes.shape), full(cot.shape)] + [anywhere] * 3,
            out_specs=[full((rows + experts, width)), anywhere],
            scratch_shapes=[
                pltpu.VMEM((3 * width, ff), BF16),
                pltpu.SemaphoreType.DMA((2, 4)),
            ],
        ),
        out_shape=[
            jax.ShapeDtypeStruct((rows + experts, width), BF16),
            jax.ShapeDtypeStruct((3 * width, ff), BF16),
        ],
        compiler_params=params(("arbitrary",)),
        cost_estimate=COST,
        name="prepare",
    )(*facts, routes, cot, *weights)


def project_body(blocks, info_ref, len_ref, x_ref, gain_ref, wq_ref, wk_ref, wv_ref, fine_ref, start_ref,
                 n_ref, q_ref, kv_ref, cos_ref, sin_ref):
    step = pl.program_id(0)
    wide = q_ref.shape[1]
    nq = pl.num_programs(0) - 2
    rows = x_ref.shape[0]

    @pl.when(step == 0)
    def _():
        x = x_ref[...].astype(F32)
        scale = lax.rsqrt(jnp.mean(x * x, -1, keepdims=True) + EPS)
        n_ref[...] = (x * scale * gain_ref[...]).astype(BF16)
        cos_f, sin_f = fine_ref[:rows], fine_ref[rows:]
        cos_c = start_ref[pl.ds(info_ref[1], 1), :]
        sin_c = start_ref[pl.ds(info_ref[1] + blocks, 1), :]
        lane = lax.broadcasted_iota(jnp.int32, (rows, 128), 1)
        sign = jnp.where(lane % HEAD_DIM < HEAD_DIM // 2, -1.0, 1.0)
        cos_ref[...] = cos_f * cos_c - sin_f * sin_c
        sin_ref[...] = (sin_f * cos_c + cos_f * sin_c) * sign

    def rope(lin):
        cos = jnp.concatenate([cos_ref[...]] * (wide // 128), 1)
        sin = jnp.concatenate([sin_ref[...]] * (wide // 128), 1)
        return lin * cos + swap_halves(lin, lambda v, s: pltpu.roll(v, s, 1)) * sin

    @pl.when(step < nq)
    def _():
        lin = dot(n_ref[...], wq_ref[...], 1, 0)
        q_ref[...] = (rope(lin) * (LOG2E * HEAD_DIM**-0.5)).astype(BF16)

    @pl.when(step == nq)
    def _():
        kv_ref[...] = rope(dot(n_ref[...], wk_ref[...], 1, 0)).astype(BF16)[None]

    @pl.when(step == nq + 1)
    def _():
        kv_ref[...] = dot(n_ref[...], wv_ref[...], 1, 0).astype(BF16)[None]


def project(facts, x, gain, wq, wk, wv, fine, starts, blocks):
    rows, width = x.shape
    kvw = wk.shape[1]
    nq = wq.shape[1] // kvw
    clip = lambda v, hi: jnp.minimum(jnp.maximum(v, 0), hi)
    full = lambda shape: pl.BlockSpec(shape, lambda i, *s: (0, 0))
    return pl.pallas_call(
        functools.partial(project_body, blocks),
        grid_spec=pltpu.PrefetchScalarGridSpec(
            num_scalar_prefetch=2,
            grid=(nq + 2,),
            in_specs=[
                full((rows, width)),
                full((1, width)),
                pl.BlockSpec((width, kvw), lambda i, *s: (0, clip(i, nq - 1))),
                full((width, kvw)),
                full((width, kvw)),
                full(fine.shape),
                full(starts.shape),
            ],
            out_specs=[
                full((rows, width)),
                pl.BlockSpec((rows, kvw), lambda i, *s: (0, clip(i, nq - 1))),
                pl.BlockSpec((1, rows, kvw), lambda i, *s: (clip(i - nq, 1), 0, 0)),
                full((rows, 128)),
                full((rows, 128)),
            ],
        ),
        out_shape=[
            jax.ShapeDtypeStruct((rows, width), BF16),
            jax.ShapeDtypeStruct((rows, wq.shape[1]), BF16),
            jax.ShapeDtypeStruct((2, rows, kvw), BF16),
            jax.ShapeDtypeStruct((rows, 128), F32),
            jax.ShapeDtypeStruct((rows, 128), F32),
        ],
        compiler_params=params(("arbitrary",)),
        cost_estimate=COST,
        name="project",
    )(*facts, x, gain, wq, wk, wv, fine, starts)


def split_heads(block):
    lane = lax.broadcasted_iota(jnp.int32, block.shape, 1)
    low = lane < HEAD_DIM
    zero = jnp.zeros_like(block)
    turned = jnp.concatenate([block[:, HEAD_DIM:], block[:, :HEAD_DIM]], 1)
    first = jnp.concatenate([jnp.where(low, block, zero), jnp.where(low, zero, turned)], 0)
    second = jnp.concatenate([jnp.where(low, turned, zero), jnp.where(low, zero, block)], 0)
    return first, second


def with_mask(active, start, rows, seq_len, diagonal, work):
    if diagonal:
        pl.when(active)(lambda: work(True))
        return
    whole = start + rows <= seq_len
    pl.when(active & whole)(lambda: work(False))
    pl.when(active & jnp.logical_not(whole))(lambda: work(True))


def mask_of(start, rows, seq_len, diagonal):
    key = lax.broadcasted_iota(jnp.int32, (rows, rows), 0)
    bad = key + start >= seq_len
    if diagonal:
        bad = bad | (key > lax.broadcasted_iota(jnp.int32, (rows, rows), 1))
    return jnp.where(bad, NEG, 0.0)


def attend_blocks(info_ref, len_ref, base, q_ref, kv_refs, acc, top, low, diagonal):
    rows = q_ref.shape[0]
    seq_len = len_ref[0]

    def work(role, start, masked):
        if masked:
            bias = mask_of(start, rows, seq_len, diagonal and role == 0)
        for group in range(q_ref.shape[1] // 256):
            lanes = slice(group * 128, group * 128 + 128)
            keys = split_heads(kv_refs[role][0, :, lanes])
            values = split_heads(kv_refs[role][1, :, lanes])
            for pair in range(2):
                at = 256 * group + 128 * pair
                scores = dot(keys[pair], q_ref[:, at : at + 128], 1, 1)
                weights, shrinks = [], []
                for head in range(2):
                    at = 2 * pair + head
                    part = scores[head * rows : (head + 1) * rows]
                    if masked:
                        part = part + bias
                    old = top[group, at : at + 1, :]
                    new = jnp.maximum(old, jnp.max(part, 0, keepdims=True))
                    prob = jnp.exp2(part - new)
                    shrink = jnp.exp2(old - new)
                    top[group, at : at + 1, :] = new
                    fresh = jnp.sum(prob, 0, keepdims=True)
                    low[group, at : at + 1, :] = low[group, at : at + 1, :] * shrink + fresh
                    weights.append(prob.astype(BF16))
                    shrinks.append(jnp.broadcast_to(shrink, (HEAD_DIM, rows)))
                fresh = dot(values[pair], jnp.concatenate(weights, 0), 0, 0)
                acc[group, pair] = acc[group, pair] * jnp.concatenate(shrinks, 0) + fresh

    for role in range(len(kv_refs)):
        start = info_ref[base + 2 * role]
        active = (info_ref[base + 2 * role + 1] > 0) & (start < seq_len)
        with_mask(
            active, start, rows, seq_len, diagonal and role == 0, functools.partial(work, role, start)
        )


def attend_start_body(base, roles, info_ref, len_ref, q_ref, *refs):
    acc, top, low = refs[roles:]
    acc[...] = jnp.zeros_like(acc)
    top[...] = jnp.full_like(top, NEG)
    low[...] = jnp.zeros_like(low)
    attend_blocks(info_ref, len_ref, base, q_ref, refs[:roles], acc, top, low, True)


def attend_finish_body(base, roles, info_ref, len_ref, q_ref, *refs):
    acc_in, top_in, low_in, wo_ref, x_ref, gain_ref = refs[roles : roles + 6]
    att_ref, lse_ref, hid_ref, mix_ref, acc, top, low, proj = refs[roles + 6 :]
    step = pl.program_id(0)
    rows = q_ref.shape[0]
    acc[...] = acc_in[...]
    top[...] = top_in[...]
    low[...] = low_in[...]
    attend_blocks(info_ref, len_ref, base, q_ref, refs[:roles], acc, top, low, False)
    for group in range(q_ref.shape[1] // 256):
        for pair in range(2):
            sums = [low[group, 2 * pair + head : 2 * pair + head + 1, :] for head in range(2)]
            total = [jnp.broadcast_to(1.0 / s, (HEAD_DIM, rows)) for s in sums]
            att = acc[group, pair] * jnp.concatenate(total, 0)
            at = 256 * group + 128 * pair
            att_ref[:, at : at + 128] = jnp.transpose(att).astype(BF16)
    lse_ref[...] = top[...] + jnp.log2(jnp.maximum(low[...], 1e-30))

    @pl.when(step == 0)
    def _():
        proj[...] = x_ref[...].astype(F32)

    proj[...] += dot(att_ref[...], wo_ref[...], 1, 0)

    @pl.when(step == pl.num_programs(0) - 1)
    def _():
        hidden = proj[...]
        scale = lax.rsqrt(jnp.mean(hidden * hidden, -1, keepdims=True) + EPS)
        hid_ref[...] = hidden
        mix_ref[...] = (hidden * scale * gain_ref[...]).astype(BF16)


def attend(facts, base, q, blocks, state, wo=None, x=None, gain=None):
    rows, width = q.shape
    groups = width // 256
    per = PER_STEP
    steps = groups // per
    roles = len(blocks)
    full = lambda shape: pl.BlockSpec(shape, lambda i, *s: (0, 0))
    wide = pl.BlockSpec((rows, 256 * per), lambda i, *s: (0, i))
    heads = pl.BlockSpec((per, 8, rows), lambda i, *s: (i, 0, 0))
    accs = pl.BlockSpec((per, 2, 128, rows), lambda i, *s: (i, 0, 0, 0))
    in_specs = [wide] + [pl.BlockSpec((2, rows, 128 * per), lambda i, *s: (0, 0, i))] * roles
    state_specs = [accs, heads, heads]
    state_shapes = [jax.ShapeDtypeStruct((groups, 2, 128, rows), F32)]
    state_shapes += [jax.ShapeDtypeStruct((groups, 8, rows), F32)] * 2
    args = [*facts, q, *blocks]
    scratch = []
    if state is None:
        body, out_specs, out_shape = attend_start_body, state_specs, state_shapes
    else:
        body = attend_finish_body
        args += [*state, wo, x, gain]
        in_specs += state_specs
        in_specs += [
            pl.BlockSpec((256 * per, x.shape[1]), lambda i, *s: (i, 0)),
            full(x.shape),
            full((1, x.shape[1])),
        ]
        out_specs = [wide, heads, full(x.shape), full(x.shape)]
        out_shape = [
            jax.ShapeDtypeStruct((rows, width), BF16),
            jax.ShapeDtypeStruct((groups, 8, rows), F32),
            jax.ShapeDtypeStruct(x.shape, F32),
            jax.ShapeDtypeStruct(x.shape, BF16),
        ]
        scratch = [
            pltpu.VMEM((per, 2, 128, rows), F32),
            pltpu.VMEM((per, 8, rows), F32),
            pltpu.VMEM((per, 8, rows), F32),
            pltpu.VMEM(x.shape, F32),
        ]
    return pl.pallas_call(
        functools.partial(body, base, roles),
        grid_spec=pltpu.PrefetchScalarGridSpec(
            num_scalar_prefetch=2,
            grid=(steps,),
            in_specs=in_specs,
            out_specs=out_specs,
            scratch_shapes=scratch,
        ),
        out_shape=out_shape,
        compiler_params=params(("arbitrary",)),
        cost_estimate=COST,
        name="attend",
    )(*args)


def attend_back_body(base, roles, diagonal, info_ref, len_ref, q_ref, do_ref, lse_ref, delta_ref, *refs):
    kv_refs, (start_ref, dq_ref), dkv_refs = refs[:roles], refs[-roles - 2 : -roles], refs[-roles:]
    rows = q_ref.shape[0]
    seq_len = len_ref[0]
    if len(refs) > 2 * roles + 1:
        dq_ref[...] = start_ref[...]
    else:
        dq_ref[...] = jnp.zeros_like(dq_ref)
    lane = lax.broadcasted_iota(jnp.int32, (rows, 128), 1)
    low = lane < HEAD_DIM

    def work(role, start, masked):
        if masked:
            bias = mask_of(start, rows, seq_len, diagonal and role == 0)
        for group in range(q_ref.shape[1] // 256):
            lanes = slice(group * 128, group * 128 + 128)
            keys = split_heads(kv_refs[role][0, :, lanes])
            values = split_heads(kv_refs[role][1, :, lanes])
            dks, dvs = [], []
            for pair in range(2):
                cols = slice(256 * group + 128 * pair, 256 * group + 128 * pair + 128)
                q = q_ref[:, cols]
                do = do_ref[:, cols]
                scores = dot(keys[pair], q, 1, 1)
                grads = dot(values[pair], do, 1, 1)
                probs, raws = [], []
                for head in range(2):
                    at = 2 * pair + head
                    part = scores[head * rows : (head + 1) * rows]
                    if masked:
                        part = part + bias
                    prob = jnp.exp2(part - lse_ref[group, at : at + 1, :])
                    grad = grads[head * rows : (head + 1) * rows]
                    raws.append((prob * (grad - delta_ref[group, at : at + 1, :])).astype(BF16))
                    probs.append(prob.astype(BF16))
                raw = jnp.concatenate(raws, 0)
                dq_ref[:, cols] += dot(raw, keys[pair], 0, 0)
                dks.append(dot(raw, q, 1, 0) * (1.0 / LOG2E))
                dvs.append(dot(jnp.concatenate(probs, 0), do, 1, 0))
            for which, parts in enumerate((dks, dvs)):
                top_a, bottom_a = parts[0][:rows], parts[0][rows:]
                top_b, bottom_b = parts[1][:rows], parts[1][rows:]
                turn = pltpu.roll(jnp.where(low, top_b, bottom_a), HEAD_DIM, 1)
                whole = jnp.where(low, top_a, bottom_b) + turn
                dkv_refs[role][which, :, lanes] = whole.astype(dkv_refs[role].dtype)

    for role in range(roles):
        start = info_ref[base + 2 * role]
        active = (info_ref[base + 2 * role + 1] > 0) & (start < seq_len)

        @pl.when(jnp.logical_not(active))
        def _(role=role):
            dkv_refs[role][...] = jnp.zeros_like(dkv_refs[role])

        with_mask(
            active, start, rows, seq_len, diagonal and role == 0, functools.partial(work, role, start)
        )


def attend_back(facts, base, q, do, lse, delta, blocks, before, diagonal):
    rows, width = q.shape
    per = PER_STEP
    steps = width // (256 * per)
    roles = len(blocks)
    kvw = blocks[0].shape[2]
    wide = pl.BlockSpec((rows, 256 * per), lambda i, *s: (0, i))
    heads = pl.BlockSpec((per, 8, rows), lambda i, *s: (i, 0, 0))
    kv = pl.BlockSpec((2, rows, 128 * per), lambda i, *s: (0, 0, i))
    more = [] if before is None else [before]
    return pl.pallas_call(
        functools.partial(attend_back_body, base, roles, diagonal),
        grid_spec=pltpu.PrefetchScalarGridSpec(
            num_scalar_prefetch=2,
            grid=(steps,),
            in_specs=[wide, wide, heads, heads] + [kv] * roles + [wide] * len(more),
            out_specs=[wide] + [kv] * roles,
        ),
        out_shape=[jax.ShapeDtypeStruct((rows, width), F32)]
        + [jax.ShapeDtypeStruct((2, rows, kvw), BF16)] * roles,
        compiler_params=params(("arbitrary",)),
        cost_estimate=cost(40 * rows * rows * roles * width, 16 * 1024 * 1024),
        name="attend_back",
    )(*facts, q, do, lse, delta, *blocks, *more)


def expert_body(base, own, remotes, twins, first, carry, experts, info_ref, len_ref, *refs):
    x_refs, c_refs, wr_ref = refs[:twins], refs[twins : 2 * twins], refs[2 * twins]
    at = 2 * twins + 1
    near = refs[at : at + (3 if own else 0)]
    at += len(near)
    far = refs[at : at + remotes]
    at += remotes
    lead = refs[at : at + (3 if own else 1)]
    at += len(lead)
    before, out_before = (refs[at], refs[at + 1]) if carry else (None, None)
    outs = refs[-15 if first else -13 :]
    gm_ref, gate_ref, out_ref, inner_ref, dg_ref, du_ref = outs[:6]
    copies = outs[6:8] if first else ()
    wbuf, sem, gm_acc, out_acc, gates, back, picked = outs[-7:]
    step = pl.program_id(0)
    total = own + remotes
    rows, width = x_refs[0].shape
    ff = width // 2
    slot = lax.rem(step, 2)
    offsets = (0, width, 2 * width, 2 * width + ff)
    sizes = (width, width, ff, ff)

    def fetch(target, where):
        def start(sources):
            for piece, (ref, off, size) in enumerate(zip(sources, offsets, sizes)):
                pltpu.make_async_copy(
                    ref, wbuf.at[where, pl.ds(off, size)], sem.at[where, piece]
                ).start()

        if own:

            @pl.when(target < own)
            def _():
                down = [near[2].at[target, :, pl.ds(k * ff, ff)] for k in range(2)]
                start([near[0].at[target], near[1].at[target]] + down)

        for i in range(remotes):

            @pl.when(target == own + i)
            def _(i=i):
                start([far[i].at[pl.ds(off, size)] for off, size in zip(offsets, sizes)])

    @pl.when(step + 1 < total)
    def _():
        fetch(step + 1, lax.rem(step + 1, 2))

    lane = lax.broadcasted_iota(jnp.int32, (rows, 128), 1)
    if twins == 2:
        x_ref, cot_ref = picked.at[0, pl.ds(0, rows)], picked.at[1]
    else:
        x_ref, cot_ref = x_refs[0], c_refs[0]

    @pl.when(step == 0)
    def _():
        if twins == 2:
            use = info_ref[base + 3] > 0
            picked[0, :rows] = jnp.where(use, x_refs[0][...], x_refs[1][...])
            picked[1] = jnp.where(use, c_refs[0][...], c_refs[1][...])
        logits = dot(x_ref[...], wr_ref[...], 1, 0)
        mask_t = cot_ref[pl.ds(rows, experts), :rows].astype(F32)
        mask_t = jnp.concatenate([mask_t, jnp.zeros((128 - experts, rows), F32)], 0)
        mask = jnp.transpose(mask_t) > 0.5
        high = jnp.max(jnp.where(mask, logits, NEG), 1, keepdims=True)
        raised = jnp.where(mask, jnp.exp(logits - high), 0.0)
        gates[...] = raised / jnp.sum(raised, 1, keepdims=True)
        gate_ref[...] = gates[...]
        back[...] = jnp.zeros_like(back)
        if carry:
            out_acc[...] = out_before[0].astype(F32)
            gm_acc[...] = before[:rows, :].astype(F32)
        else:
            out_acc[...] = jnp.zeros_like(out_acc)
            gm_acc[...] = jnp.zeros_like(gm_acc)
        if first:
            copies[0][0] = x_ref[...]
            copies[1][0] = cot_ref[pl.ds(0, rows), :]

    def expert(wg, wu, wd0, wd1):
        which = info_ref[base + 2] + info_ref[base + 4 + step]
        x = x_ref[...]
        cot = cot_ref[pl.ds(0, rows), :]
        g = dot(x, wg, 1, 0)
        u = dot(x, wu, 1, 0)
        raw = dot(cot[:, :ff], wd0, 1, 1) + dot(cot[:, ff:], wd1, 1, 1)
        gate = jnp.sum(jnp.where(lane == which, gates[...], 0.0), 1, keepdims=True)
        sig = 1.0 / (1.0 + jnp.exp(-g))
        silu = g * sig
        inner = silu * u
        gg = jnp.sum(raw * inner, 1, keepdims=True)
        back[...] += jnp.where(lane == which, gg, 0.0)
        scaled = (gate * inner).astype(BF16)
        gi = gate * raw
        dg = (gi * u * (sig * (1.0 + g * (1.0 - sig)))).astype(BF16)
        du = (gi * silu).astype(BF16)
        inner_ref[0] = scaled
        dg_ref[0] = dg
        du_ref[0] = du
        out_acc[:, :ff] += dot(scaled, wd0, 1, 0)
        out_acc[:, ff:] += dot(scaled, wd1, 1, 0)
        gm_acc[...] += dot(dg, wg, 1, 1) + dot(du, wu, 1, 1)

    @pl.when(step == 0)
    def _():
        if own:
            down = lead[2][0]
            expert(lead[0][0], lead[1][0], down[:, :ff], down[:, ff:])
        else:
            expert(*(lead[0][off : off + size] for off, size in zip(offsets, sizes)))

    @pl.when(step > 0)
    def _():
        for piece, (off, size) in enumerate(zip(offsets, sizes)):
            place = wbuf.at[slot, pl.ds(off, size)]
            pltpu.make_async_copy(place, place, sem.at[slot, piece]).wait()
        expert(*(wbuf[slot, off : off + size, :] for off, size in zip(offsets, sizes)))

    @pl.when(step == total - 1)
    def _():
        tail = jnp.transpose(back[...])[:experts, :]
        tail = jnp.concatenate([tail, jnp.zeros((experts, width - rows), F32)], 1)
        if carry:
            tail = tail + before[rows:, :].astype(F32)
        gm_ref[:rows, :] = gm_acc[...].astype(BF16)
        gm_ref[rows:, :] = tail.astype(BF16)
        out_ref[0] = out_acc[...].astype(BF16)


def expert_call(facts, base, xs, cots, wr, own_weights, far, experts, kept, before=None):
    rows, width = xs[0].shape
    own = own_weights[0].shape[0] if own_weights else 0
    remotes = len(far)
    total = own + remotes
    twins = len(xs)
    carry = before is not None
    first = not carry
    ff = width // 2
    full = lambda shape: pl.BlockSpec(shape, lambda i, *s: (0,) * len(shape))
    anywhere = pl.BlockSpec(memory_space=pl.ANY)
    big = pl.BlockSpec((1, rows, width), lambda i, s, n: (s[base + 1], 0, 0))
    part = pl.BlockSpec((1, rows, ff), lambda i, s, n: (s[base + 1], 0, s[base + 4 + i]))
    count = 6 if first else 4
    fresh = isinstance(kept[0], jax.ShapeDtypeStruct)
    aliased = [] if fresh else list(kept[:count])
    lead = list(own_weights) if own else [far[0]]
    inputs = [*xs, *cots, wr, *own_weights, *far, *lead] + ([before] if carry else [])
    specs = [full((rows, width))] * twins + [full(cots[0].shape)] * twins + [full(wr.shape)]
    specs += [anywhere] * (len(own_weights) + remotes)
    specs += [full((1,) + w.shape[1:] if own else w.shape) for w in lead]
    specs += [full(before.shape)] if carry else []
    specs += [big if carry and k == 0 else anywhere for k in range(len(aliased))]
    gm_shape = (rows + experts, width)
    outs = pl.pallas_call(
        functools.partial(expert_body, base, own, remotes, twins, first, carry, experts),
        grid_spec=pltpu.PrefetchScalarGridSpec(
            num_scalar_prefetch=2,
            grid=(total,),
            in_specs=specs,
            out_specs=[full(gm_shape), full((rows, 128)), big, part, part, part]
            + ([big, big] if first else []),
            scratch_shapes=[
                pltpu.VMEM((2, 3 * width, ff), BF16),
                pltpu.SemaphoreType.DMA((2, 4)),
                pltpu.VMEM((rows, width), F32),
                pltpu.VMEM((rows, width), F32),
                pltpu.VMEM((rows, 128), F32),
                pltpu.VMEM((rows, 128), F32),
                pltpu.VMEM((2,) + gm_shape, BF16),
            ],
        ),
        out_shape=[
            jax.ShapeDtypeStruct(gm_shape, BF16),
            jax.ShapeDtypeStruct((rows, 128), F32),
        ]
        + [jax.ShapeDtypeStruct(k.shape, k.dtype) for k in kept[:count]],
        input_output_aliases={2 + len(inputs) + k: 2 + k for k in range(len(aliased))},
        compiler_params=params(("arbitrary",)),
        cost_estimate=COST
        if not far
        else cost(12 * rows * width * ff * total, total * 6 * width * ff),
        name="experts",
    )(*facts, *inputs, *aliased)
    return outs[0], outs[1], tuple(outs[2:]) + tuple(kept[count:])


def expert_grads_body(base, info_ref, len_ref, x_hbm, c_hbm, in_hbm, dg_hbm, du_hbm, o_ref, x, c, cols, sem):
    place, kind = pl.program_id(0), pl.program_id(1)
    step = place * 3 + kind
    ff = cols.shape[2]
    hidden = (dg_hbm, du_hbm, in_hbm)

    def fetch(target, start):
        at = lax.rem(target, 2)
        off = pl.ds(pl.multiple_of(info_ref[base + lax.div(target, 3)] * ff, 128), ff)
        for k, ref in enumerate(hidden):

            @pl.when(lax.rem(target, 3) == k)
            def _(ref=ref):
                pltpu.make_async_copy(ref.at[:, off], cols.at[at], sem.at[at]).start()

    @pl.when(step == 0)
    def _():
        pltpu.make_async_copy(x_hbm, x, sem.at[2]).start()
        fetch(step, True)
        pltpu.make_async_copy(c_hbm, c, sem.at[3]).start()
        pltpu.make_async_copy(x_hbm, x, sem.at[2]).wait()

    @pl.when(step + 1 < 3 * pl.num_programs(0))
    def _():
        fetch(step + 1, True)

    slot = lax.rem(step, 2)
    pltpu.make_async_copy(cols.at[slot], cols.at[slot], sem.at[slot]).wait()

    @pl.when(kind < 2)
    def _():
        o_ref[0, 0] = dot(x[...], cols[slot], 0, 0).astype(BF16)

    @pl.when(step == 2)
    def _():
        pltpu.make_async_copy(c_hbm, c, sem.at[3]).wait()

    @pl.when(kind == 2)
    def _():
        o_ref[0, 0, :ff] = dot(cols[slot], c[:, :ff], 0, 0).astype(BF16)
        o_ref[0, 0, ff:] = dot(cols[slot], c[:, ff:], 0, 0).astype(BF16)


def expert_grads(facts, base, count, x, c, inner, dg, du):
    rows, width = x.shape
    ff = width // 2
    anywhere = pl.BlockSpec(memory_space=pl.ANY)
    return pl.pallas_call(
        functools.partial(expert_grads_body, base),
        grid_spec=pltpu.PrefetchScalarGridSpec(
            num_scalar_prefetch=2,
            grid=(count, 3),
            in_specs=[anywhere] * 5,
            out_specs=pl.BlockSpec((1, 1, width, ff), lambda i, k, *s: (i, k, 0, 0)),
            scratch_shapes=[
                pltpu.VMEM((rows, width), BF16),
                pltpu.VMEM((rows, width), BF16),
                pltpu.VMEM((2, rows, ff), BF16),
                pltpu.SemaphoreType.DMA((4,)),
            ],
        ),
        out_shape=jax.ShapeDtypeStruct((count, 3, width, ff), BF16),
        compiler_params=params(("arbitrary",) * 2),
        cost_estimate=cost(6 * rows * width * ff * count, 16 * 1024 * 1024),
        name="expert_grads",
    )(*facts, x, c, inner, dg, du)


def middle_body(experts, *refs):
    sums, ends, refs = refs[:4], refs[4:8], refs[8:]
    gate_ref, wr_ref, hid_ref, cot_ref, att_ref, mix_ref, gain_ref, wo_hbm = refs[:8]
    gh_ref, gb_ref, do_ref, delta_ref, ffn_ref, router_ref, wo, sem, deltas, logit = refs[8:]
    step = pl.program_id(0)
    part, width = hid_ref.shape
    rows = gate_ref.shape[0]
    span = pl.ds(pl.multiple_of(step * part, part), part)

    @pl.when(step == 0)
    def _():
        pltpu.make_async_copy(wo_hbm, wo, sem).start()
        ffn_ref[...] = jnp.zeros_like(ffn_ref)
        router_ref[...] = jnp.zeros_like(router_ref)
        gg = ends[0][:, :rows].astype(F32)
        for ref in ends[1:]:
            gg = gg + ref[:, :rows].astype(F32)
        gg = jnp.transpose(jnp.concatenate([gg, jnp.zeros((128 - experts, rows), F32)], 0))
        gates = gate_ref[...]
        logit[...] = (gates * (gg - jnp.sum(gates * gg, 1, keepdims=True))).astype(BF16)

    total = sums[0][...].astype(F32)
    for ref in sums[1:]:
        total = total + ref[...].astype(F32)
    gl = logit[span, :]
    router_ref[...] += dot(gl, mix_ref[...], 0, 0)
    hidden = hid_ref[...]
    grad_mixed = total + dot(gl, wr_ref[...], 1, 1)
    scale = lax.rsqrt(jnp.mean(hidden * hidden, -1, keepdims=True) + EPS)
    ffn_ref[...] += jnp.sum(grad_mixed * hidden * scale, 0, keepdims=True)
    weighted = grad_mixed * gain_ref[...]
    mean = jnp.mean(weighted * hidden, -1, keepdims=True)
    grad = cot_ref[...].astype(F32) + scale * weighted - hidden * (scale * scale * scale * mean)
    gh_ref[...] = grad
    low = grad.astype(BF16)
    gb_ref[...] = low

    @pl.when(step == 0)
    def _():
        pltpu.make_async_copy(wo_hbm, wo, sem).wait()

    do = dot(low, wo[...], 1, 1).astype(BF16)
    do_ref[...] = do
    both = do.astype(F32) * att_ref[...].astype(F32)
    lane = lax.broadcasted_iota(jnp.int32, (part, 128), 1)
    found = jnp.zeros((part, 128), F32)
    for block in range(both.shape[1] // 128):
        pair = both[:, block * 128 : block * 128 + 128]
        front = jnp.sum(jnp.where(lane < HEAD_DIM, pair, 0.0), 1, keepdims=True)
        back = jnp.sum(jnp.where(lane < HEAD_DIM, 0.0, pair), 1, keepdims=True)
        found = jnp.where(lane == 2 * block, front, found)
        found = jnp.where(lane == 2 * block + 1, back, found)
    deltas[span, :] = found

    @pl.when(step == pl.num_programs(0) - 1)
    def _():
        turned = jnp.transpose(deltas[...])
        for group in range(delta_ref.shape[0]):
            delta_ref[group, :4, :] = turned[4 * group : 4 * group + 4]
            delta_ref[group, 4:, :] = jnp.zeros((4, rows), F32)


def middle(sums, gates, wr, hidden, cot_ext, attended, mixed, gain, wo, experts):
    rows, width = hidden.shape
    steps = 1
    heads = attended.shape[1] // HEAD_DIM
    row = lambda w: pl.BlockSpec((rows // steps, w), lambda i: (i, 0))
    end = pl.BlockSpec((experts, width), lambda i: (rows // experts, 0))
    full = lambda shape: pl.BlockSpec(shape, lambda i: (0,) * len(shape))
    return pl.pallas_call(
        functools.partial(middle_body, experts),
        grid=(steps,),
        in_specs=[row(width)] * 4
        + [end] * 4
        + [
            full((rows, 128)),
            full(wr.shape),
            row(width),
            row(width),
            row(attended.shape[1]),
            row(width),
            full((1, width)),
            pl.BlockSpec(memory_space=pl.ANY),
        ],
        out_specs=[
            row(width),
            row(width),
            row(attended.shape[1]),
            full((heads // 4, 8, rows)),
            full((1, width)),
            full((128, width)),
        ],
        out_shape=[
            jax.ShapeDtypeStruct((rows, width), F32),
            jax.ShapeDtypeStruct((rows, width), BF16),
            jax.ShapeDtypeStruct(attended.shape, BF16),
            jax.ShapeDtypeStruct((heads // 4, 8, rows), F32),
            jax.ShapeDtypeStruct((1, width), F32),
            jax.ShapeDtypeStruct((128, width), F32),
        ],
        scratch_shapes=[
            pltpu.VMEM(wo.shape, BF16),
            pltpu.SemaphoreType.DMA(()),
            pltpu.VMEM((rows, 128), F32),
            pltpu.VMEM((rows, 128), BF16),
        ],
        compiler_params=params(("arbitrary",)),
        cost_estimate=COST,
        name="middle",
    )(*sums, *sums, gates, wr, hidden, cot_ext, attended, mixed, gain, wo)


def early_body(experts, info_ref, len_ref, att_ref, gb_ref, router_ref, ffn_ref, give_ref, keep_ref):
    size = att_ref.shape[1] // 2
    core = info_ref[0]
    width = gb_ref.shape[1]
    row = lax.broadcasted_iota(jnp.int32, (16, width), 0)
    extra = jnp.concatenate([router_ref[:experts], jnp.where(row == 0, ffn_ref[...], 0.0)], 0)
    for ref, half in ((keep_ref, core), (give_ref, 1 - core)):
        part = att_ref[:, pl.ds(pl.multiple_of(half * size, 128), size)]
        ref[:size] = dot(part, gb_ref[...], 0, 0).astype(BF16)
        ref[size : size + experts + 16] = jnp.where(half == 0, extra, 0.0).astype(BF16)
        rest = ref.shape[0] - (size + experts + 16)
        ref[size + experts + 16 :] = jnp.zeros((rest, width), BF16)


def early_grads(facts, attended, gb, router, ffn, experts):
    rows, width = gb.shape
    count = attended.shape[1]
    col = lambda r: pl.BlockSpec((r, 512), lambda i, *s: (0, i))
    size = count // 2 + count // 8
    return pl.pallas_call(
        functools.partial(early_body, experts),
        grid_spec=pltpu.PrefetchScalarGridSpec(
            num_scalar_prefetch=2,
            grid=(width // 512,),
            in_specs=[
                pl.BlockSpec(attended.shape, lambda i, *s: (0, 0)),
                col(rows),
                col(router.shape[0]),
                col(1),
            ],
            out_specs=[col(size)] * 2,
        ),
        out_shape=[jax.ShapeDtypeStruct((size, width), BF16)] * 2,
        compiler_params=params(("arbitrary",)),
        cost_estimate=COST,
        name="early_grads",
    )(*facts, attended, gb, router, ffn)


def rope_back(g, cos_ref, sin_ref):
    cos = jnp.concatenate([cos_ref[...]] * (g.shape[1] // 128), 1)
    sin = jnp.concatenate([sin_ref[...]] * (g.shape[1] // 128), 1)
    return g * cos - swap_halves(g, lambda v, s: pltpu.roll(v, s, 1)) * sin


def split_rows(core, n_ref, lin, give_ref, keep_ref):
    size = n_ref.shape[1] // 2
    for ref, half in ((give_ref, 1 - core), (keep_ref, core)):
        part = n_ref[:, pl.ds(pl.multiple_of(half * size, 128), size)]
        ref[...] = dot(part, lin, 0, 0).astype(BF16)


def query_back_body(info_ref, len_ref, dq_ref, n_ref, cos_ref, sin_ref, lin_ref, give_ref, keep_ref):
    lin = rope_back(dq_ref[...] * HEAD_DIM**-0.5, cos_ref, sin_ref).astype(BF16)
    lin_ref[...] = lin
    split_rows(info_ref[0], n_ref, lin, give_ref, keep_ref)


def query_back(facts, dq, normed, cos, sin):
    rows, width = dq.shape
    col = lambda r: pl.BlockSpec((r, 512), lambda i, *s: (0, i))
    full = lambda shape: pl.BlockSpec(shape, lambda i, *s: (0, 0))
    size = normed.shape[1] // 2
    return pl.pallas_call(
        query_back_body,
        grid_spec=pltpu.PrefetchScalarGridSpec(
            num_scalar_prefetch=2,
            grid=(width // 512,),
            in_specs=[col(rows), full(normed.shape), full(cos.shape), full(sin.shape)],
            out_specs=[col(rows), col(size), col(size)],
        ),
        out_shape=[
            jax.ShapeDtypeStruct((rows, width), BF16),
            jax.ShapeDtypeStruct((size, width), BF16),
            jax.ShapeDtypeStruct((size, width), BF16),
        ],
        compiler_params=params(("arbitrary",)),
        cost_estimate=cost(2 * rows * width * width, 8 * 1024 * 1024),
        name="query_back",
    )(*facts, dq, normed, cos, sin)


def pair_back_body(parts, half_steps, info_ref, len_ref, *refs):
    n_ref, cos_ref, sin_ref, lin_ref, give_ref, keep_ref = refs[parts:]
    step = pl.program_id(0)
    total = refs[0][0].astype(F32)
    for ref in refs[1:parts]:
        total = total + ref[0].astype(F32)

    @pl.when(step < half_steps)
    def _():
        lin_ref[...] = rope_back(total, cos_ref, sin_ref).astype(BF16)

    @pl.when(step >= half_steps)
    def _():
        lin_ref[...] = total.astype(BF16)

    split_rows(info_ref[0], n_ref, lin_ref[...], give_ref, keep_ref)


def pair_back(facts, parts, normed, cos, sin):
    _, rows, kvw = parts[0].shape
    half_steps = kvw // 512
    col = lambda r: pl.BlockSpec((r, 512), lambda i, *s: (0, i))
    full = lambda shape: pl.BlockSpec(shape, lambda i, *s: (0, 0))
    part = pl.BlockSpec((1, rows, 512), lambda i, *s: (i // half_steps, 0, i % half_steps))
    size = normed.shape[1] // 2
    return pl.pallas_call(
        functools.partial(pair_back_body, len(parts), half_steps),
        grid_spec=pltpu.PrefetchScalarGridSpec(
            num_scalar_prefetch=2,
            grid=(2 * half_steps,),
            in_specs=[part] * len(parts) + [full(normed.shape), full(cos.shape), full(sin.shape)],
            out_specs=[col(rows), col(size), col(size)],
        ),
        out_shape=[
            jax.ShapeDtypeStruct((rows, 2 * kvw), BF16),
            jax.ShapeDtypeStruct((size, 2 * kvw), BF16),
            jax.ShapeDtypeStruct((size, 2 * kvw), BF16),
        ],
        compiler_params=params(("arbitrary",)),
        cost_estimate=COST,
        name="pair_back",
    )(*facts, *parts, normed, cos, sin)


def tokens_back_body(lq_ref, lkv_ref, wq_ref, wk_ref, wv_ref, x_ref, gh_ref, gain_ref, o_ref):
    kvw = wk_ref.shape[1]
    grad = dot(lq_ref[...], wq_ref[...], 1, 1)
    grad = grad + dot(lkv_ref[:, :kvw], wk_ref[...], 1, 1)
    grad = grad + dot(lkv_ref[:, kvw:], wv_ref[...], 1, 1)
    x = x_ref[...].astype(F32)
    scale = lax.rsqrt(jnp.mean(x * x, -1, keepdims=True) + EPS)
    weighted = grad * gain_ref[...]
    mean = jnp.mean(weighted * x, -1, keepdims=True)
    total = gh_ref[...] + scale * weighted - x * (scale * scale * scale * mean)
    o_ref[...] = total.astype(BF16)


def tokens_back(lq, lkv, wq, wk, wv, x, gh, gain):
    rows, width = x.shape
    row = lambda w: pl.BlockSpec((rows, w), lambda i: (i, 0))
    full = lambda shape: pl.BlockSpec(shape, lambda i: (0, 0))
    return pl.pallas_call(
        tokens_back_body,
        grid=(1,),
        in_specs=[
            row(lq.shape[1]),
            row(lkv.shape[1]),
            full(wq.shape),
            full(wk.shape),
            full(wv.shape),
            row(width),
            row(width),
            full((1, width)),
        ],
        out_specs=row(width),
        out_shape=jax.ShapeDtypeStruct((rows, width), BF16),
        compiler_params=params(("arbitrary",)),
        cost_estimate=COST,
        name="tokens_back",
    )(lq, lkv, wq, wk, wv, x, gh, gain)


def finish_body(info_ref, len_ref, qa, qb, pa, pb, wq_ref, wk_ref, wv_ref, gain_ref, q_ref, k_ref, v_ref, n_ref):
    mine = pl.program_id(0) // (pl.num_programs(0) // 2) == info_ref[0]
    q = jnp.where(mine, qa[...].astype(F32), qb[...].astype(F32))
    pair = jnp.where(mine, pa[...].astype(F32), pb[...].astype(F32))
    kvw = k_ref.shape[1]
    q_ref[...] = q
    k_ref[...] = pair[:, :kvw]
    v_ref[...] = pair[:, kvw:]
    gain = jnp.sum(q * wq_ref[...].astype(F32), 1, keepdims=True)
    gain = gain + jnp.sum(pair[:, :kvw] * wk_ref[...].astype(F32), 1, keepdims=True)
    gain = gain + jnp.sum(pair[:, kvw:] * wv_ref[...].astype(F32), 1, keepdims=True)
    turned = jnp.transpose(jnp.broadcast_to(gain, (gain.shape[0], 128)))
    n_ref[...] = turned[:1] / gain_ref[...]


def finish(facts, qa, qb, pa, pb, wq, wk, wv, gain):
    width = wq.shape[0]
    part = width // 2
    half = lambda w: pl.BlockSpec((part, w), lambda i, *s: (0, 0))
    row = lambda w: pl.BlockSpec((part, w), lambda i, *s: (i, 0))
    line = pl.BlockSpec((1, part), lambda i, *s: (0, i))
    return pl.pallas_call(
        finish_body,
        grid_spec=pltpu.PrefetchScalarGridSpec(
            num_scalar_prefetch=2,
            grid=(2,),
            in_specs=[half(width)] * 4
            + [row(wq.shape[1]), row(wk.shape[1]), row(wv.shape[1]), line],
            out_specs=[row(wq.shape[1]), row(wk.shape[1]), row(wv.shape[1]), line],
        ),
        out_shape=[
            jax.ShapeDtypeStruct(wq.shape, F32),
            jax.ShapeDtypeStruct(wk.shape, F32),
            jax.ShapeDtypeStruct(wv.shape, F32),
            jax.ShapeDtypeStruct((1, width), F32),
        ],
        compiler_params=params(("arbitrary",)),
        cost_estimate=COST,
        name="finish",
    )(*facts, qa, qb, pa, pb, wq, wk, wv, gain)


def total_of(parts):
    total = parts[0].astype(F32)
    for part in parts[1:]:
        total = total + part.astype(F32)
    return total.astype(BF16)


def scatter_start(buf, axis):
    name, size, pos, pairs = axis
    rows = buf.shape[0] // size
    take = lambda k: lax.dynamic_slice_in_dim(buf, k * rows, rows, 0)
    parts = [take(pos)]
    for shift in range(1, size):
        parts.append(lax.ppermute(take((pos + shift) % size), name, pairs(shift)))
    return parts


def gather_start(buf, axis):
    name, size, pos, pairs = axis
    return [lax.ppermute(buf, name, pairs(shift)) for shift in range(size - 1, 0, -1)] + [buf]


def gather_end(order, axis):
    name, size, pos, pairs = axis
    rows = order[0].shape[0]
    if size == 2:
        pick = lambda a, b: jnp.concatenate([a, b], 0)
        return jnp.where(pos == 0, pick(order[1], order[0]), pick(order[0], order[1]))
    double = jnp.concatenate(order + order[:-1], 0)
    return lax.dynamic_slice_in_dim(double, (size - 1 - pos) * rows, size * rows, 0)


def device_facts(nx, ny, own, rows, ep_index, ctx_index):
    group = nx * own
    table = np.zeros((NZ * nx, ny * CORES, 160), np.int32)
    for ep in range(NZ * nx):
        for ctx in range(ny * CORES):
            z, x, y, core = ep // nx, ep % nx, ctx // CORES, ctx % CORES
            out = table[ep, ctx]
            out[0], out[1] = core, ctx
            out[16:20] = ctx * rows, 1, (ctx - 1) * rows, core
            for back in range(1, ny):
                at, block = 16 + 4 * back, (y - back) * CORES
                out[at : at + 4] = (block + core) * rows, y >= back, (block + 1 - core) * rows, y >= back
            near = [x * own + i for i in range(own)]
            far = [(x - s) % nx * own + i for s in range(1, nx) for i in (core, 1 - core)]
            shard_c, shard_d, inside = (2, 2, 1, 1)[z], (3, 3, 0, 0)[z], int(z in (1, 2))
            calls = [(z, 1, near), (z, 1, far), (z ^ 1, 1, near + far)]
            calls += [(shard_c, inside, near + far), (shard_d, inside, near + far)]
            for k, (shard, pick, places) in enumerate(calls):
                out[48 + 16 * k : 52 + 16 * k] = 0, shard, z * group, pick
                out[52 + 16 * k : 52 + 16 * k + len(places)] = places
            for j in range(nx):
                out[128 + j] = (x + j) % nx * own + 1 - core
                out[144 + j] = (x + j) % nx * own + core
    line = lax.dynamic_slice(
        jnp.asarray(table), (ep_index, ctx_index, jnp.int32(0)), (1, 1, table.shape[2])
    )
    return line.reshape(-1)


def local(
    tokens,
    lengths,
    routes,
    cotangent,
    attn_norm,
    w_query,
    w_key,
    w_value,
    w_out,
    ffn_norm,
    w_router,
    expert_gate_weight,
    expert_up_weight,
    expert_down_weight,
):
    rows, width = tokens.shape[1:]
    half = rows // 2
    experts = w_router.shape[1]
    own = expert_gate_weight.shape[0]
    ff = expert_gate_weight.shape[2]
    kvw = w_key.shape[1]
    ctx_size, ep_size = lax.axis_size("ctx"), lax.axis_size("ep")
    ny, nx = ctx_size // CORES, ep_size // NZ
    ctx_index, ep_index = lax.axis_index("ctx"), lax.axis_index("ep")
    y, core = ctx_index // CORES, ctx_index % CORES
    z, xpos = ep_index // nx, ep_index % nx
    seq_len = lengths[0]
    tokens = tokens[0]
    valid_flag = ctx_index * rows + jnp.arange(rows, dtype=jnp.int32) < seq_len
    valid = valid_flag.astype(F32)[:, None]
    tie = lax.optimization_barrier

    core_swap = [(c, c ^ 1) for c in range(ctx_size)]
    core_up = [(c, c + 1) for c in range(0, ctx_size, CORES)]
    core_down = [(c + 1, c) for c in range(0, ctx_size, CORES)]
    y_up = lambda k: [(c, c + CORES * k) for c in range(ctx_size - CORES * k)]
    y_down = lambda k: [(b, a) for a, b in y_up(k)]
    zx = lambda pairs: [(a * nx + i, b * nx + i) for a, b in pairs for i in range(nx)]
    z_groups = [[i + nx * k for k in range(NZ)] for i in range(nx)]
    x_shift = lambda s: [(k * nx + i, k * nx + (i + s) % nx) for k in range(NZ) for i in range(nx)]
    y_ring = lambda s: [(c, (c + CORES * s) % ctx_size) for c in range(ctx_size)]
    core_axis = ("ctx", CORES, core, lambda s: core_swap)
    y_axis = ("ctx", ny, y, y_ring)
    x_axis = ("ep", nx, xpos, x_shift)
    z_axis = ("ep", NZ, z, lambda s: zx([(k, (k + s) % NZ) for k in range(NZ)]))

    weights = (expert_gate_weight, expert_up_weight, expert_down_weight)
    facts = (device_facts(nx, ny, own, rows, ep_index, ctx_index), lengths)
    cot_ext, sent = prepare(facts, routes[0].T, cotangent[0], weights, experts)
    arrived = [lax.ppermute(sent, "ep", x_shift(shift)) for shift in range(1, nx)]

    swap, mid, out = [(0, 1), (1, 0), (2, 3), (3, 2)], [(1, 2), (2, 1)], [(1, 0), (2, 3)]
    cot_near = lax.ppermute(cot_ext, "ep", zx(swap))
    cot_middle = lax.ppermute(cot_ext, "ep", zx(mid))
    tokens, cot_ext, sent = tie((tokens, cot_ext, sent))
    fine, starts = rope_constants(ctx_size, rows)
    normed, q, kv, cos, sin = project(
        facts, tokens, attn_norm[None], w_query, w_key, w_value, fine, starts, ctx_size
    )

    blocks = [kv, lax.ppermute(kv, "ctx", core_up)]
    travelling = kv
    for back in range(1, ny):
        travelling = lax.ppermute(travelling, "ctx", y_up(1))
        blocks.append(travelling)
    near_row, far_row = 16, 20
    state = attend(facts, near_row, q, blocks[:2], None)
    came, state, cot_near, cot_middle = tie((blocks[2:], state, cot_near, cot_middle))
    cot_across = lax.ppermute(cot_near, "ep", zx(mid))
    cot_outward = lax.ppermute(cot_middle, "ep", zx(out))
    blocks = blocks[:2]
    for piece in came:
        blocks += [piece, lax.ppermute(piece, "ctx", core_swap)]
    attended, lse, hidden, mixed = attend(
        facts, far_row, q, blocks[2:], state, w_out, tokens, ffn_norm[None]
    )

    wr = jnp.pad(w_router, ((0, 0), (0, 128 - experts)))
    group = nx * own
    widths = (width, group * ff, group * ff, group * ff, width, width)
    kept = tuple(jax.ShapeDtypeStruct((NZ, rows, w), BF16) for w in widths)

    def run(call, data, cots, near, far, kept, before=None):
        return expert_call(
            facts, 48 + 16 * call, data, cots, wr, near, far, experts, kept, before
        )

    ends, away = [(0, 1), (3, 2)], [(2, 3), (1, 0)]
    near = lax.ppermute(mixed, "ep", zx(swap))
    middle_rows = lax.ppermute(mixed, "ep", zx(mid))
    mixed, cot_across, cot_outward = tie((mixed, cot_across, cot_outward))
    gm_a, gates, kept = run(0, (mixed,), (cot_ext,), weights, [], kept)
    near, middle_rows, arrived, kept = tie((near, middle_rows, arrived, kept))
    across = lax.ppermute(near, "ep", zx(mid))
    outward = lax.ppermute(middle_rows, "ep", zx(out))
    far = []
    for piece in arrived:
        far += [piece, lax.ppermute(piece, "ctx", core_swap)]
    gm_a, _, kept = run(1, (mixed,), (cot_ext,), (), far, kept, gm_a)
    across, outward, kept = tie((across, outward, kept))
    last = lax.ppermute(across, "ep", zx(out))
    gm_b, _, kept = run(2, (near,), (cot_near,), weights, far, kept)
    third = lax.ppermute(gm_b, "ep", zx(ends))
    last, kept, cot_across = tie((last, kept, cot_across))
    cot_last = lax.ppermute(cot_across, "ep", zx(out))
    cots = (cot_middle, cot_outward)
    gm_c, _, kept = run(3, (middle_rows, outward), cots, weights, far, kept)
    second = lax.ppermute(gm_c, "ep", zx(ends))
    third, cot_last, kept = tie((third, cot_last, kept))
    cots = (cot_across, cot_last)
    gm_d, _, kept = run(4, (across, last), cots, weights, far, kept)
    first = lax.ppermute(gm_d, "ep", zx(ends))

    add = lambda a, b: (a.astype(F32) + b.astype(F32)).astype(BF16)
    line = lambda a: a.reshape(NZ * rows, a.shape[2])
    saved = lambda kept: [line(kept[k]) for k in (4, 5, 1, 2, 3)]
    second, kept = tie((second, kept))
    turned = lax.ppermute(add(gm_c, second), "ep", zx(mid))
    give = expert_grads(facts, 128, nx, *saved(kept))
    first, turned, give, kept = tie((first, turned, give, kept))
    carried = lax.ppermute(add(gm_d, first), "ep", zx(mid))
    came = lax.ppermute(give, "ctx", core_swap)
    keep = expert_grads(facts, 144, nx, *saved(kept))
    carried, keep, came = tie((carried, keep, came))
    send, keep, came = tie((add(gm_b, carried), keep, came))
    final = lax.ppermute(send, "ep", zx(away))
    total = [[add(keep[j, 0], came[j, 0]) for j in range(nx)]]
    total, keep, came = tie((total, keep, came))
    total += [[add(keep[j, k], came[j, k]) for j in range(nx)] for k in (1, 2)]
    over_x = lambda k: [lax.ppermute(total[k][s], "ep", x_shift(s)) for s in range(1, nx)]
    x_came = [over_x(0)]

    sums = [gm_a, third, turned, final]
    gh, gb, do, delta, grad_ffn, grad_router = middle(
        sums, gates, wr, hidden, cot_ext, attended, mixed, ffn_norm[None], w_out, experts
    )
    give, early = early_grads(facts, attended, gb, grad_router, grad_ffn, experts)
    give, early, do, x_came, out_all = tie((give, early, do, x_came, kept[0]))
    expert_sum = lax.psum_scatter(
        line(out_all), "ep", scatter_dimension=0, axis_index_groups=z_groups, tiled=True
    )

    y_parts = [scatter_start(total_of([total[0][0]] + x_came[0]), y_axis)]
    x_came.append(over_x(1))
    early = [early, lax.ppermute(give, "ctx", core_swap)]
    dq = None
    far_dkv = []
    if ny > 1:
        dq, *far_dkv = attend_back(facts, far_row, q, do, lse, delta, blocks[2:], None, False)
    dq, far_dkv, y_parts, x_came, early = tie((dq, far_dkv, y_parts, x_came, early))

    homeward = [
        lax.ppermute(add(far_dkv[2 * k], lax.ppermute(far_dkv[2 * k + 1], "ctx", core_swap)), "ctx", y_down(k + 1))
        for k in range(ny - 1)
    ]
    x_came.append(over_x(2))
    early = total_of(early)
    dq, *near_dkv = attend_back(facts, near_row, q, do, lse, delta, blocks[:2], dq, True)
    dq, homeward, x_came, near_dkv, early = tie((dq, homeward, x_came, near_dkv, early))

    parts = [near_dkv[0], lax.ppermute(near_dkv[1], "ctx", core_down), *homeward]
    y_parts.append(scatter_start(total_of([total[1][0]] + x_came[1]), y_axis))
    early = scatter_start(early, x_axis)
    lin_q, give, keep = query_back(facts, dq, normed, cos, sin)
    parts, lin_q, give, keep = tie((parts, lin_q, give, keep))

    half_q = [keep, lax.ppermute(give, "ctx", core_swap)]
    lin_kv, give, keep = pair_back(facts, parts, normed, cos, sin)
    half_q, lin_kv, give, keep, expert_sum = tie((half_q, lin_kv, give, keep, expert_sum))

    half_kv = [keep, lax.ppermute(give, "ctx", core_swap)]
    one = scatter_start(total_of(half_q), y_axis)
    two = scatter_start(total_of(half_kv), x_axis)
    grad_tokens = tokens_back(
        lin_q, lin_kv, w_query, w_key, w_value, tokens, gh, attn_norm[None]
    )
    one, two, early, grad_tokens, y_parts, x_came = tie(
        (one, two, early, grad_tokens, y_parts, x_came)
    )
    one = scatter_start(total_of(one), x_axis)
    two = scatter_start(total_of(two), y_axis)
    early = scatter_start(total_of(early), z_axis)
    y_parts.append(scatter_start(total_of([total[2][0]] + x_came[2]), y_axis))
    one, two = tie((one, two))
    both = scatter_start(jnp.concatenate([total_of(one), total_of(two)], 0), z_axis)
    grads = [gather_start(total_of(y_parts[0]), y_axis)]
    both, early, y_parts = tie((both, early, y_parts))
    both = gather_start(total_of(both), z_axis)
    early = scatter_start(total_of(early), y_axis)
    grads.append(gather_start(total_of(y_parts[1]), y_axis))
    both, early, grads[0] = tie((both, early, grads[0]))
    early = gather_start(total_of(early), y_axis)
    both = gather_end(both, z_axis)
    size = both.shape[0] // 2
    one, two = gather_start(both[:size], x_axis), gather_start(both[size:], y_axis)
    result_out = (valid * (hidden + expert_sum.astype(F32))).astype(BF16)
    one, two, result_out, grads, early = tie((one, two, result_out, grads, early))
    early = gather_start(gather_end(early, y_axis), z_axis)
    one = gather_start(gather_end(one, x_axis), y_axis)
    two = gather_start(gather_end(two, y_axis), x_axis)
    whole = lambda g: gather_end(gather_start(gather_end(g, y_axis)[None], core_axis), core_axis)
    ready = [whole(g).reshape(own, width, ff).astype(F32) for g in grads]
    grads = gather_start(total_of(y_parts[2]), y_axis)
    one, two, ready, early = tie((one, two, ready, early))
    one, two = gather_end(one, y_axis), gather_end(two, x_axis)
    swapped = lax.ppermute(one, "ctx", core_swap), lax.ppermute(two, "ctx", core_swap)
    early = gather_start(gather_end(early, z_axis), x_axis)
    swapped, one, two = tie((swapped, one, two))
    late_q, late_k, late_v, gain = finish(
        facts, one, swapped[0], two, swapped[1], w_query, w_key, w_value, attn_norm[None]
    )
    early, late_q, grads = tie((early, late_q, grads))
    early = gather_end(early, x_axis)
    down = gather_end(grads, y_axis)
    early = gather_end(gather_start(early[None], core_axis), core_axis)
    w_out_sum = early[:, : width // 2].reshape(width, width).astype(F32)
    small = early[0, width // 2 :].astype(F32)
    down = gather_end(gather_start(down[None], core_axis), core_axis).reshape(own, width, ff)
    down = jnp.concatenate([down[:, :ff], down[:, ff:]], -1).astype(F32)
    return (
        result_out[None],
        grad_tokens[None],
        gain[0],
        late_q,
        late_k,
        late_v,
        w_out_sum,
        small[experts],
        small[:experts].T,
        *ready,
        down,
    )


def solution(mesh):
    rows, whole, split = P("ep", "ctx", None), P(), P("ep", None, None)
    return jax.shard_map(
        local,
        mesh=mesh,
        in_specs=(rows, P("ep"), rows, rows) + (whole,) * 7 + (split,) * 3,
        out_specs=(rows, rows) + (whole,) * 7 + (split,) * 3,
        check_vma=False,
    )
```
